32 devices in a mesh: dp: 2 (over core), row: 4 (over y, x), col: 4 (over z).
Axes of the slice: x: 2, y: 2, z: 4, core: 2. Of those that a mesh axis runs over, the one named last changes fastest.
Arguments:
- inputs: bfloat16 [768, 8192], P('col', ('dp', 'row')), may hold values from -6 to 6
- encoder: bfloat16 [768, 16384], P('col', ('dp', 'row')), may hold values from -6 to 6
- prefix: int32 [8], P(('dp', 'col')), may hold values from 102 to 512
- targets: int32 [8192], P(('dp', 'row')), may hold values from 0 to 32127
- gain_self: float32 [768], P('col'), may hold values from 0.1 to 1.9
- w_query: bfloat16 [768, 768], P('col', 'row'), may hold values from -0.4375 to 0.4375
- w_key: bfloat16 [768, 768], P('col', 'row'), may hold values from -0.21875 to 0.21875
- w_value: bfloat16 [768, 768], P('col', 'row'), may hold values from -0.21875 to 0.21875
- w_attn_out: bfloat16 [768, 768], P('row', 'col'), may hold values from -0.875 to 0.875
- gain_cross: float32 [768], P('col'), may hold values from 0.1 to 1.9
- w_cross_query: bfloat16 [768, 768], P('col', 'row'), may hold values from -0.4375 to 0.4375
- w_cross_key: bfloat16 [768, 768], P('col', 'row'), may hold values from -0.21875 to 0.21875
- w_cross_value: bfloat16 [768, 768], P('col', 'row'), may hold values from -0.21875 to 0.21875
- w_cross_out: bfloat16 [768, 768], P('row', 'col'), may hold values from -0.875 to 0.875
- gain_ff: float32 [768], P('col'), may hold values from 0.1 to 1.9
- w_gate: bfloat16 [768, 2048], P('col', 'row'), may hold values from -0.21875 to 0.21875
- w_up: bfloat16 [768, 2048], P('col', 'row'), may hold values from -0.21875 to 0.21875
- w_ff_out: bfloat16 [768, 2048], P('col', 'row'), may hold values from -0.125 to 0.125
- gain_final: float32 [768], P('col'), may hold values from 0.1 to 1.9
- embed_table: bfloat16 [768, 32128], P('row', 'col'), may hold values from -0.4375 to 0.4375
Outputs:
- output: bfloat16 [768, 8192], P('col', ('dp', 'row'))
- loss: float32 [8192], P(('dp', 'row'))
- grad_inputs: float32 [768, 8192], P('col', ('dp', 'row'))
- grad_encoder: float32 [768, 16384], P('col', ('dp', 'row'))
- grad_gain_self: float32 [768], P('col')
- grad_w_query: float32 [768, 768], P(('col', 'dp'), 'row')
- grad_w_key: float32 [768, 768], P(('col', 'dp'), 'row')
- grad_w_value: float32 [768, 768], P(('col', 'dp'), 'row')
- grad_w_attn_out: float32 [768, 768], P(('row', 'dp'), 'col')
- grad_gain_cross: float32 [768], P('col')
- grad_w_cross_query: float32 [768, 768], P(('col', 'dp'), 'row')
- grad_w_cross_key: float32 [768, 768], P(('col', 'dp'), 'row')
- grad_w_cross_value: float32 [768, 768], P(('col', 'dp'), 'row')
- grad_w_cross_out: float32 [768, 768], P(('row', 'dp'), 'col')
- grad_gain_ff: float32 [768], P('col')
- grad_w_gate: float32 [768, 2048], P(('col', 'dp'), 'row')
- grad_w_up: float32 [768, 2048], P(('col', 'dp'), 'row')
- grad_w_ff_out: float32 [768, 2048], P(('col', 'dp'), 'row')
- grad_gain_final: float32 [768], P('col')
- grad_embed_table: float32 [768, 32128], P(('dp', 'row'), 'col')
The draws below stay inside these ranges and needn't reach their ends.
All inputs are finite; a program needn't handle non-finite values.
Results may differ from the reference program's by a relative error of at most 0.025.
Values may be sent and summed in bfloat16 or wider, within the bound.
No kernel may reach another device: no remote copies, remote signals or barrier semaphores. Data moves between devices by JAX's collectives and lax.ppermute only.
A program may use at most 256 MiB of HBM per device.

```python
import math
import jax
import jax.numpy as jnp
import numpy as np
from jax import lax

D = 768
HEADS = 12
HEAD = 64
FF = 2048
VOCAB = 32128
SEQ = 1024
ENC = 2048
SEQS = 8
TOKENS = 8192
ENC_TOKENS = 16384


def with_ends(entries, key, least, high):
    longest = entries.shape.index(max(entries.shape))
    spots = []
    for shift in (0, 1):
        where = [jax.random.randint(jax.random.fold_in(key, axis), (), 0, length) for axis, length in enumerate(entries.shape)]
        where[longest] = (where[longest] + shift) % entries.shape[longest]
        spots.append(tuple(where))
    return entries.at[spots[0]].set(least).at[spots[1]].set(high)


def shard_levels(key, dims, cuts, least, top_value):
    def one(dim, parts):
        draws = jax.random.uniform(jax.random.fold_in(jax.random.fold_in(key, 6), dim), (parts,), jnp.float32, least / len(cuts), top_value / len(cuts))
        return jnp.repeat(jnp.exp(draws), dims[dim] // parts).reshape((-1,) + (1,) * (len(dims) - dim - 1))

    factor_of = one(*cuts[0])
    for cut in cuts[1:]:
        factor_of = factor_of * one(*cut)
    return factor_of


def cumulative_ranks(amount, slope):
    loads = [(1 << 20) // math.isqrt(rank ** slope) + 1 for rank in range(1, amount + 1)]
    scale = 1 + sum(loads) // (1 << 30)
    return np.cumsum(np.array([max(1, weight // scale) for weight in loads]))


def skewed_ids(key, extent, count, slope):
    grid = cumulative_ranks(count, slope)
    ticket = jax.random.randint(jax.random.fold_in(key, 1), extent, 0, int(grid[count - 1]))
    rank = jnp.searchsorted(jnp.asarray(grid, jnp.int32), ticket, side="right")
    return jax.random.permutation(jax.random.fold_in(key, 2), count)[rank].astype(jnp.int32)


def bell_draw(stream_key, dims, width, most, pieces=(), kind=jnp.bfloat16):
    level = shard_levels(stream_key, dims, pieces, -0.22, 0.18) if pieces else 1.0
    values = jax.random.normal(stream_key, dims, jnp.float32) * width * level
    return jnp.minimum(jnp.maximum(values, -most), most).astype(kind)


def setup_inputs(seed: int = 0) -> dict:
    seeds = jax.random.split(jax.random.key(seed), 21)
    inputs = bell_draw(seeds[0], (D, TOKENS), 1.0, 6.0, ((0, 4), (1, 8)))
    encoder = bell_draw(seeds[1], (D, ENC_TOKENS), 1.0, 6.0, ((0, 4), (1, 8)))
    prefix = with_ends(jax.random.randint(seeds[2], (SEQS,), max(1, SEQ // 10), SEQ // 2 + 1), jax.random.fold_in(seeds[2], 1), max(1, SEQ // 10), (SEQ // 2 + 1) - 1).astype(jnp.int32)
    targets = with_ends(skewed_ids(seeds[3], (TOKENS,), VOCAB, 2), jax.random.fold_in(seeds[3], 3), 0, VOCAB - 1).astype(jnp.int32)
    gain_self = jnp.clip(1.0 + 0.18 * jax.random.normal(seeds[4], (D,), jnp.float32), 0.1, 1.9)
    w_query = bell_draw(seeds[5], (D, HEADS * HEAD), (D // 4) ** -0.5, 0.4375, ((0, 4), (1, 4)))
    w_key = bell_draw(seeds[6], (D, HEADS * HEAD), D ** -0.5, 0.21875, ((0, 4), (1, 4)))
    w_value = bell_draw(seeds[7], (D, HEADS * HEAD), D ** -0.5, 0.21875, ((0, 4), (1, 4)))
    w_attn_out = bell_draw(seeds[8], (HEADS * HEAD, D), (HEADS * HEAD // 16) ** -0.5, 0.875, ((0, 4), (1, 4)))
    gain_cross = jnp.clip(1.0 + 0.18 * jax.random.normal(seeds[9], (D,), jnp.float32), 0.1, 1.9)
    w_cross_query = bell_draw(seeds[10], (D, HEADS * HEAD), (D // 4) ** -0.5, 0.4375, ((0, 4), (1, 4)))
    w_cross_key = bell_draw(seeds[11], (D, HEADS * HEAD), D ** -0.5, 0.21875, ((0, 4), (1, 4)))
    w_cross_value = bell_draw(seeds[12], (D, HEADS * HEAD), D ** -0.5, 0.21875, ((0, 4), (1, 4)))
    w_cross_out = bell_draw(seeds[13], (HEADS * HEAD, D), (HEADS * HEAD // 16) ** -0.5, 0.875, ((0, 4), (1, 4)))
    gain_ff = jnp.clip(1.0 + 0.18 * jax.random.normal(seeds[14], (D,), jnp.float32), 0.1, 1.9)
    w_gate = bell_draw(seeds[15], (D, FF), D ** -0.5, 0.21875, ((0, 4), (1, 4)))
    w_up = bell_draw(seeds[16], (D, FF), D ** -0.5, 0.21875, ((0, 4), (1, 4)))
    w_ff_out = bell_draw(seeds[17], (D, FF), FF ** -0.5, 0.125, ((0, 4), (1, 4)))
    gain_final = jnp.clip(1.0 + 0.18 * jax.random.normal(seeds[18], (D,), jnp.float32), 0.1, 1.9)
    embed_table = bell_draw(seeds[19], (D, VOCAB), (D // 4) ** -0.5, 0.4375, ((0, 4), (1, 4)))
    return {"inputs": inputs, "encoder": encoder, "prefix": prefix, "targets": targets, "gain_self": gain_self, "w_query": w_query, "w_key": w_key, "w_value": w_value, "w_attn_out": w_attn_out, "gain_cross": gain_cross, "w_cross_query": w_cross_query, "w_cross_key": w_cross_key, "w_cross_value": w_cross_value, "w_cross_out": w_cross_out, "gain_ff": gain_ff, "w_gate": w_gate, "w_up": w_up, "w_ff_out": w_ff_out, "gain_final": gain_final, "embed_table": embed_table}


@jax.custom_vjp
def low(v):
    return lax.optimization_barrier(v.astype(jnp.bfloat16)).astype(jnp.float32)

@jax.custom_vjp
def low_back(v):
    return v

def low_keep(v):
    return (low(v), None)

def low_pass(kept, grad):
    return (grad,)

def back_keep(v):
    return (v, None)

def back_low(kept, grad):
    return (low(grad),)
low.defvjp(low_keep, low_pass)
low_back.defvjp(back_keep, back_low)
EPS = 1e-06
NEGATIVE = -1e+30
HIGHEST = lax.Precision.HIGHEST

def normalize(states, gain):
    scale = lax.rsqrt(lax.optimization_barrier(jnp.mean(states * states, axis=-1, keepdims=True)) + EPS)
    return states * scale * gain

def matmul(left, right):
    return jnp.dot(left, right, precision=HIGHEST)

def attend(query, key, value, visible):
    heads_all = query.shape[1] // HEAD
    query = query.reshape(query.shape[0], heads_all, HEAD)
    key = key.reshape(key.shape[0], heads_all, HEAD)
    value = value.reshape(value.shape[0], heads_all, HEAD)
    scores = low_back(jnp.einsum('qhe,khe->hqk', query, key, precision=HIGHEST) * HEAD ** (-0.5))
    if visible is not None:
        scores = jnp.where(visible[None], scores, NEGATIVE)
    weights = jax.nn.softmax(scores, axis=-1)
    mixed = jnp.einsum('hqk,khe->qhe', low(weights), value, precision=HIGHEST)
    return mixed.reshape(mixed.shape[0], heads_all * HEAD)

def layer(states, encoded, prefix_len, target, params):
    gain_self, w_query, w_key, w_value, w_attn_out, gain_cross, w_cross_query, w_cross_key, w_cross_value, w_cross_out, gain_ff, w_gate, w_up, w_ff_out, gain_final, embed_table = params
    normed = low(normalize(states, gain_self))
    query = low_back(low(matmul(normed, w_query)))
    key = low_back(low(matmul(normed, w_key)))
    value = low_back(low(matmul(normed, w_value)))
    position = jnp.arange(SEQ, dtype=jnp.int32)
    visible = (position[None, :] <= position[:, None]) | (position[None, :] < prefix_len)
    attended = low_back(low(attend(query, key, value, visible)))
    first = states + low_back(matmul(attended, w_attn_out))
    normed_cross = low(normalize(first, gain_cross))
    cross_query = low_back(low(matmul(normed_cross, w_cross_query)))
    cross_key = low_back(low(matmul(encoded, w_cross_key)))
    cross_value = low_back(low(matmul(encoded, w_cross_value)))
    crossed = low_back(low(attend(cross_query, cross_key, cross_value, None)))
    second = first + low_back(matmul(crossed, w_cross_out))
    normed_ff = low(normalize(second, gain_ff))
    gate = low_back(matmul(normed_ff, w_gate))
    upward = low_back(matmul(normed_ff, w_up))
    hidden = low(jax.nn.gelu(gate, approximate=True) * upward)
    third = second + low_back(matmul(hidden, w_ff_out.T))
    final = low(normalize(third, gain_final))
    logits = low_back(jnp.dot(final, embed_table, precision=HIGHEST))
    totals = jax.nn.logsumexp(logits, axis=-1)
    picked = jnp.take_along_axis(logits, target[:, None], axis=1)[:, 0]
    return (third, totals - picked)

def reference(inputs, encoder, prefix, targets, gain_self, w_query, w_key, w_value, w_attn_out, gain_cross, w_cross_query, w_cross_key, w_cross_value, w_cross_out, gain_ff, w_gate, w_up, w_ff_out, gain_final, embed_table):
    params = tuple((item.astype(jnp.float32) for item in (gain_self, w_query, w_key, w_value, w_attn_out, gain_cross, w_cross_query, w_cross_key, w_cross_value, w_cross_out, gain_ff, w_gate, w_up, w_ff_out, gain_final, embed_table)))
    states_all = inputs.astype(jnp.float32).T.reshape(SEQS, SEQ, D)
    encoded_all = encoder.astype(jnp.float32).T.reshape(SEQS, ENC, D)
    targets_all = targets.reshape(SEQS, SEQ)

    def step(total, item):
        states, encoded, prefix_len, target = item

        def run(states_in, encoded_in, params_in):
            return layer(states_in, encoded_in, prefix_len, target, params_in)
        (third, losses), pull = jax.vjp(run, states, encoded, params)
        grad_states, grad_encoded, grad_params = pull((jnp.zeros_like(third), jnp.ones_like(losses)))
        total = jax.tree.map(lambda left, right: left + right, total, grad_params)
        return (total, (third, losses, grad_states, grad_encoded))
    zeros = jax.tree.map(jnp.zeros_like, params)
    total, (thirds, losses, grad_states, grad_encoded) = lax.scan(step, zeros, (states_all, encoded_all, prefix, targets_all))
    return (thirds.reshape(TOKENS, D).T.astype(jnp.bfloat16), losses.reshape(TOKENS), grad_states.reshape(TOKENS, D).T, grad_encoded.reshape(ENC_TOKENS, D).T, total[0], total[1], total[2], total[3], total[4], total[5], total[6], total[7], total[8], total[9], total[10], total[11], total[12], total[13], total[14], total[15])
```

```python
from functools import partial

import jax
import jax.numpy as jnp
from jax import lax
from jax.experimental import pallas as pl
from jax.experimental.pallas import tpu as pltpu
from jax.sharding import PartitionSpec as P

HEAD = 64
EPS = 1e-06
NEGATIVE = -1e30
BF = jnp.bfloat16
F32 = jnp.float32
MIB = 1 << 20


def mm(left, right, dims):
    return lax.dot_general(left, right, (dims, ((), ())), preferred_element_type=F32)


def nn(left, right):
    return mm(left, right, ((1,), (0,)))


def tn(left, right):
    return mm(left, right, ((0,), (0,)))


def nt(left, right):
    return mm(left, right, ((1,), (1,)))


def params(mib, axes=1):
    return pltpu.CompilerParams(
        dimension_semantics=("arbitrary",) * axes, vmem_limit_bytes=mib * MIB
    )


def whole(shape):
    return pl.BlockSpec(shape, lambda *_: (0,) * len(shape))


def scores_of(key, query, start, prefix, causal):
    scores = tn(key, query * jnp.asarray(HEAD**-0.5, BF))
    if causal:
        keys = lax.broadcasted_iota(jnp.int32, scores.shape, 0)
        rows = lax.broadcasted_iota(jnp.int32, scores.shape, 1) + start
        scores = jnp.where((keys <= rows) | (keys < prefix), scores, NEGATIVE)
    return scores


def attend_forward(info, query, key, value, causal):
    (q_arr, q_row, q_moves), (k_arr, k_row), (v_arr, v_row) = query, key, value
    tq = info["tq"]
    blocks = q_arr.shape[0]
    heads = info["heads"]
    tk = k_arr.shape[2]

    def body(s_ref, q_ref, k_ref, v_ref, o_ref, l_ref):
        scores = scores_of(k_ref[0], q_ref[0], s_ref[0] * tq, s_ref[1], causal)
        top = jnp.max(scores, axis=0, keepdims=True)
        weights = jnp.exp(scores - top)
        total = jnp.sum(weights, axis=0, keepdims=True)
        mixed = nn(v_ref[0], weights.astype(BF))
        o_ref[0] = (mixed / total).astype(BF)
        l_ref[0] = top + jnp.log(total)

    return pl.pallas_call(
        body,
        out_shape=(
            jax.ShapeDtypeStruct((blocks, heads * HEAD, tq), BF),
            jax.ShapeDtypeStruct((blocks * heads, 1, tq), F32),
        ),
        grid_spec=pltpu.PrefetchScalarGridSpec(
            num_scalar_prefetch=1,
            grid=(blocks, heads),
            in_specs=[
                pl.BlockSpec(
                    (1, HEAD, tq), lambda b, h, s: (b, q_row + h, s[0] if q_moves else 0)
                ),
                pl.BlockSpec((1, HEAD, tk), lambda b, h, s: (b, k_row + h, 0)),
                pl.BlockSpec((1, HEAD, tk), lambda b, h, s: (b, v_row + h, 0)),
            ],
            out_specs=(
                pl.BlockSpec((1, HEAD, tq), lambda b, h, s: (b, h, 0)),
                pl.BlockSpec((1, 1, tq), lambda b, h, s: (b * heads + h, 0, 0)),
            ),
        ),
        compiler_params=params(48, 2),
    )(info["scalars"], q_arr, k_arr, v_arr)


def attend_backward(info, query, key, value, incoming, totals, causal):
    (q_arr, q_row, q_moves), (k_arr, k_row), (v_arr, v_row) = query, key, value
    tq = info["tq"]
    blocks = q_arr.shape[0]
    heads = info["heads"]
    tk = k_arr.shape[2]

    def body(s_ref, q_ref, k_ref, v_ref, g_ref, l_ref, dq_ref, dk_ref, dv_ref):
        q = q_ref[0]
        scores = scores_of(k_ref[0], q, s_ref[0] * tq, s_ref[1], causal)
        weights = jnp.exp(scores - l_ref[0])
        dp = tn(v_ref[0], g_ref[0])
        inner = weights * dp
        centre = jnp.sum(inner, axis=0, keepdims=True)
        ds = (inner - weights * centre).astype(BF)
        dv_ref[0] = nt(g_ref[0], weights.astype(BF)).astype(BF)
        dq_ref[0] = (nn(k_ref[0], ds) * HEAD**-0.5).astype(BF)
        dk_ref[0] = (nt(q, ds) * HEAD**-0.5).astype(BF)

    return pl.pallas_call(
        body,
        out_shape=(
            jax.ShapeDtypeStruct((blocks, heads * HEAD, tq), BF),
            jax.ShapeDtypeStruct((blocks, heads * HEAD, tk), BF),
            jax.ShapeDtypeStruct((blocks, heads * HEAD, tk), BF),
        ),
        grid_spec=pltpu.PrefetchScalarGridSpec(
            num_scalar_prefetch=1,
            grid=(blocks, heads),
            in_specs=[
                pl.BlockSpec(
                    (1, HEAD, tq), lambda b, h, s: (b, q_row + h, s[0] if q_moves else 0)
                ),
                pl.BlockSpec((1, HEAD, tk), lambda b, h, s: (b, k_row + h, 0)),
                pl.BlockSpec((1, HEAD, tk), lambda b, h, s: (b, v_row + h, 0)),
                pl.BlockSpec((1, HEAD, tq), lambda b, h, s: (b, h, 0)),
                pl.BlockSpec((1, 1, tq), lambda b, h, s: (b * heads + h, 0, 0)),
            ],
            out_specs=(
                pl.BlockSpec((1, HEAD, tq), lambda b, h, s: (b, h, 0)),
                pl.BlockSpec((1, HEAD, tk), lambda b, h, s: (b, h, 0)),
                pl.BlockSpec((1, HEAD, tk), lambda b, h, s: (b, h, 0)),
            ),
        ),
        compiler_params=params(48, 2),
    )(info["scalars"], q_arr, k_arr, v_arr, incoming, totals)


GELU_A = 0.7978845608028654
GELU_B = 0.044715


def gelu_parts(gate):
    inner = jnp.tanh(GELU_A * (gate + GELU_B * gate * gate * gate))
    value = 0.5 * gate * (1.0 + inner)
    slope = 0.5 * (1.0 + inner) + 0.5 * gate * (1.0 - inner * inner) * (
        GELU_A * (1.0 + 3.0 * GELU_B * gate * gate)
    )
    return value, slope


def ff_forward(packs, normed):
    blocks, d, lanes = packs[0].shape
    wide = lanes // 3
    tokens = normed.shape[1]
    n = len(packs)

    def body(*refs):
        w_refs, x_ref, save_refs, out_ref = refs[:n], refs[n], refs[n + 1 : 2 * n + 1], refs[-1]

        @pl.when(pl.program_id(0) == 0)
        def _():
            out_ref[...] = jnp.zeros_like(out_ref)

        for w_ref, save_ref in zip(w_refs, save_refs):
            both = tn(w_ref[0, :, : 2 * wide], x_ref[...])
            save_ref[0] = both
            value, _ = gelu_parts(both[:wide])
            hidden = (value * both[wide:]).astype(BF)
            out_ref[...] += nn(w_ref[0, :, 2 * wide :], hidden)

    return pl.pallas_call(
        body,
        grid=(blocks,),
        in_specs=[pl.BlockSpec((1, d, lanes), lambda b: (b, 0, 0))] * n
        + [whole((d, tokens))],
        out_specs=[pl.BlockSpec((1, 2 * wide, tokens), lambda b: (b, 0, 0))] * n
        + [whole((d, tokens))],
        out_shape=[jax.ShapeDtypeStruct((blocks, 2 * wide, tokens), F32)] * n
        + [jax.ShapeDtypeStruct((d, tokens), F32)],
        compiler_params=params(48),
    )(*packs, normed)


def ff_backward(packs, saved, normed, grad):
    blocks, d, lanes = packs[0].shape
    wide = lanes // 3
    tokens = normed.shape[1]
    n = len(packs)

    def body(*refs):
        w_refs, save_refs = refs[:n], refs[n : 2 * n]
        x_ref, g_ref = refs[2 * n], refs[2 * n + 1]
        dw_refs, out_ref = refs[2 * n + 2 : 3 * n + 2], refs[-1]

        @pl.when(pl.program_id(0) == 0)
        def _():
            out_ref[...] = jnp.zeros_like(out_ref)

        for w_ref, save_ref, dw_ref in zip(w_refs, save_refs, dw_refs):
            dh = tn(w_ref[0, :, 2 * wide :], g_ref[...])
            gate, up = save_ref[0, :wide], save_ref[0, wide:]
            value, slope = gelu_parts(gate)
            hidden = (value * up).astype(BF)
            grads = jnp.concatenate(
                [(dh * up * slope).astype(BF), (dh * value).astype(BF)], axis=0
            )
            dw_ref[0, :, : 2 * wide] = nt(x_ref[...], grads).astype(BF)
            dw_ref[0, :, 2 * wide :] = nt(g_ref[...], hidden).astype(BF)
            out_ref[...] += nn(w_ref[0, :, : 2 * wide], grads)

    return pl.pallas_call(
        body,
        grid=(blocks,),
        in_specs=[pl.BlockSpec((1, d, lanes), lambda b: (b, 0, 0))] * n
        + [pl.BlockSpec((1, 2 * wide, tokens), lambda b: (b, 0, 0))] * n
        + [whole((d, tokens))] * 2,
        out_specs=[pl.BlockSpec((1, d, lanes), lambda b: (b, 0, 0))] * n
        + [whole((d, tokens))],
        out_shape=[jax.ShapeDtypeStruct((blocks, d, lanes), BF)] * n
        + [jax.ShapeDtypeStruct((d, tokens), F32)],
        compiler_params=params(56),
    )(*packs, *saved, normed, grad)


def project(pack, normed, low, high):
    blocks, d, _ = pack.shape
    tokens = normed.shape[1]

    def body(w_ref, x_ref, o_ref):
        o_ref[0] = tn(w_ref[0, :, low:high], x_ref[...]).astype(BF)

    return pl.pallas_call(
        body,
        grid=(blocks,),
        in_specs=[pl.BlockSpec((1, d, pack.shape[2]), lambda b: (b, 0, 0)), whole((d, tokens))],
        out_specs=pl.BlockSpec((1, high - low, tokens), lambda b: (b, 0, 0)),
        out_shape=jax.ShapeDtypeStruct((blocks, high - low, tokens), BF),
        compiler_params=params(40),
    )(pack, normed)


def combine(pack, rows, low, high, kind=F32):
    blocks, d, _ = pack.shape
    tokens = rows.shape[2]

    def body(w_ref, x_ref, o_ref):
        @pl.when(pl.program_id(0) == 0)
        def _():
            o_ref[...] = jnp.zeros_like(o_ref)

        o_ref[...] += nn(w_ref[0, :, low:high], x_ref[0])

    return pl.pallas_call(
        body,
        grid=(blocks,),
        in_specs=[
            pl.BlockSpec((1, d, pack.shape[2]), lambda b: (b, 0, 0)),
            pl.BlockSpec((1, high - low, tokens), lambda b: (b, 0, 0)),
        ],
        out_specs=whole((d, tokens)),
        out_shape=jax.ShapeDtypeStruct((d, tokens), kind),
        compiler_params=params(40),
    )(pack, rows)


def weight_grads(pairs, lanes):
    d = pairs[0][0].shape[0]
    blocks = pairs[0][1].shape[0]
    n = len(pairs)
    lefts = [left for left, _ in pairs]
    rights = [right for _, right in pairs]

    def body(*refs):
        out_ref = refs[-1]
        at = 0
        for left_ref, right_ref in zip(refs[:n], refs[n : 2 * n]):
            width = right_ref.shape[1]
            out_ref[0, :, at : at + width] = nt(left_ref[...], right_ref[0]).astype(BF)
            at += width

    return pl.pallas_call(
        body,
        grid=(blocks,),
        in_specs=[whole(left.shape) for left in lefts]
        + [pl.BlockSpec((1,) + right.shape[1:], lambda b: (b, 0, 0)) for right in rights],
        out_specs=pl.BlockSpec((1, d, lanes), lambda b: (b, 0, 0)),
        out_shape=jax.ShapeDtypeStruct((blocks, d, lanes), BF),
        compiler_params=params(48),
    )(*lefts, *rights)


def source_grads(pack, own, own_low, wide, wide_low, place, width, kind):
    blocks, d, lanes = pack.shape
    tq = own.shape[2] if own is not None else 0
    n = len(wide)
    tokens = wide[0].shape[2]
    step = min(1024, tokens)

    def body(*refs):
        s_ref, w_ref = refs[0], refs[1]
        wide_refs = refs[2 : 2 + n]
        o_ref = refs[-1]
        acc = jnp.zeros((d, step), F32)
        for b in range(blocks):
            for at, ref in zip(wide_low, wide_refs):
                acc += nn(w_ref[b, :, at : at + width], ref[b])
        o_ref[...] = acc.astype(kind)
        if own is not None:
            own_ref = refs[2 + n]
            part = jnp.zeros((d, tq), F32)
            for b in range(blocks):
                part += nn(w_ref[b, :, own_low : own_low + width], own_ref[b])
            where = pl.ds(pl.multiple_of(s_ref[0] * tq, tq), tq)
            o_ref[:, where] += part.astype(kind)

    return pl.pallas_call(
        body,
        out_shape=jax.ShapeDtypeStruct((d, tokens), kind),
        grid_spec=pltpu.PrefetchScalarGridSpec(
            num_scalar_prefetch=1,
            grid=(tokens // step,),
            in_specs=[pl.BlockSpec((blocks, d, lanes), lambda i, s: (0, 0, 0))]
            + [pl.BlockSpec((blocks, width, step), lambda i, s: (0, 0, i))] * n
            + (
                [pl.BlockSpec((blocks, width, tq), lambda i, s: (0, 0, 0))]
                if own is not None
                else []
            ),
            out_specs=pl.BlockSpec((d, step), lambda i, s: (0, i)),
        ),
        compiler_params=params(40),
    )(place, pack, *wide, *([own] if own is not None else []))


VB = 512


def assemble(s_ref, own_ref, one_ref, two_ref, out_ref):
    size = own_ref.shape[0]
    out_ref[:size] = own_ref[...]
    out_ref[pl.ds(pl.multiple_of((1 + s_ref[1]) * size, size), size), :] = one_ref[...]
    out_ref[pl.ds(pl.multiple_of((2 - s_ref[1]) * size, size), size), :] = two_ref[0]
    out_ref[3 * size :] = two_ref[1]


def table_specs(size):
    return [
        pl.BlockSpec((size, VB), lambda v, s: (0, v)),
        pl.BlockSpec((size, VB), lambda v, s: (0, v)),
        pl.BlockSpec((2, size, VB), lambda v, s: (0, 0, v)),
    ]


def vocab_forward(scalars, hidden, table, wanted):
    chunks, d, step = hidden.shape
    own, one, two = table
    size, width = own.shape
    parts = width // VB

    def body(s_ref, h_ref, own_ref, one_ref, two_ref, t_ref, e_ref, m_ref, top_ref, sum_ref, pick_ref, blk, flip):
        vb = pl.program_id(0)

        @pl.when(vb == 0)
        def _():
            top_ref[...] = jnp.full_like(top_ref, NEGATIVE)
            sum_ref[...] = jnp.zeros_like(sum_ref)
            pick_ref[...] = jnp.zeros_like(pick_ref)

        assemble(s_ref, own_ref, one_ref, two_ref, blk)
        flip[...] = blk[...].T
        ids = lax.broadcasted_iota(jnp.int32, (VB, step), 0) + vb * VB

        def one_chunk(n, carry):
            logits = nn(flip[...], h_ref[n])
            pick_ref[n] += jnp.sum(
                jnp.where(ids == t_ref[n], logits, 0.0), axis=0, keepdims=True
            )
            logits = jnp.where(ids < s_ref[0], logits, NEGATIVE)
            before = top_ref[n]
            top = jnp.maximum(before, jnp.max(logits, axis=0, keepdims=True))
            exps = jnp.exp(logits - top)
            sum_ref[n] = sum_ref[n] * jnp.exp(before - top) + jnp.sum(
                exps, axis=0, keepdims=True
            )
            top_ref[n] = top
            m_ref[0, n] = top
            e_ref[n] = exps.astype(BF)
            return carry

        lax.fori_loop(0, chunks, one_chunk, 0)

    row = jax.ShapeDtypeStruct((chunks, 1, step), F32)
    return pl.pallas_call(
        body,
        out_shape=(
            jax.ShapeDtypeStruct((chunks, width, step), BF),
            jax.ShapeDtypeStruct((parts, chunks, 1, step), F32),
            row,
            row,
            row,
        ),
        grid_spec=pltpu.PrefetchScalarGridSpec(
            num_scalar_prefetch=1,
            grid=(parts,),
            in_specs=[whole((chunks, d, step))] + table_specs(size) + [whole((chunks, 1, step))],
            out_specs=(
                pl.BlockSpec((chunks, VB, step), lambda v, s: (0, v, 0)),
                pl.BlockSpec((1, chunks, 1, step), lambda v, s: (v, 0, 0, 0)),
                whole((chunks, 1, step)),
                whole((chunks, 1, step)),
                whole((chunks, 1, step)),
            ),
            scratch_shapes=[pltpu.VMEM((d, VB), BF), pltpu.VMEM((VB, d), BF)],
        ),
        compiler_params=params(48),
    )(scalars, hidden, own, one, two, wanted)


def vocab_hidden_grad(scalars, exps, tops, logsum, table, wanted):
    chunks, width, step = exps.shape
    own, one, two = table
    size = own.shape[0]
    d = 4 * size
    parts = width // VB

    def body(s_ref, e_ref, m_ref, l_ref, own_ref, one_ref, two_ref, t_ref, g_ref, o_ref, blk, acc):
        vb = pl.program_id(0)

        @pl.when(vb == 0)
        def _():
            acc[...] = jnp.zeros_like(acc)

        assemble(s_ref, own_ref, one_ref, two_ref, blk)
        ids = lax.broadcasted_iota(jnp.int32, (VB, step), 0) + vb * VB

        def one_chunk(n, carry):
            scale = jnp.exp(m_ref[0, n] - l_ref[n])
            probs = e_ref[n].astype(F32) * scale
            grads = jnp.where(ids == t_ref[n], probs - 1.0, probs).astype(BF)
            g_ref[n] = grads
            acc[n] += nn(blk[...], grads)
            return carry

        lax.fori_loop(0, chunks, one_chunk, 0)

        @pl.when(vb == parts - 1)
        def _():
            o_ref[...] = acc[...].astype(BF)

    return pl.pallas_call(
        body,
        out_shape=(
            jax.ShapeDtypeStruct((chunks, width, step), BF),
            jax.ShapeDtypeStruct((chunks, d, step), BF),
        ),
        grid_spec=pltpu.PrefetchScalarGridSpec(
            num_scalar_prefetch=1,
            grid=(parts,),
            in_specs=[
                pl.BlockSpec((chunks, VB, step), lambda v, s: (0, v, 0)),
                pl.BlockSpec((1, chunks, 1, step), lambda v, s: (v, 0, 0, 0)),
                whole((chunks, 1, step)),
            ]
            + table_specs(size)
            + [whole((chunks, 1, step))],
            out_specs=(
                pl.BlockSpec((chunks, VB, step), lambda v, s: (0, v, 0)),
                whole((chunks, d, step)),
            ),
            scratch_shapes=[pltpu.VMEM((d, VB), BF), pltpu.VMEM((chunks, d, step), F32)],
        ),
        input_output_aliases={1: 0},
        compiler_params=params(56),
    )(scalars, exps, tops, logsum, own, one, two, wanted)


def vocab_table_grad(places, hidden, grads):
    chunks, width, step = grads.shape
    d = hidden.shape[1]
    unit = d // 8
    parts = width // VB

    def body(s_ref, h_ref, g_ref, o_ref):
        acc = nt(h_ref[0], g_ref[0])
        for n in range(1, chunks):
            acc += nt(h_ref[n], g_ref[n])
        for u in range(8):
            spot = pl.ds(pl.multiple_of(s_ref[u] * unit, unit), unit)
            o_ref[spot, :] = acc[u * unit : (u + 1) * unit].astype(BF)

    return pl.pallas_call(
        body,
        out_shape=jax.ShapeDtypeStruct((d, width), BF),
        grid_spec=pltpu.PrefetchScalarGridSpec(
            num_scalar_prefetch=1,
            grid=(parts,),
            in_specs=[
                whole((chunks, d, step)),
                pl.BlockSpec((chunks, VB, step), lambda v, s: (0, v, 0)),
            ],
            out_specs=pl.BlockSpec((d, VB), lambda v, s: (0, v)),
        ),
        compiler_params=params(48),
    )(places, hidden, grads)


def norm_forward(states, gain):
    scale = lax.rsqrt(jnp.mean(states * states, axis=0, keepdims=True) + EPS)
    return ((states * scale * gain).astype(BF), scale)


def norm_backward(states, gain, scale, incoming):
    weighted = incoming * gain
    inner = jnp.mean(weighted * states, axis=0, keepdims=True)
    through = scale * weighted - states * (scale * scale * scale * inner)
    return (through, jnp.sum(incoming * states * scale, axis=1))


class Moves:
    def __init__(self, dp):
        self.dp = dp

    def core(self, x):
        return lax.ppermute(x, "dp", [(i, i ^ 1) for i in range(self.dp)])

    def col(self, x, bit):
        return lax.ppermute(x, "col", [(i, i ^ bit) for i in range(4)])

    def rows(self, x, pairs):
        perm = []
        for i in range(self.dp):
            for r in range(4):
                flip, bit = pairs[i % 2]
                perm.append((i * 4 + r, (i ^ flip) * 4 + (r ^ bit)))
        return lax.ppermute(x, ("dp", "row"), perm)

    def spread(self, x, turn, back=False):
        perm = []
        for i in range(self.dp):
            for c in range(4):
                dest = (i - i % 2 + c // 2) * 4 + 2 * (i % 2) + (c % 2 ^ turn)
                perm.append((dest, i * 4 + c) if back else (i * 4 + c, dest))
        return lax.ppermute(x, ("dp", "col"), perm)


STEP_ONE = {0: (0, 1), 1: (0, 2)}
STEP_TWO = {0: (1, 2), 1: (1, 1)}
STEP_TWO_BACK = {0: (1, 1), 1: (1, 2)}
SAME_TWO = {0: (0, 2), 1: (0, 1)}


def local(
    inputs,
    encoder,
    prefix,
    targets,
    gain_self,
    w_query,
    w_key,
    w_value,
    w_attn_out,
    gain_cross,
    w_cross_query,
    w_cross_key,
    w_cross_value,
    w_cross_out,
    gain_ff,
    w_gate,
    w_up,
    w_ff_out,
    gain_final,
    embed_table,
    *,
    dp,
):
    move = Moves(dp)
    dpi = lax.axis_index("dp")
    core = dpi % 2
    row = lax.axis_index("row")
    col = lax.axis_index("col")
    first_core = core == 0
    side = col // 2
    half = col % 2
    block = inputs.shape[0]
    d = 4 * block
    seq = inputs.shape[1]
    tq = seq // 2
    tc = tq // 2
    heads = w_query.shape[1] // HEAD
    ff_half = w_gate.shape[1] // 2
    vocab = embed_table.shape[1]
    width = -(-vocab // (2 * VB)) * VB
    mine = side == core

    def pick(flag, a, b):
        return jnp.where(flag, a, b)

    def bring(x):
        got = jnp.stack([move.spread(x, 0), move.spread(x, 1)])
        other = move.core(got)
        near, far = pick(mine, got, other), pick(mine, other, got)
        return jnp.concatenate([near[0], far[0], near[1], far[1]], axis=0)

    def hand_back(parts):
        hi = [pick(mine, parts[0], parts[1]), pick(mine, parts[2], parts[3])]
        got = [move.spread(hi[0], 0, True), move.spread(hi[1], 1, True)]
        return pick(
            half == 0,
            jnp.concatenate([got[0], got[1]], axis=1),
            jnp.concatenate([got[1], got[0]], axis=1),
        )

    def fold_back(partial_sum):
        blocks4 = partial_sum.reshape(4, block, -1)
        near = jnp.stack([blocks4[0], blocks4[2]])
        far = jnp.stack([blocks4[1], blocks4[3]])
        keep, send = pick(mine, near, far), pick(mine, far, near)
        total = (keep.astype(F32) + move.core(send).astype(F32)).astype(BF)
        whole_sum = (total[0].astype(F32) + move.col(total[1], 1).astype(F32)).astype(BF)
        perm = []
        for i in range(dp):
            for c in range(4):
                perm.append((i * 4 + c, (i - i % 2 + c // 2) * 4 + 2 * (i % 2) + c % 2))
        return lax.ppermute(whole_sum, ("dp", "col"), perm)

    def gather_pair(zero, one):
        own = pick(first_core, zero, one)
        got = jnp.stack([own, move.col(own, 2)])
        got = jnp.concatenate([got, move.col(got, 1)]).reshape(d, own.shape[1])
        both = jnp.stack([got, move.rows(got, STEP_ONE)])
        other = move.rows(both, STEP_TWO)
        return pick(first_core, both, other), pick(first_core, other, both)

    def scatter_pair(zero, one):
        send, keep = pick(first_core, one, zero), pick(first_core, zero, one)
        got = move.rows(send, STEP_TWO_BACK)
        both = (keep.astype(F32) + got.astype(F32)).astype(BF)
        got = move.rows(both[1], STEP_ONE)
        one_block = (both[0].astype(F32) + got.astype(F32)).astype(BF)
        cut = one_block.reshape(2, 2, block, one_block.shape[1])
        cut = (cut[0].astype(F32) + move.col(cut[1], 1).astype(F32)).astype(BF)
        return cut[0].astype(F32) + move.col(cut[1], 2).astype(F32)

    padded = jnp.pad(embed_table, ((0, 0), (0, 2 * width - vocab)))
    table_own = pick(first_core, padded[:, :width], padded[:, width:])

    pack_self = jnp.concatenate([w_query, w_key, w_value, w_attn_out.T], axis=1)
    pack_cross = jnp.concatenate([w_cross_query, w_cross_key, w_cross_value, w_cross_out.T], axis=1)
    pack_ff = [
        jnp.concatenate([w[:, s : s + ff_half] for w in (w_gate, w_up, w_ff_out)], axis=1)
        for s in (0, ff_half)
    ]
    gains_own = jnp.stack([gain_self, gain_cross, gain_ff, gain_final])
    gains = jnp.stack([gains_own, move.col(gains_own, 2)])
    gains = jnp.concatenate([gains, move.col(gains, 1)])
    gains = gains.transpose(1, 0, 2).reshape(4, d, 1)
    g_self, g_cross, g_ff, g_final = (gains[n] for n in range(4))

    perm = []
    for i in range(dp):
        for r in range(4):
            for c in range(4):
                dest = ((i - i % 2 + r // 2) * 4 + c) * 4 + 2 * (i % 2) + r % 2
                perm.append(((i * 4 + r) * 4 + c, dest))
    length = lax.ppermute(prefix, ("dp", "row", "col"), perm)
    scalars = jnp.concatenate([half[None], length]).astype(jnp.int32)
    info = {"tq": tq, "heads": heads, "scalars": scalars}

    states_low = bring(inputs)
    ws, wc = gather_pair(pack_self, pack_cross)
    enc_all = bring(encoder)
    wf = gather_pair(*pack_ff)
    table_one = move.rows(table_own, STEP_ONE)
    table_two = move.rows(jnp.stack([table_own, table_one]), SAME_TWO)
    table = (table_own, table_one, table_two)

    hw = heads * HEAD
    states_all = states_low.astype(F32)
    normed_all, scale_all = norm_forward(states_all, g_self)

    def own_lanes(x, axis=1):
        return lax.dynamic_slice_in_dim(x, half * tq, tq, axis)

    states = own_lanes(states_low).astype(F32)
    qkv = project(ws, normed_all, 0, 3 * hw)
    self_args = ((qkv, 0, True), (qkv, heads), (qkv, 2 * heads))
    attended, totals_self = attend_forward(info, *self_args, True)
    branch = combine(ws, attended, 3 * hw, 4 * hw)
    first = states + (branch + move.core(branch))

    normed_cross, scale_cross = norm_forward(first, g_cross)
    cq = project(wc, normed_cross, 0, hw)
    ckv = project(wc, enc_all, hw, 3 * hw)
    cross_args = ((cq, 0, False), (ckv, 0), (ckv, heads))
    crossed, totals_cross = attend_forward(info, *cross_args, False)
    branch = combine(wc, crossed, 3 * hw, 4 * hw)
    second = first + (branch + move.core(branch))

    normed_ff, scale_ff = norm_forward(second, g_ff)
    *saved, branch = ff_forward(wf, normed_ff)
    third = second + (branch + move.core(branch))
    out_low = third.astype(BF)
    output = hand_back(out_low.reshape(4, block, tq))

    normed_final, scale_final = norm_forward(third, g_final)

    def swap_bits(n):
        return n // 2 + 2 * (n % 2)

    def reorder(x, index):
        parts = x.reshape(4, block, x.shape[-1])
        return jnp.concatenate(
            [lax.dynamic_index_in_dim(parts, i, 0, keepdims=False) for i in index], axis=0
        )

    piece = lax.dynamic_slice_in_dim(normed_final, core * tc, tc, 1)
    piece = reorder(piece, [swap_bits(col ^ row ^ s) for s in range(4)])
    got = jnp.stack([piece, move.col(piece, 2)])
    got = jnp.concatenate([got, move.col(got, 1)])
    hidden = jnp.concatenate([got, move.core(got)])

    other_targets = move.core(targets)
    near, far = pick(mine, targets, other_targets), pick(mine, other_targets, targets)

    def target_chunks(which_core):
        out = []
        for seq_targets, lo in ((near, half), (far, half), (near, 1 - half), (far, 1 - half)):
            out.append(lax.dynamic_slice_in_dim(seq_targets, lo * tq + which_core * tc, tc, 0))
        return out

    wanted = jnp.stack(target_chunks(core) + target_chunks(1 - core))
    wanted = wanted - col * vocab
    wanted = jnp.where((wanted >= 0) & (wanted < vocab), wanted - core * width, -1)[:, None, :]
    valid = jnp.where(first_core, width, vocab - width)
    vocab_scalars = jnp.stack([valid, core]).astype(jnp.int32)
    exps, tops, top, total, picked = vocab_forward(vocab_scalars, hidden, table, wanted)

    def merge(items):
        peak = items[0][0]
        for item in items[1:]:
            peak = jnp.maximum(peak, item[0])
        amount = sum(item[1] * jnp.exp(item[0] - peak) for item in items)
        return jnp.stack([peak, amount, sum(item[2] for item in items)])

    stats = jnp.stack([top[:, 0], total[:, 0], picked[:, 0]])
    stats = merge([stats, jnp.roll(move.core(stats), 4, axis=1)])
    cube = stats.reshape(3, 2, 2, 2, tc)
    items = [cube]
    for bit in (1, 2, 3):
        come = move.col(cube, bit)
        if bit & 1:
            come = come[:, :, ::-1]
        if bit & 2:
            come = come[:, :, :, ::-1]
        items.append(come)
    stats = merge(items).reshape(3, 8, tc)
    logsum = stats[0] + jnp.log(stats[1])
    losses = logsum - stats[2]

    by_core = losses.reshape(2, 2, 2, tc)
    by_core = pick(first_core, by_core, by_core[::-1])
    by_seq = pick(mine, by_core[:, :, 0], by_core[:, :, 1])
    by_half = pick(half == 0, by_seq, by_seq[:, ::-1])
    loss = by_half.transpose(1, 0, 2).reshape(seq)

    grads, grad_hidden = vocab_hidden_grad(
        vocab_scalars, exps, tops, logsum[:, None], table, wanted
    )
    part = (grad_hidden[:4].astype(F32) + move.core(grad_hidden[4:]).astype(F32)).astype(BF)
    part = (part[:2].astype(F32) + move.col(part[2:], 1).astype(F32)).astype(BF)
    part = (part[0].astype(F32) + move.col(part[1], 2).astype(F32)).astype(BF)
    part = reorder(part, [col ^ row ^ swap_bits(n) for n in range(4)])
    other = move.core(part)
    grad_normed = jnp.concatenate(
        [pick(first_core, part, other), pick(first_core, other, part)], axis=1
    ).astype(F32)

    row_hi, row_lo = row // 2, row % 2
    places = []
    for unit in range(8):
        s_hi, s_lo, sub = unit // 4, unit // 2 % 2, unit % 2
        to_hi = row_lo ^ s_lo ^ row_hi
        to_lo = sub ^ row_lo
        upper = row_hi ^ s_hi
        places.append(
            jnp.where(first_core, to_lo * 4 + to_hi * 2, to_hi * 4 + to_lo * 2) + upper
        )
    places = jnp.stack(places).astype(jnp.int32)
    grad_table = vocab_table_grad(places, hidden, grads)

    through, gg_final = norm_backward(third, g_final, scale_final, grad_normed)
    grad_third = through
    *ff_weight_grads, partial_normed = ff_backward(wf, saved, normed_ff, grad_third.astype(BF))
    grad_normed = partial_normed + move.core(partial_normed)
    through, gg_ff = norm_backward(second, g_ff, scale_ff, grad_normed)
    grad_second = grad_third + through

    low = grad_second.astype(BF)
    grad_crossed = project(wc, low, 3 * hw, 4 * hw)
    dcq, dck, dcv = attend_backward(info, *cross_args, grad_crossed, totals_cross, False)
    partial_normed = combine(wc, dcq, 0, hw)
    grad_normed = partial_normed + move.core(partial_normed)
    through, gg_cross = norm_backward(first, g_cross, scale_cross, grad_normed)
    grad_first = grad_second + through
    grad_enc = source_grads(wc, None, 0, (dck, dcv), (hw, 2 * hw), scalars, hw, BF)
    cross_weight_grads = weight_grads(
        [(normed_cross, dcq), (enc_all, dck), (enc_all, dcv), (low, crossed)], 4 * hw
    )

    low = grad_first.astype(BF)
    grad_attended = project(ws, low, 3 * hw, 4 * hw)
    dq, dk, dv = attend_backward(info, *self_args, grad_attended, totals_self, True)
    partial_normed = source_grads(ws, dq, 0, (dk, dv), (hw, 2 * hw), scalars, hw, F32)
    through, gg_self = norm_backward(states_all, g_self, scale_all, partial_normed)
    zero = jnp.zeros_like(grad_first)
    spot = pick(
        half == 0,
        jnp.concatenate([grad_first, zero], axis=1),
        jnp.concatenate([zero, grad_first], axis=1),
    )
    grad_states = (through + pick(first_core, spot, 0.0)).astype(BF)
    self_weight_grads = weight_grads(
        [(own_lanes(normed_all), dq), (normed_all, dk), (normed_all, dv), (low, attended)], 4 * hw
    )

    grad_encoder = fold_back(grad_enc).astype(F32)
    grad_inputs = fold_back(grad_states).astype(F32)

    table_sum = None
    if dp == 2:
        cut = grad_table.reshape(2, d // 2, width)
        cut = (cut[0].astype(F32) + move.rows(cut[1], STEP_ONE).astype(F32)).astype(BF)
        cut = cut.reshape(2, d // 4, width)
        cut = cut[0].astype(F32) + move.rows(cut[1], SAME_TWO).astype(F32)
        cut = cut.reshape(2, d // 8, width)
        keep, send = pick(first_core, cut[0], cut[1]), pick(first_core, cut[1], cut[0])
        got = move.core(send.astype(BF)).astype(F32)
        table_sum = jnp.concatenate(
            [pick(first_core, keep, got), pick(first_core, got, keep)[:, : vocab - width]], axis=1
        )
    else:
        units = grad_table.reshape(8, d // 8, width)
        ordered = []
        for e in range(8):
            rel = (e // 2) ^ row
            at = places[rel * 2 + e % 2]
            ordered.append(lax.dynamic_index_in_dim(units, at, 0, keepdims=False))
        full = jnp.concatenate(ordered, axis=0)
        blank = jnp.zeros_like(full)
        full = pick(
            first_core,
            jnp.concatenate([full, blank], axis=1),
            jnp.concatenate([blank, full], axis=1),
        )[:, :vocab]
        table_sum = lax.psum_scatter(
            full, ("dp", "row"), scatter_dimension=0, tiled=True
        ).astype(F32)

    sum_attn = scatter_pair(self_weight_grads, cross_weight_grads)
    sum_ff = scatter_pair(*ff_weight_grads)

    def split_cores(x, flip_out):
        if flip_out:
            x = jnp.concatenate([x[:, : 3 * hw], x[:, 3 * hw :].T], axis=1)
        rows_half = block // 2
        top_half, low_half = x[:rows_half], x[rows_half:]
        if dp == 2:
            keep = pick(first_core, top_half, low_half)
            got = move.core(pick(first_core, low_half, top_half))
            return pick(first_core, keep, got), pick(first_core, got, keep)
        zero_pack = pick(first_core, x, 0.0).astype(BF)
        one_pack = pick(first_core, 0.0, x).astype(BF)
        both = lax.psum_scatter(
            jnp.concatenate([zero_pack, one_pack], axis=1), "dp", scatter_dimension=0, tiled=True
        ).astype(F32)
        return both[:, : x.shape[1]], both[:, x.shape[1] :]

    out_self, out_cross = split_cores(sum_attn, True)
    out_ff0, out_ff1 = split_cores(sum_ff, False)

    def ff_part(n):
        sl = slice(n * ff_half, (n + 1) * ff_half)
        return jnp.concatenate([out_ff0[:, sl], out_ff1[:, sl]], axis=1)

    once = jnp.where(first_core, 1.0, 0.0)
    packed = jnp.stack([gg_self, gg_cross * once, gg_ff * once, gg_final * once])
    packed = packed.reshape(4, 4, block)
    packed = jnp.stack(
        [
            lax.dynamic_index_in_dim(packed, swap_bits(col ^ f), 1, keepdims=False)
            for f in range(4)
        ],
        axis=1,
    )
    packed = lax.psum(packed, ("dp", "row", "col"))
    packed = lax.dynamic_index_in_dim(packed, col, 1, keepdims=False)

    return (
        output,
        loss,
        grad_inputs,
        grad_encoder,
        packed[0],
        out_self[:, :hw],
        out_self[:, hw : 2 * hw],
        out_self[:, 2 * hw : 3 * hw],
        out_self[:, 3 * hw :],
        packed[1],
        out_cross[:, :hw],
        out_cross[:, hw : 2 * hw],
        out_cross[:, 2 * hw : 3 * hw],
        out_cross[:, 3 * hw :],
        packed[2],
        ff_part(0),
        ff_part(1),
        ff_part(2),
        packed[3],
        table_sum,
    )


def solution(mesh):
    return jax.shard_map(
        partial(local, dp=mesh.shape["dp"]),
        mesh=mesh,
        in_specs=(
            P("col", ("dp", "row")),
            P("col", ("dp", "row")),
            P(("dp", "col")),
            P(("dp", "row")),
            P("col"),
            P("col", "row"),
            P("col", "row"),
            P("col", "row"),
            P("row", "col"),
            P("col"),
            P("col", "row"),
            P("col", "row"),
            P("col", "row"),
            P("row", "col"),
            P("col"),
            P("col", "row"),
            P("col", "row"),
            P("col", "row"),
            P("col"),
            P("row", "col"),
        ),
        out_specs=(
            P("col", ("dp", "row")),
            P(("dp", "row")),
            P("col", ("dp", "row")),
            P("col", ("dp", "row")),
            P("col"),
            P(("col", "dp"), "row"),
            P(("col", "dp"), "row"),
            P(("col", "dp"), "row"),
            P(("row", "dp"), "col"),
            P("col"),
            P(("col", "dp"), "row"),
            P(("col", "dp"), "row"),
            P(("col", "dp"), "row"),
            P(("row", "dp"), "col"),
            P("col"),
            P(("col", "dp"), "row"),
            P(("col", "dp"), "row"),
            P(("col", "dp"), "row"),
            P("col"),
            P(("dp", "row"), "col"),
        ),
        check_vma=False,
    )
```

```python
from functools import partial

import jax
import jax.numpy as jnp
from jax import lax
from jax.experimental import pallas as pl
from jax.experimental.pallas import tpu as pltpu
from jax.sharding import PartitionSpec as P

HEAD = 64
EPS = 1e-06
NEGATIVE = -1e30
BF = jnp.bfloat16
F32 = jnp.float32
MIB = 1 << 20


def mm(left, right, dims):
    return lax.dot_general(left, right, (dims, ((), ())), preferred_element_type=F32)


def nn(left, right):
    return mm(left, right, ((1,), (0,)))


def tn(left, right):
    return mm(left, right, ((0,), (0,)))


def nt(left, right):
    return mm(left, right, ((1,), (1,)))


def params(mib, axes=1):
    return pltpu.CompilerParams(
        dimension_semantics=("arbitrary",) * axes, vmem_limit_bytes=mib * MIB
    )


def whole(shape):
    return pl.BlockSpec(shape, lambda *_: (0,) * len(shape))


def scores_of(key, query, start, prefix, causal):
    scores = tn(key, query * jnp.asarray(HEAD**-0.5, BF))
    if causal:
        keys = lax.broadcasted_iota(jnp.int32, scores.shape, 0)
        rows = lax.broadcasted_iota(jnp.int32, scores.shape, 1) + start
        scores = jnp.where((keys <= rows) | (keys < prefix), scores, NEGATIVE)
    return scores


def attend_forward(info, query, key, value, causal):
    (q_arr, q_row, q_moves), (k_arr, k_row), (v_arr, v_row) = query, key, value
    tq = info["tq"]
    blocks = q_arr.shape[0]
    heads = info["heads"]
    tk = k_arr.shape[2]

    def body(s_ref, q_ref, k_ref, v_ref, o_ref, l_ref):
        scores = scores_of(k_ref[0], q_ref[0], s_ref[0] * tq, s_ref[1], causal)
        top = jnp.max(scores, axis=0, keepdims=True)
        weights = jnp.exp(scores - top)
        total = jnp.sum(weights, axis=0, keepdims=True)
        mixed = nn(v_ref[0], weights.astype(BF))
        o_ref[0] = (mixed / total).astype(BF)
        l_ref[0] = top + jnp.log(total)

    return pl.pallas_call(
        body,
        out_shape=(
            jax.ShapeDtypeStruct((blocks, heads * HEAD, tq), BF),
            jax.ShapeDtypeStruct((blocks * heads, 1, tq), F32),
        ),
        grid_spec=pltpu.PrefetchScalarGridSpec(
            num_scalar_prefetch=1,
            grid=(blocks, heads),
            in_specs=[
                pl.BlockSpec(
                    (1, HEAD, tq), lambda b, h, s: (b, q_row + h, s[0] if q_moves else 0)
                ),
                pl.BlockSpec((1, HEAD, tk), lambda b, h, s: (b, k_row + h, 0)),
                pl.BlockSpec((1, HEAD, tk), lambda b, h, s: (b, v_row + h, 0)),
            ],
            out_specs=(
                pl.BlockSpec((1, HEAD, tq), lambda b, h, s: (b, h, 0)),
                pl.BlockSpec((1, 1, tq), lambda b, h, s: (b * heads + h, 0, 0)),
            ),
        ),
        compiler_params=params(48, 2),
    )(info["scalars"], q_arr, k_arr, v_arr)


def attend_backward(info, query, key, value, incoming, totals, causal):
    (q_arr, q_row, q_moves), (k_arr, k_row), (v_arr, v_row) = query, key, value
    tq = info["tq"]
    blocks = q_arr.shape[0]
    heads = info["heads"]
    tk = k_arr.shape[2]

    def body(s_ref, q_ref, k_ref, v_ref, g_ref, l_ref, dq_ref, dk_ref, dv_ref):
        q = q_ref[0]
        scores = scores_of(k_ref[0], q, s_ref[0] * tq, s_ref[1], causal)
        weights = jnp.exp(scores - l_ref[0])
        dp = tn(v_ref[0], g_ref[0])
        inner = weights * dp
        centre = jnp.sum(inner, axis=0, keepdims=True)
        ds = (inner - weights * centre).astype(BF)
        dv_ref[0] = nt(g_ref[0], weights.astype(BF)).astype(BF)
        dq_ref[0] = (nn(k_ref[0], ds) * HEAD**-0.5).astype(BF)
        dk_ref[0] = (nt(q, ds) * HEAD**-0.5).astype(BF)

    return pl.pallas_call(
        body,
        out_shape=(
            jax.ShapeDtypeStruct((blocks, heads * HEAD, tq), BF),
            jax.ShapeDtypeStruct((blocks, heads * HEAD, tk), BF),
            jax.ShapeDtypeStruct((blocks, heads * HEAD, tk), BF),
        ),
        grid_spec=pltpu.PrefetchScalarGridSpec(
            num_scalar_prefetch=1,
            grid=(blocks, heads),
            in_specs=[
                pl.BlockSpec(
                    (1, HEAD, tq), lambda b, h, s: (b, q_row + h, s[0] if q_moves else 0)
                ),
                pl.BlockSpec((1, HEAD, tk), lambda b, h, s: (b, k_row + h, 0)),
                pl.BlockSpec((1, HEAD, tk), lambda b, h, s: (b, v_row + h, 0)),
                pl.BlockSpec((1, HEAD, tq), lambda b, h, s: (b, h, 0)),
                pl.BlockSpec((1, 1, tq), lambda b, h, s: (b * heads + h, 0, 0)),
            ],
            out_specs=(
                pl.BlockSpec((1, HEAD, tq), lambda b, h, s: (b, h, 0)),
                pl.BlockSpec((1, HEAD, tk), lambda b, h, s: (b, h, 0)),
                pl.BlockSpec((1, HEAD, tk), lambda b, h, s: (b, h, 0)),
            ),
        ),
        compiler_params=params(48, 2),
    )(info["scalars"], q_arr, k_arr, v_arr, incoming, totals)


GELU_A = 0.7978845608028654
GELU_B = 0.044715


def gelu_parts(gate):
    inner = jnp.tanh(GELU_A * (gate + GELU_B * gate * gate * gate))
    value = 0.5 * gate * (1.0 + inner)
    slope = 0.5 * (1.0 + inner) + 0.5 * gate * (1.0 - inner * inner) * (
        GELU_A * (1.0 + 3.0 * GELU_B * gate * gate)
    )
    return value, slope


def ff_forward(packs, normed):
    d, lanes = packs[0].shape
    wide = lanes // 3
    tokens = normed.shape[1]
    n = len(packs)

    def body(*refs):
        w_refs, x_ref, save_refs, out_ref = refs[:n], refs[n], refs[n + 1 : 2 * n + 1], refs[-1]
        for b, (w_ref, save_ref) in enumerate(zip(w_refs, save_refs)):
            both = tn(w_ref[:, : 2 * wide], x_ref[...])
            save_ref[...] = both.astype(BF)
            value, _ = gelu_parts(both[:wide])
            hidden = (value * both[wide:]).astype(BF)
            part = nn(w_ref[:, 2 * wide :], hidden)
            out_ref[...] = part if b == 0 else out_ref[...] + part

    return pl.pallas_call(
        body,
        out_shape=[jax.ShapeDtypeStruct((2 * wide, tokens), BF)] * n
        + [jax.ShapeDtypeStruct((d, tokens), F32)],
        compiler_params=params(48, 0),
    )(*packs, normed)


def ff_backward(order, packs, saved, normed, grad):
    d, lanes = packs[0].shape
    wide = lanes // 3
    tokens = normed.shape[1]
    n = len(packs)

    def body(s_ref, *refs):
        w_refs, save_refs = refs[:n], refs[n : 2 * n]
        x_ref, g_ref, dw_ref, out_ref = refs[2 * n :]
        for b, (w_ref, save_ref) in enumerate(zip(w_refs, save_refs)):
            dh = tn(w_ref[:, 2 * wide :], g_ref[...])
            gate, up = save_ref[:wide].astype(F32), save_ref[wide:].astype(F32)
            value, slope = gelu_parts(gate)
            hidden = (value * up).astype(BF)
            grads = jnp.concatenate(
                [(dh * up * slope).astype(BF), (dh * value).astype(BF)], axis=0
            )
            first = nt(x_ref[...], grads).astype(BF)
            second = nt(g_ref[...], hidden).astype(BF)
            dw_ref[s_ref[b], :, : 2 * wide] = first
            dw_ref[s_ref[b], :, 2 * wide :] = second
            part = nn(w_ref[:, : 2 * wide], grads)
            out_ref[...] = part if b == 0 else out_ref[...] + part

    return pl.pallas_call(
        body,
        out_shape=(
            jax.ShapeDtypeStruct((n, d, lanes), BF),
            jax.ShapeDtypeStruct((d, tokens), F32),
        ),
        grid_spec=pltpu.PrefetchScalarGridSpec(
            num_scalar_prefetch=1,
            grid=(1,),
            in_specs=[whole((d, lanes))] * n
            + [whole((2 * wide, tokens))] * n
            + [whole((d, tokens))] * 2,
            out_specs=(whole((n, d, lanes)), whole((d, tokens))),
        ),
        compiler_params=params(60),
    )(order, *packs, *saved, normed, grad)


def norm_in(parts, gain, tokens, tile=256):
    d = parts[0].shape[0]
    n = len(parts)

    def body(*refs):
        x_refs, g_ref, sum_ref, norm_ref, scale_ref = refs[:n], refs[n], *refs[n + 1 :]
        states = x_refs[0][...].astype(F32)
        if n > 1:
            rest = x_refs[1][...]
            for ref in x_refs[2:]:
                rest = rest + ref[...]
            states = states + rest
        scale = lax.rsqrt(jnp.mean(states * states, axis=0, keepdims=True) + EPS)
        sum_ref[...] = states
        scale_ref[...] = scale
        norm_ref[...] = (states * scale * g_ref[...]).astype(BF)

    spec = pl.BlockSpec((d, tile), lambda i: (0, i))
    return pl.pallas_call(
        body,
        grid=(tokens // tile,),
        in_specs=[spec] * n + [whole((d, 1))],
        out_specs=(spec, spec, pl.BlockSpec((1, tile), lambda i: (0, i))),
        out_shape=(
            jax.ShapeDtypeStruct((d, tokens), F32),
            jax.ShapeDtypeStruct((d, tokens), BF),
            jax.ShapeDtypeStruct((1, tokens), F32),
        ),
        compiler_params=params(40),
    )(*parts, gain)


def norm_out(scalars, states, gain, scale, incoming, before, place=False, tile=256):
    d, tokens = states.shape
    n = len(incoming)
    has = before is not None
    own_tiles = before.shape[1] // tile if has else 1

    def body(*refs):
        s_ref, x_ref, g_ref, r_ref = refs[:4]
        y_refs = refs[4 : 4 + n]
        b_ref = refs[4 + n] if has else None
        outs = refs[4 + n + has :]
        i = pl.program_id(0)
        states_now = x_ref[...].astype(F32)
        dy = y_refs[0][...].astype(F32)
        for ref in y_refs[1:]:
            dy = dy + ref[...].astype(F32)
        scale_now = r_ref[...]
        weighted = dy * g_ref[...]
        inner = jnp.mean(weighted * states_now, axis=0, keepdims=True)
        total = scale_now * weighted - states_now * (scale_now * scale_now * scale_now * inner)
        if has and place:
            here = (i // own_tiles == s_ref[0]) & (s_ref[2] == 0)
            total = total + b_ref[...] * jnp.where(here, 1.0, 0.0)
        elif has:
            total = total + b_ref[...]
        gain_grad = jnp.sum(dy * states_now * scale_now, axis=1, keepdims=True)
        low_ref, gain_ref = outs[-2:]
        if not place:
            outs[0][...] = total
        low_ref[...] = total.astype(BF)

        @pl.when(i == 0)
        def _():
            gain_ref[...] = gain_grad

        @pl.when(i > 0)
        def _():
            gain_ref[...] += gain_grad

    spec = pl.BlockSpec((d, tile), lambda i, s: (0, i))
    out_shape = [] if place else [jax.ShapeDtypeStruct((d, tokens), F32)]
    out_shape += [jax.ShapeDtypeStruct((d, tokens), BF), jax.ShapeDtypeStruct((d, 1), F32)]
    return pl.pallas_call(
        body,
        out_shape=out_shape,
        grid_spec=pltpu.PrefetchScalarGridSpec(
            num_scalar_prefetch=1,
            grid=(tokens // tile,),
            in_specs=[spec, whole((d, 1)), pl.BlockSpec((1, tile), lambda i, s: (0, i))]
            + [spec] * n
            + ([pl.BlockSpec((d, tile), lambda i, s: (0, i % own_tiles))] if has else []),
            out_specs=[spec] * (len(out_shape) - 1) + [whole((d, 1))],
        ),
        compiler_params=params(40),
    )(scalars, states, gain, scale, *incoming, *([before] if has else []))


def lane_block(lanes, low, high):
    if low // 256 == (high - 1) // 256 and lanes % 256 == 0:
        return 256, low // 256, low % 256
    return lanes, 0, low


def project(pack, normed, low, high):
    blocks, d, lanes = pack.shape
    tokens = normed.shape[1]
    size, index, at = lane_block(lanes, low, high)

    def body(w_ref, x_ref, o_ref):
        o_ref[0] = tn(w_ref[0, :, at : at + high - low], x_ref[...]).astype(BF)

    return pl.pallas_call(
        body,
        grid=(blocks,),
        in_specs=[pl.BlockSpec((1, d, size), lambda b: (b, 0, index)), whole((d, tokens))],
        out_specs=pl.BlockSpec((1, high - low, tokens), lambda b: (b, 0, 0)),
        out_shape=jax.ShapeDtypeStruct((blocks, high - low, tokens), BF),
        compiler_params=params(40),
    )(pack, normed)


def combine(pack, rows, low, high):
    blocks, d, lanes = pack.shape
    tokens = rows.shape[2]
    size, index, at = lane_block(lanes, low, high)

    def body(w_ref, x_ref, o_ref):
        part = nn(w_ref[0, :, at : at + high - low], x_ref[0])
        for b in range(1, blocks):
            part += nn(w_ref[b, :, at : at + high - low], x_ref[b])
        o_ref[...] = part

    return pl.pallas_call(
        body,
        grid=(1,),
        in_specs=[
            pl.BlockSpec((blocks, d, size), lambda b: (0, 0, index)),
            whole((blocks, high - low, tokens)),
        ],
        out_specs=whole((d, tokens)),
        out_shape=jax.ShapeDtypeStruct((d, tokens), F32),
        compiler_params=params(40),
    )(pack, rows)


def weight_grads(scalars, pairs, lanes):
    d = pairs[0][0].shape[0]
    n = len(pairs)
    lefts = [left for left, _ in pairs]
    rights = [right for _, right in pairs]

    def body(*refs):
        outs = refs[2 * n + 1 :]
        at = 0
        for left_ref, right_ref in zip(refs[1 : n + 1], refs[n + 1 : 2 * n + 1]):
            width = right_ref.shape[1]
            for b, out_ref in enumerate(outs):
                out_ref[:, at : at + width] = nt(left_ref[...], right_ref[b]).astype(BF)
            at += width

    def left_spec(left, right):
        tokens = right.shape[2]
        if left.shape[1] == tokens:
            return pl.BlockSpec((d, tokens), lambda b, s: (0, 0))
        return pl.BlockSpec((d, tokens), lambda b, s: (0, s[0]))

    return pl.pallas_call(
        body,
        out_shape=[jax.ShapeDtypeStruct((d, lanes), BF)] * 2,
        grid_spec=pltpu.PrefetchScalarGridSpec(
            num_scalar_prefetch=1,
            grid=(1,),
            in_specs=[left_spec(left, right) for left, right in pairs]
            + [whole(right.shape) for right in rights],
            out_specs=[whole((d, lanes))] * 2,
        ),
        compiler_params=params(48),
    )(scalars, *lefts, *rights)


def split_sum(parts):
    d, lanes = parts[0].shape
    size = d // 4
    n = len(parts)

    def body(*refs):
        for f, out_ref in enumerate(refs[n:]):
            rows = slice(f * size, (f + 1) * size)
            acc = refs[0][rows].astype(F32)
            for ref in refs[1:n]:
                acc += ref[rows].astype(F32)
            out_ref[...] = acc.astype(BF)

    return pl.pallas_call(
        body,
        out_shape=[jax.ShapeDtypeStruct((size, lanes), BF)] * 4,
        compiler_params=params(40, 0),
    )(*parts)


def source_grads(pack, own, own_low, wide, wide_low, place, width, kind):
    blocks, d, lanes = pack.shape
    tq = own.shape[2] if own is not None else 0
    n = len(wide)
    tokens = wide[0].shape[2]
    step = min(1024, tokens)

    def body(*refs):
        s_ref, w_ref = refs[0], refs[1]
        wide_refs = refs[2 : 2 + n]
        o_ref = refs[-1]
        acc = jnp.zeros((d, step), F32)
        for b in range(blocks):
            for at, ref in zip(wide_low, wide_refs):
                acc += nn(w_ref[b, :, at : at + width], ref[b])
        o_ref[...] = acc.astype(kind)
        if own is not None:
            own_ref = refs[2 + n]
            part = jnp.zeros((d, tq), F32)
            for b in range(blocks):
                part += nn(w_ref[b, :, own_low : own_low + width], own_ref[b])
            where = pl.ds(pl.multiple_of(s_ref[0] * tq, tq), tq)
            o_ref[:, where] += part.astype(kind)

    return pl.pallas_call(
        body,
        out_shape=jax.ShapeDtypeStruct((d, tokens), kind),
        grid_spec=pltpu.PrefetchScalarGridSpec(
            num_scalar_prefetch=1,
            grid=(tokens // step,),
            in_specs=[pl.BlockSpec((blocks, d, lanes), lambda i, s: (0, 0, 0))]
            + [pl.BlockSpec((blocks, width, step), lambda i, s: (0, 0, i))] * n
            + (
                [pl.BlockSpec((blocks, width, tq), lambda i, s: (0, 0, 0))]
                if own is not None
                else []
            ),
            out_specs=pl.BlockSpec((d, step), lambda i, s: (0, i)),
        ),
        compiler_params=params(40),
    )(place, pack, *wide, *([own] if own is not None else []))


VB = 512


def assemble(s_ref, own_ref, one_ref, two_ref, three_ref, out_ref):
    size = own_ref.shape[0]
    out_ref[:size] = own_ref[...]
    out_ref[pl.ds(pl.multiple_of((1 + s_ref[1]) * size, size), size), :] = one_ref[...]
    out_ref[pl.ds(pl.multiple_of((2 - s_ref[1]) * size, size), size), :] = two_ref[...]
    out_ref[3 * size :] = three_ref[...]


def table_specs(size):
    return [pl.BlockSpec((size, VB), lambda v, s: (0, v))] * 4


def vocab_forward(scalars, hidden, table, wanted):
    half_chunks, d, step = hidden[0].shape
    chunks = 2 * half_chunks
    own = table[0]
    size, width = own.shape
    parts = width // VB

    def body(s_ref, h0_ref, h1_ref, own_ref, one_ref, two_ref, three_ref, t_ref, e_ref, m_ref, st_ref, blk, flip):
        vb = pl.program_id(0)

        @pl.when(vb == 0)
        def _():
            st_ref[0] = jnp.full((chunks, step), NEGATIVE, F32)
            st_ref[1:] = jnp.zeros((2, chunks, step), F32)

        assemble(s_ref, own_ref, one_ref, two_ref, three_ref, blk)
        flip[...] = blk[...].T
        ids = lax.broadcasted_iota(jnp.int32, (VB, step), 0)

        def one_chunk(n, states, masked):
            logits = nn(flip[...], states)
            row = slice(n, n + 1)
            st_ref[2, row] += jnp.sum(
                jnp.where(ids == t_ref[row] - vb * VB, logits, 0.0), axis=0, keepdims=True
            )
            if masked:
                logits = jnp.where(ids < s_ref[0] - vb * VB, logits, NEGATIVE)
            before = st_ref[0, row]
            top = jnp.maximum(before, jnp.max(logits, axis=0, keepdims=True))
            exps = jnp.exp(logits - top)
            st_ref[1, row] = st_ref[1, row] * jnp.exp(before - top) + jnp.sum(
                exps, axis=0, keepdims=True
            )
            st_ref[0, row] = top
            m_ref[0, row] = top
            e_ref[n] = exps.astype(BF)

        def some(masked):
            for n in range(chunks):
                one_chunk(n, (h0_ref, h1_ref)[n // half_chunks][n % half_chunks], masked)

        inside = (vb + 1) * VB <= s_ref[0]
        pl.when(inside)(partial(some, False))
        pl.when(jnp.logical_not(inside))(partial(some, True))

    return pl.pallas_call(
        body,
        out_shape=(
            jax.ShapeDtypeStruct((chunks, width, step), BF),
            jax.ShapeDtypeStruct((parts, chunks, step), F32),
            jax.ShapeDtypeStruct((3, chunks, step), F32),
        ),
        grid_spec=pltpu.PrefetchScalarGridSpec(
            num_scalar_prefetch=1,
            grid=(parts,),
            in_specs=[whole((half_chunks, d, step))] * 2
            + table_specs(size)
            + [whole((chunks, step))],
            out_specs=(
                pl.BlockSpec((chunks, VB, step), lambda v, s: (0, v, 0)),
                pl.BlockSpec((1, chunks, step), lambda v, s: (v, 0, 0)),
                whole((3, chunks, step)),
            ),
            scratch_shapes=[pltpu.VMEM((d, VB), BF), pltpu.VMEM((VB, d), BF)],
        ),
        compiler_params=params(48),
    )(scalars, *hidden, *table, wanted)


def vocab_hidden_grad(scalars, exps, tops, logsum, first_row, table, wanted):
    chunks, width, step = exps.shape
    own = table[0]
    size = own.shape[0]
    d = 4 * size
    parts = width // VB

    def body(s_ref, e_ref, m_ref, l_ref, own_ref, one_ref, two_ref, three_ref, t_ref, g_ref, o_ref, p_ref, blk, acc):
        vb = pl.program_id(0)

        @pl.when(vb == 0)
        def _():
            acc[...] = jnp.zeros_like(acc)

        assemble(s_ref, own_ref, one_ref, two_ref, three_ref, blk)
        ids = lax.broadcasted_iota(jnp.int32, (VB, step), 0)

        for n in range(chunks):
            row, at = slice(n, n + 1), slice(first_row + n, first_row + n + 1)
            scale = jnp.exp(m_ref[0, row] - l_ref[at])
            probs = e_ref[n].astype(F32) * scale
            grads = jnp.where(ids == t_ref[row] - vb * VB, probs - 1.0, probs).astype(BF)
            g_ref[n] = grads
            acc[n] += nn(blk[...], grads)

        @pl.when(vb == parts - 1)
        def _():
            o_ref[...] = acc[: chunks // 2].astype(BF)
            p_ref[...] = acc[chunks // 2 :].astype(BF)

    return pl.pallas_call(
        body,
        out_shape=(
            jax.ShapeDtypeStruct((chunks, width, step), BF),
            jax.ShapeDtypeStruct((chunks // 2, d, step), BF),
            jax.ShapeDtypeStruct((chunks // 2, d, step), BF),
        ),
        grid_spec=pltpu.PrefetchScalarGridSpec(
            num_scalar_prefetch=1,
            grid=(parts,),
            in_specs=[
                pl.BlockSpec((chunks, VB, step), lambda v, s: (0, v, 0)),
                pl.BlockSpec((1, chunks, step), lambda v, s: (v, 0, 0)),
                whole(logsum.shape),
            ]
            + table_specs(size)
            + [whole((chunks, step))],
            out_specs=(
                pl.BlockSpec((chunks, VB, step), lambda v, s: (0, v, 0)),
                whole((chunks // 2, d, step)),
                whole((chunks // 2, d, step)),
            ),
            scratch_shapes=[pltpu.VMEM((d, VB), BF), pltpu.VMEM((chunks, d, step), F32)],
        ),
        input_output_aliases={1: 0},
        compiler_params=params(56),
    )(scalars, exps, tops, logsum, *table, wanted)


def vocab_table_grad(places, hidden, grads):
    per, d, step = hidden[0].shape
    chunks, width, _ = grads[0].shape
    unit = d // 8
    parts = width // VB
    nh, ng = len(hidden), len(grads)

    def body(*refs):
        s_ref, h_refs, g_refs, o_ref = refs[0], refs[1 : 1 + nh], refs[1 + nh : -1], refs[-1]
        acc = None
        for n in range(nh * per):
            part = nt(h_refs[n // per][n % per], g_refs[n // chunks][n % chunks])
            acc = part if acc is None else acc + part
        for u in range(8):
            spot = pl.ds(pl.multiple_of(s_ref[u] * unit, unit), unit)
            o_ref[spot, :] = acc[u * unit : (u + 1) * unit].astype(BF)

    return pl.pallas_call(
        body,
        out_shape=jax.ShapeDtypeStruct((d, width), BF),
        grid_spec=pltpu.PrefetchScalarGridSpec(
            num_scalar_prefetch=1,
            grid=(parts,),
            in_specs=[whole((per, d, step))] * nh
            + [pl.BlockSpec((chunks, VB, step), lambda v, s: (0, v, 0))] * ng,
            out_specs=pl.BlockSpec((d, VB), lambda v, s: (0, v)),
        ),
        compiler_params=params(48),
    )(places, *hidden, *grads)


def merge_core(mine, other):
    def body(a_ref, b_ref, o_ref):
        for i in range(8):
            row, far = slice(i, i + 1), slice(i ^ 2, (i ^ 2) + 1)
            top = jnp.maximum(a_ref[0, row], b_ref[0, far])
            o_ref[0, row] = top
            o_ref[1, row] = a_ref[1, row] * jnp.exp(a_ref[0, row] - top) + b_ref[
                1, far
            ] * jnp.exp(b_ref[0, far] - top)
            o_ref[2, row] = a_ref[2, row] + b_ref[2, far]

    return pl.pallas_call(
        body,
        out_shape=jax.ShapeDtypeStruct(mine.shape, F32),
        compiler_params=params(16, 0),
    )(mine, other)


def merge_chips(spots, items):
    step = items[0].shape[2]
    flips = (0, 4, 1, 5)

    def body(s_ref, *refs):
        log_ref, loss_ref, rows = refs[-3:]
        for i in range(8):
            at = [slice(i ^ f, (i ^ f) + 1) for f in flips]
            top = refs[0][0, at[0]]
            for ref, row in zip(refs[1:4], at[1:]):
                top = jnp.maximum(top, ref[0, row])
            total = jnp.zeros((1, step), F32)
            picked = jnp.zeros((1, step), F32)
            for ref, row in zip(refs[:4], at):
                total += ref[1, row] * jnp.exp(ref[0, row] - top)
                picked += ref[2, row]
            logsum = top + jnp.log(total)
            log_ref[at[0]] = logsum
            rows[i] = logsum - picked
        for n in range(4):
            loss_ref[n] = rows[s_ref[n]]

    return pl.pallas_call(
        body,
        out_shape=(
            jax.ShapeDtypeStruct((8, step), F32),
            jax.ShapeDtypeStruct((4, 1, step), F32),
        ),
        grid_spec=pltpu.PrefetchScalarGridSpec(
            num_scalar_prefetch=1,
            grid=(1,),
            in_specs=[whole(items[0].shape)] * 4,
            out_specs=(whole((8, step)), whole((4, 1, step))),
            scratch_shapes=[pltpu.VMEM((8, 1, step), F32)],
        ),
        compiler_params=params(16),
    )(spots, *items)


class Moves:
    def __init__(self, dp):
        self.dp = dp

    def core(self, x):
        return lax.ppermute(x, "dp", [(i, i ^ 1) for i in range(self.dp)])

    def col(self, x, bit):
        return lax.ppermute(x, "col", [(i, i ^ bit) for i in range(4)])

    def cols(self, x, bit, core):
        perm = []
        for i in range(core, self.dp, 2):
            for c in range(4):
                perm.append((i * 4 + c, i * 4 + (c ^ bit)))
        return lax.ppermute(x, ("dp", "col"), perm)

    def row(self, x, bit):
        return lax.ppermute(x, "row", [(i, i ^ bit) for i in range(4)])

    def rows(self, x, pairs):
        perm = []
        for i in range(self.dp):
            for r in range(4):
                if i % 2 in pairs:
                    flip, bit = pairs[i % 2]
                    perm.append((i * 4 + r, (i ^ flip) * 4 + (r ^ bit)))
        return lax.ppermute(x, ("dp", "row"), perm)

    def spread(self, x, turn, back=False):
        perm = []
        for i in range(self.dp):
            for c in range(4):
                dest = (i - i % 2 + c // 2) * 4 + 2 * (i % 2) + (c % 2 ^ turn)
                perm.append((dest, i * 4 + c) if back else (i * 4 + c, dest))
        return lax.ppermute(x, ("dp", "col"), perm)


STEP_ONE = {0: (0, 1), 1: (0, 2)}
STEP_TWO = {0: (1, 2), 1: (1, 1)}
STEP_TWO_BACK = {0: (1, 1), 1: (1, 2)}
SAME_TWO = {0: (0, 2), 1: (0, 1)}


def same(bit):
    return {0: (0, bit), 1: (0, bit)}


def tie(*xs):
    return lax.optimization_barrier(xs)


def plus(a, b, kind=BF):
    return (a.astype(F32) + b.astype(F32)).astype(kind)


def local(
    inputs,
    encoder,
    prefix,
    targets,
    gain_self,
    w_query,
    w_key,
    w_value,
    w_attn_out,
    gain_cross,
    w_cross_query,
    w_cross_key,
    w_cross_value,
    w_cross_out,
    gain_ff,
    w_gate,
    w_up,
    w_ff_out,
    gain_final,
    embed_table,
    *,
    dp,
):
    move = Moves(dp)
    core = lax.axis_index("dp") % 2
    row = lax.axis_index("row")
    col = lax.axis_index("col")
    first_core = core == 0
    side = col // 2
    half = col % 2
    block = inputs.shape[0]
    d = 4 * block
    seq = inputs.shape[1]
    tq = seq // 2
    tc = tq // 2
    heads = w_query.shape[1] // HEAD
    hw = heads * HEAD
    ff_half = w_gate.shape[1] // 2
    vocab = embed_table.shape[1]
    width = -(-vocab // (2 * VB)) * VB
    mine = side == core
    pick = jnp.where

    def settle(got):
        other = move.core(got)
        near, far = pick(mine, got, other), pick(mine, other, got)
        return jnp.concatenate([near[0], far[0], near[1], far[1]], axis=0)

    def hand_back(parts):
        hi = [pick(mine, parts[0], parts[1]), pick(mine, parts[2], parts[3])]
        return [move.spread(hi[0], 0, True), move.spread(hi[1], 1, True)]

    def in_order(got):
        return pick(
            half == 0,
            jnp.concatenate([got[0], got[1]], axis=1),
            jnp.concatenate([got[1], got[0]], axis=1),
        )

    def fold_core(partial_sum):
        blocks4 = partial_sum.reshape(4, block, -1)
        near = jnp.stack([blocks4[0], blocks4[2]])
        far = jnp.stack([blocks4[1], blocks4[3]])
        return pick(mine, near, far), move.core(pick(mine, far, near))

    def fold_out(keep, got):
        return [move.spread(plus(keep[n], got[n]), n, True) for n in range(2)]

    def z_sum(parts, cores):
        own, two, one, three = split_sum(parts)
        send = [(two, 2), (one, 1), (three, 3)]
        if cores is None:
            return [own] + [move.col(x, bit) for x, bit in send]
        return [own] + [move.cols(x, bit, cores) for x, bit in send]

    def total(parts):
        return sum(x.astype(F32) for x in parts)

    def swap_bits(n):
        return n // 2 + 2 * (n % 2)

    other_targets = move.core(targets)
    near, far = pick(mine, targets, other_targets), pick(mine, other_targets, targets)

    def target_chunks(lo):
        out = []
        for which in (core, 1 - core):
            for seq_targets in (near, far):
                out.append(lax.dynamic_slice_in_dim(seq_targets, lo * tq + which * tc, tc, 0))
        wanted = jnp.stack(out) - col * vocab
        return jnp.where((wanted >= 0) & (wanted < vocab), wanted - core * width, -1)

    want_near, want_far = target_chunks(half), target_chunks(1 - half)
    valid = jnp.where(first_core, width, vocab - width)
    vocab_scalars = jnp.stack([valid, core]).astype(jnp.int32)
    chip = jnp.where(mine, 0, 1)
    spots = []
    for lo in range(2):
        for h in range(2):
            spots.append((half ^ lo) * 4 + (core ^ h) * 2 + chip)
    spots = jnp.stack(spots).astype(jnp.int32)
    own_places = jnp.stack([row, row ^ (1 + core), row ^ (2 - core), row ^ 3]).astype(jnp.int32)
    places = []
    for unit in range(8):
        e = 2 * (row ^ (unit // 2)) + unit % 2
        places.append(e % 4 * 2 + e // 4)
    places = jnp.stack(places).astype(jnp.int32)

    pack_self = jnp.concatenate([w_query, w_key, w_value, w_attn_out.T], axis=1)
    pack_cross = jnp.concatenate([w_cross_query, w_cross_key, w_cross_value, w_cross_out.T], axis=1)
    sc_own = pick(first_core, pack_self, pack_cross)
    sc_own, embed_table = tie(sc_own, embed_table)
    padded = jnp.pad(embed_table, ((0, 0), (0, 2 * width - vocab)))
    table_own = pick(first_core, padded[:, :width], padded[:, width:])
    pack_ff = [
        jnp.concatenate([w[:, s : s + ff_half] for w in (w_gate, w_up, w_ff_out)], axis=1)
        for s in (0, ff_half)
    ]
    ff_own = pick(first_core, *pack_ff)

    columns = [gain_self, gain_cross, gain_ff, gain_final]
    tops = [lax.reduce_precision(g, 8, 7) for g in columns]
    columns = tops + [g - t for g, t in zip(columns, tops)]
    high = (prefix // 256).astype(F32)
    columns += [jnp.broadcast_to(high, (block,)), jnp.broadcast_to(prefix - high * 256, (block,))]
    extras = jnp.pad(jnp.stack(columns, axis=1).astype(BF), ((0, 0), (0, 128 - len(columns))))
    x_in = jnp.concatenate([inputs, extras], axis=1)

    sc_got = [move.col(sc_own, bit) for bit in (2, 1, 3)]
    table_one = move.rows(table_own, STEP_ONE)
    table_two = move.rows(table_own, SAME_TWO)
    sc, x_in, ff_own, want_near, want_far, spots, places, own_places, table_one, table_two = tie(
        jnp.concatenate([sc_own, *sc_got]), x_in, ff_own, want_near, want_far, spots, places, own_places, table_one, table_two
    )
    sc_row = move.rows(sc, STEP_ONE)
    x_got = [move.spread(x_in, 0), move.spread(x_in, 1)]
    x_near, x_far, sc_row, sc, ff_own = tie(*x_got, sc_row, sc, ff_own)
    sc_one = move.rows(sc, STEP_TWO)
    sc_two = move.rows(sc_row, STEP_TWO)
    ff_got = [move.col(ff_own, bit) for bit in (2, 1, 3)]
    states_low = settle(jnp.stack([x_near, x_far]))
    small = states_low[:, seq : seq + 16].astype(F32)
    g_self, g_cross, g_ff, g_final = (small[:, n : n + 1] + small[:, n + 4 : n + 5] for n in range(4))
    length = lax.dynamic_slice(small, (swap_bits(col ^ row) * block, 8), (1, 2))
    length = (length[0, :1] * 256 + length[0, 1:]).astype(jnp.int32)
    scalars = jnp.concatenate([half[None], length, core[None]]).astype(jnp.int32)
    info = {"tq": tq, "heads": heads, "scalars": scalars}
    states_all, normed_all, scale_all = norm_in([states_low], g_self, seq)
    states_own = lax.dynamic_slice_in_dim(states_low, half * tq, tq, 1)
    own_blocks = jnp.stack([sc, sc_row])
    normed_all, states_own, own_blocks, scalars, ff_own, *ff_got = tie(
        normed_all, states_own, own_blocks, scalars, ff_own, *ff_got
    )
    ff, enc_in = tie(jnp.concatenate([ff_own, *ff_got]), encoder)
    enc_zero = move.spread(enc_in, 0)
    other_blocks = jnp.stack([sc_one, sc_two])
    ws = pick(first_core, own_blocks, other_blocks)
    wc = pick(first_core, other_blocks, own_blocks)

    qkv = project(ws, normed_all, 0, 3 * hw)
    self_args = ((qkv, 0, True), (qkv, heads), (qkv, 2 * heads))
    qkv, ff = tie(qkv, ff)
    self_args = ((qkv, 0, True), (qkv, heads), (qkv, 2 * heads))
    ff_row = move.rows(ff, STEP_ONE)
    ff_one = move.rows(ff, SAME_TWO)
    attended, totals_self = attend_forward(info, *self_args, True)
    attended, enc_zero, enc_in = tie(attended, enc_zero, enc_in)
    enc_one = move.spread(enc_in, 1)
    branch = combine(ws, attended, 3 * hw, 4 * hw)
    first, normed_cross, scale_cross = norm_in([states_own, branch, move.core(branch)], g_cross, tq)


    cq = project(wc, normed_cross, 0, hw)
    cq, enc_one, ff_row, ff_one = tie(cq, enc_one, ff_row, ff_one)
    ff_two = move.rows(ff_row, SAME_TWO)
    enc_all = settle(jnp.stack([enc_zero, enc_one]))
    ckv = project(wc, enc_all, hw, 3 * hw)
    cross_args = ((cq, 0, False), (ckv, 0), (ckv, heads))
    crossed, totals_cross = attend_forward(info, *cross_args, False)
    crossed, ff_two, table_one = tie(crossed, ff_two, table_one)
    table_three = move.rows(table_one, SAME_TWO)
    branch = combine(wc, crossed, 3 * hw, 4 * hw)
    second, normed_ff, scale_ff = norm_in([first, branch, move.core(branch)], g_ff, tq)

    wf = (ff, ff_row, ff_one, ff_two)
    *saved, branch = ff_forward(wf, normed_ff)
    third, normed_final, scale_final = norm_in([second, branch, move.core(branch)], g_final, tq)

    def reorder(x, index):
        parts = x.reshape(4, block, x.shape[-1])
        return jnp.concatenate(
            [lax.dynamic_index_in_dim(parts, i, 0, keepdims=False) for i in index], axis=0
        )

    piece = lax.dynamic_slice_in_dim(normed_final, core * tc, tc, 1)
    piece = reorder(piece, [swap_bits(col ^ row ^ s) for s in range(4)])
    near_pieces, table_three = tie(jnp.stack([piece, move.col(piece, 2)]), table_three)
    table = (table_own, table_one, table_two, table_three)
    far_pieces = move.col(near_pieces, 1)
    hidden_near = (near_pieces, move.core(near_pieces))
    exps_near, tops_near, stats_near = vocab_forward(
        vocab_scalars, hidden_near, table, want_near
    )
    far_pieces, stats_near, out_low = tie(far_pieces, stats_near, third.astype(BF))
    hidden_far = (far_pieces, move.core(far_pieces))
    out_got = hand_back(out_low.reshape(4, block, tq))
    exps_far, tops_far, stats_far = vocab_forward(vocab_scalars, hidden_far, table, want_far)
    stats_far, *out_got = tie(stats_far, *out_got)

    stats = jnp.concatenate([stats_near, stats_far], axis=1)
    stats = merge_core(stats, move.core(stats))
    items = [stats] + [move.col(stats, bit) for bit in (1, 2, 3)]
    logsum, loss = merge_chips(spots, items)
    loss = loss.reshape(seq)

    grads_far, own_far, oth_far = vocab_hidden_grad(
        vocab_scalars, exps_far, tops_far, logsum, 4, table, want_far
    )
    part_far, exps_near = tie(plus(own_far, move.core(oth_far)), exps_near)
    come_far = move.col(part_far, 1)
    grads_near, own_near, oth_near = vocab_hidden_grad(
        vocab_scalars, exps_near, tops_near, logsum, 0, table, want_near
    )
    part = plus(own_near, move.core(oth_near), F32) + come_far.astype(F32)
    part_last, grads_near = tie(part[1].astype(BF), grads_near)
    come_last = move.col(part_last, 2)
    grad_table = vocab_table_grad(
        places, (*hidden_near, *hidden_far), (grads_near, grads_far)
    )
    if dp == 2:
        table_sum = lax.psum_scatter(grad_table, "row", scatter_dimension=0, tiled=True)
    come_last, _ = tie(come_last, grad_table)
    part = plus(part[0], come_last)
    part = reorder(part, [col ^ row ^ swap_bits(n) for n in range(4)])
    other = move.core(part)
    grad_normed = jnp.concatenate(
        [pick(first_core, part, other), pick(first_core, other, part)], axis=1
    )

    grad_third, low, gg_final = norm_out(
        scalars, third, g_final, scale_final, [grad_normed], None
    )
    ff_grads, partial_normed = ff_backward(own_places, wf, saved, normed_ff, low)
    ff_sum = lax.psum_scatter(ff_grads.reshape(4 * d, -1), "row", scatter_dimension=0, tiled=True)
    grad_second, low, gg_ff = norm_out(
        scalars, second, g_ff, scale_ff, [partial_normed, move.core(partial_normed)], grad_third
    )
    grad_crossed = project(wc, low, 3 * hw, 4 * hw)
    dcq, dck, dcv = attend_backward(info, *cross_args, grad_crossed, totals_cross, False)
    partial_normed = combine(wc, dcq, 0, hw)
    partial_other = move.core(partial_normed)
    dck, partial_normed = tie(dck, partial_normed)
    grad_enc = source_grads(wc, None, 0, (dck, dcv), (hw, 2 * hw), scalars, hw, BF)
    partial_other, grad_enc = tie(partial_other, grad_enc)
    grad_first, low_self, gg_cross = norm_out(
        scalars, first, g_cross, scale_cross, [partial_normed, partial_other], grad_second
    )
    enc_keep, enc_come = fold_core(grad_enc)
    enc_keep, enc_come, low_self, normed_cross = tie(enc_keep, enc_come, low_self, normed_cross)
    enc_come = fold_out(enc_keep, enc_come)
    cross_zero, cross_one = weight_grads(
        scalars, [(normed_cross, dcq), (enc_all, dck), (enc_all, dcv), (low, crossed)], 4 * hw
    )
    cross_zero, cross_one, low_self = tie(cross_zero, cross_one, low_self)
    cross_come = [
        move.rows(cross_zero, {0: (1, 1)}),
        move.rows(cross_one, {0: (1, 3)}),
        move.rows(cross_one, {1: (0, 2)}),
    ]

    grad_attended = project(ws, low_self, 3 * hw, 4 * hw)
    dq, dk, dv = attend_backward(info, *self_args, grad_attended, totals_self, True)
    dq, dk, ff_sum = tie(dq, dk, ff_sum)
    self_zero, self_one = weight_grads(
        scalars, [(normed_all, dq), (normed_all, dk), (normed_all, dv), (low_self, attended)], 4 * hw
    )
    self_come = [
        move.rows(self_one, {0: (0, 1)}),
        move.rows(self_zero, {1: (1, 2)}),
        move.rows(self_one, {1: (1, 3)}),
    ]
    dk, self_zero, ff_sum = tie(dk, self_zero, ff_sum)
    ff_parts = [ff_sum[p * block : (p + 1) * block] for p in range(4)]
    ff_parts[1:] = [move.col(x, bit) for x, bit in zip(ff_parts[1:], (2, 1, 3))]
    partial_normed = source_grads(ws, dq, 0, (dk, dv), (hw, 2 * hw), scalars, hw, F32)
    partial_normed, *cross_come = tie(partial_normed, *cross_come)
    cross_parts = z_sum([cross_zero, *cross_come], 1)
    partial_normed, cross_own = tie(partial_normed, cross_parts[0])
    grad_states, gg_self = norm_out(
        scalars, states_all, g_self, scale_all, [partial_normed], grad_first, True
    )
    once = jnp.where(first_core, 1.0, 0.0)
    gain_columns = jnp.concatenate([gg_self, gg_cross * once, gg_ff * once, gg_final * once], axis=1)
    gain_columns = jnp.pad(gain_columns.astype(BF), ((0, 0), (0, 124)))
    grad_states = jnp.concatenate([grad_states, gain_columns], axis=1)
    grad_states, *enc_come = tie(grad_states, *enc_come)
    in_keep, in_come = fold_core(grad_states)
    in_come = fold_out(in_keep, in_come)
    in_come[0], cross_parts[1:], ff_parts, self_come = tie(
        in_come[0], cross_parts[1:], ff_parts, self_come
    )
    self_parts = z_sum([self_zero, *self_come], 0)
    in_come = in_come[0].astype(F32) + in_come[1].astype(F32)
    in_come, self_own = tie(in_come, self_parts[0])
    packed = in_come[:, seq : seq + 4].T
    if dp == 2:
        come = [move.row(packed, bit) for bit in (1, 2, 3)]
        packed, come, self_parts[1:], table_sum = tie(packed, come, self_parts[1:], table_sum)
        packed = packed + come[0] + come[1] + come[2]
        packed = packed + move.core(packed)
    else:
        packed = lax.psum(packed, ("dp", "row"))

    grad_encoder = enc_come[0].astype(F32) + enc_come[1].astype(F32)
    grad_inputs = in_come[:, :seq]
    sum_self = total([self_own, *self_parts[1:]])
    sum_cross = total([cross_own, *cross_parts[1:]])
    sum_ff = total(ff_parts)

    if dp == 2:
        cut = table_sum.reshape(2, d // 8, width)
        keep, got = pick(first_core, cut[0], cut[1]), move.core(pick(first_core, cut[1], cut[0]))
        table_sum = jnp.concatenate(
            [pick(first_core, keep, got), pick(first_core, got, keep)[:, : vocab - width]], axis=1
        ).astype(F32)
    else:
        full = grad_table.reshape(4, 2, d // 8, width).transpose(1, 0, 2, 3).reshape(d, width)
        blank = jnp.zeros_like(full)
        full = pick(
            first_core,
            jnp.concatenate([full, blank], axis=1),
            jnp.concatenate([blank, full], axis=1),
        )[:, :vocab]
        table_sum = lax.psum_scatter(
            full, ("dp", "row"), scatter_dimension=0, tiled=True
        ).astype(F32)

    def flip_last(x):
        return jnp.concatenate([x[:, :-hw], x[:, -hw:].T], axis=1)

    both = jnp.concatenate(
        [flip_last(pick(first_core, sum_self, sum_cross)), sum_ff], axis=1
    )
    if dp == 2:
        rows_half = block // 2
        keep = pick(first_core, both[:rows_half], both[rows_half:])
        got = move.core(pick(first_core, both[rows_half:], both[:rows_half]))
        lower, upper = pick(first_core, keep, got), pick(first_core, got, keep)
    else:
        both = jnp.concatenate([pick(first_core, both, 0.0), pick(first_core, 0.0, both)], axis=1)
        both = lax.psum_scatter(both, "dp", scatter_dimension=0, tiled=True)
        lower, upper = jnp.split(both, 2, axis=1)
    out_ff0, out_ff1 = lower[:, 4 * hw :], upper[:, 4 * hw :]

    def ff_part(n):
        sl = slice(n * ff_half, (n + 1) * ff_half)
        return jnp.concatenate([out_ff0[:, sl], out_ff1[:, sl]], axis=1)

    return (
        in_order(out_got),
        loss,
        grad_inputs,
        grad_encoder,
        packed[0],
        *(lower[:, n * hw : (n + 1) * hw] for n in range(4)),
        packed[1],
        *(upper[:, n * hw : (n + 1) * hw] for n in range(4)),
        packed[2],
        ff_part(0),
        ff_part(1),
        ff_part(2),
        packed[3],
        table_sum,
    )


def solution(mesh):
    return jax.shard_map(
        partial(local, dp=mesh.shape["dp"]),
        mesh=mesh,
        in_specs=(
            P("col", ("dp", "row")),
            P("col", ("dp", "row")),
            P(("dp", "col")),
            P(("dp", "row")),
            P("col"),
            P("col", "row"),
            P("col", "row"),
            P("col", "row"),
            P("row", "col"),
            P("col"),
            P("col", "row"),
            P("col", "row"),
            P("col", "row"),
            P("row", "col"),
            P("col"),
            P("col", "row"),
            P("col", "row"),
            P("col", "row"),
            P("col"),
            P("row", "col"),
        ),
        out_specs=(
            P("col", ("dp", "row")),
            P(("dp", "row")),
            P("col", ("dp", "row")),
            P("col", ("dp", "row")),
            P("col"),
            P(("col", "dp"), "row"),
            P(("col", "dp"), "row"),
            P(("col", "dp"), "row"),
            P(("row", "dp"), "col"),
            P("col"),
            P(("col", "dp"), "row"),
            P(("col", "dp"), "row"),
            P(("col", "dp"), "row"),
            P(("row", "dp"), "col"),
            P("col"),
            P(("col", "dp"), "row"),
            P(("col", "dp"), "row"),
            P(("col", "dp"), "row"),
            P("col"),
            P(("dp", "row"), "col"),
        ),
        check_vma=False,
    )
```

```python
from functools import partial

import jax
import jax.numpy as jnp
from jax import lax
from jax.experimental import pallas as pl
from jax.experimental.pallas import tpu as pltpu
from jax.sharding import PartitionSpec as P

HEAD = 64
EPS = 1e-06
NEGATIVE = -1e30
BF = jnp.bfloat16
F32 = jnp.float32
MIB = 1 << 20


def mm(left, right, dims):
    return lax.dot_general(left, right, (dims, ((), ())), preferred_element_type=F32)


def nn(left, right):
    return mm(left, right, ((1,), (0,)))


def tn(left, right):
    return mm(left, right, ((0,), (0,)))


def nt(left, right):
    return mm(left, right, ((1,), (1,)))


def params(mib, axes=1):
    return pltpu.CompilerParams(
        dimension_semantics=("arbitrary",) * axes, vmem_limit_bytes=mib * MIB
    )


def whole(shape):
    return pl.BlockSpec(shape, lambda *_: (0,) * len(shape))


def scores_of(key, query, start, prefix, causal):
    scores = tn(key, query * jnp.asarray(HEAD**-0.5, BF))
    if causal:
        keys = lax.broadcasted_iota(jnp.int32, scores.shape, 0)
        rows = lax.broadcasted_iota(jnp.int32, scores.shape, 1) + start
        scores = jnp.where((keys <= rows) | (keys < prefix), scores, NEGATIVE)
    return scores


def attend_forward(info, query, key, value, causal):
    (q_arr, q_row, q_moves), (k_arr, k_row), (v_arr, v_row) = query, key, value
    tq = info["tq"]
    blocks = q_arr.shape[0]
    heads = info["heads"]
    tk = k_arr.shape[2]

    def body(s_ref, q_ref, k_ref, v_ref, o_ref, l_ref):
        scores = scores_of(k_ref[0], q_ref[0], s_ref[0] * tq, s_ref[1], causal)
        top = jnp.max(scores, axis=0, keepdims=True)
        weights = jnp.exp(scores - top)
        total = jnp.sum(weights, axis=0, keepdims=True)
        mixed = nn(v_ref[0], weights.astype(BF))
        o_ref[0] = (mixed / total).astype(BF)
        l_ref[0] = top + jnp.log(total)

    return pl.pallas_call(
        body,
        out_shape=(
            jax.ShapeDtypeStruct((blocks, heads * HEAD, tq), BF),
            jax.ShapeDtypeStruct((blocks * heads, 1, tq), F32),
        ),
        grid_spec=pltpu.PrefetchScalarGridSpec(
            num_scalar_prefetch=1,
            grid=(blocks, heads),
            in_specs=[
                pl.BlockSpec(
                    (1, HEAD, tq), lambda b, h, s: (b, q_row + h, s[0] if q_moves else 0)
                ),
                pl.BlockSpec((1, HEAD, tk), lambda b, h, s: (b, k_row + h, 0)),
                pl.BlockSpec((1, HEAD, tk), lambda b, h, s: (b, v_row + h, 0)),
            ],
            out_specs=(
                pl.BlockSpec((1, HEAD, tq), lambda b, h, s: (b, h, 0)),
                pl.BlockSpec((1, 1, tq), lambda b, h, s: (b * heads + h, 0, 0)),
            ),
        ),
        compiler_params=params(48, 2),
    )(info["scalars"], q_arr, k_arr, v_arr)


def attend_backward(info, query, key, value, incoming, totals, causal):
    (q_arr, q_row, q_moves), (k_arr, k_row), (v_arr, v_row) = query, key, value
    tq = info["tq"]
    blocks = q_arr.shape[0]
    heads = info["heads"]
    tk = k_arr.shape[2]

    def body(s_ref, q_ref, k_ref, v_ref, g_ref, l_ref, dq_ref, dk_ref, dv_ref):
        q = q_ref[0]
        scores = scores_of(k_ref[0], q, s_ref[0] * tq, s_ref[1], causal)
        weights = jnp.exp(scores - l_ref[0])
        dp = tn(v_ref[0], g_ref[0])
        inner = weights * dp
        centre = jnp.sum(inner, axis=0, keepdims=True)
        ds = (inner - weights * centre).astype(BF)
        dv_ref[0] = nt(g_ref[0], weights.astype(BF)).astype(BF)
        dq_ref[0] = (nn(k_ref[0], ds) * HEAD**-0.5).astype(BF)
        dk_ref[0] = (nt(q, ds) * HEAD**-0.5).astype(BF)

    return pl.pallas_call(
        body,
        out_shape=(
            jax.ShapeDtypeStruct((blocks, heads * HEAD, tq), BF),
            jax.ShapeDtypeStruct((blocks, heads * HEAD, tk), BF),
            jax.ShapeDtypeStruct((blocks, heads * HEAD, tk), BF),
        ),
        grid_spec=pltpu.PrefetchScalarGridSpec(
            num_scalar_prefetch=1,
            grid=(blocks, heads),
            in_specs=[
                pl.BlockSpec(
                    (1, HEAD, tq), lambda b, h, s: (b, q_row + h, s[0] if q_moves else 0)
                ),
                pl.BlockSpec((1, HEAD, tk), lambda b, h, s: (b, k_row + h, 0)),
                pl.BlockSpec((1, HEAD, tk), lambda b, h, s: (b, v_row + h, 0)),
                pl.BlockSpec((1, HEAD, tq), lambda b, h, s: (b, h, 0)),
                pl.BlockSpec((1, 1, tq), lambda b, h, s: (b * heads + h, 0, 0)),
            ],
            out_specs=(
                pl.BlockSpec((1, HEAD, tq), lambda b, h, s: (b, h, 0)),
                pl.BlockSpec((1, HEAD, tk), lambda b, h, s: (b, h, 0)),
                pl.BlockSpec((1, HEAD, tk), lambda b, h, s: (b, h, 0)),
            ),
        ),
        compiler_params=params(48, 2),
    )(info["scalars"], q_arr, k_arr, v_arr, incoming, totals)


GELU_A = 0.7978845608028654
GELU_B = 0.044715


def gelu_parts(gate):
    inner = jnp.tanh(GELU_A * (gate + GELU_B * gate * gate * gate))
    value = 0.5 * gate * (1.0 + inner)
    slope = 0.5 * (1.0 + inner) + 0.5 * gate * (1.0 - inner * inner) * (
        GELU_A * (1.0 + 3.0 * GELU_B * gate * gate)
    )
    return value, slope


def ff_forward(packs, normed):
    d, lanes = packs[0].shape
    wide = lanes // 3
    tokens = normed.shape[1]
    n = len(packs)

    def body(*refs):
        w_refs, x_ref, save_refs, out_ref = refs[:n], refs[n], refs[n + 1 : 2 * n + 1], refs[-1]
        for b, (w_ref, save_ref) in enumerate(zip(w_refs, save_refs)):
            both = tn(w_ref[:, : 2 * wide], x_ref[...])
            save_ref[...] = both.astype(BF)
            value, _ = gelu_parts(both[:wide])
            hidden = (value * both[wide:]).astype(BF)
            part = nn(w_ref[:, 2 * wide :], hidden)
            out_ref[...] = part if b == 0 else out_ref[...] + part

    return pl.pallas_call(
        body,
        out_shape=[jax.ShapeDtypeStruct((2 * wide, tokens), BF)] * n
        + [jax.ShapeDtypeStruct((d, tokens), F32)],
        compiler_params=params(48, 0),
    )(*packs, normed)


def ff_backward(order, packs, saved, normed, grad):
    d, lanes = packs[0].shape
    wide = lanes // 3
    tokens = normed.shape[1]
    n = len(packs)
    size = d // 4

    def body(s_ref, *refs):
        w_refs, save_refs = refs[:n], refs[n : 2 * n]
        x_ref, g_ref, dw_ref, out_ref = refs[2 * n :]
        for b, (w_ref, save_ref) in enumerate(zip(w_refs, save_refs)):
            dh = tn(w_ref[:, 2 * wide :], g_ref[...])
            gate, up = save_ref[:wide].astype(F32), save_ref[wide:].astype(F32)
            value, slope = gelu_parts(gate)
            hidden = (value * up).astype(BF)
            grads = jnp.concatenate(
                [(dh * up * slope).astype(BF), (dh * value).astype(BF)], axis=0
            )
            first = nt(x_ref[...], grads).astype(BF)
            second = nt(g_ref[...], hidden).astype(BF)
            for p in range(4):
                at = pl.ds(pl.multiple_of(s_ref[4 + p] * size, size), size)
                dw_ref[s_ref[b], at, : 2 * wide] = first[p * size : (p + 1) * size]
                dw_ref[s_ref[b], at, 2 * wide :] = second[p * size : (p + 1) * size]
            part = nn(w_ref[:, : 2 * wide], grads)
            out_ref[...] = part if b == 0 else out_ref[...] + part

    return pl.pallas_call(
        body,
        out_shape=(
            jax.ShapeDtypeStruct((n, d, lanes), BF),
            jax.ShapeDtypeStruct((d, tokens), F32),
        ),
        grid_spec=pltpu.PrefetchScalarGridSpec(
            num_scalar_prefetch=1,
            grid=(1,),
            in_specs=[whole((d, lanes))] * n
            + [whole((2 * wide, tokens))] * n
            + [whole((d, tokens))] * 2,
            out_specs=(whole((n, d, lanes)), whole((d, tokens))),
        ),
        compiler_params=params(60),
    )(order, *packs, *saved, normed, grad)


def norm_in(parts, gain, tokens, tile=256):
    d = parts[0].shape[0]
    n = len(parts)

    def body(*refs):
        x_refs, g_ref, sum_ref, norm_ref, scale_ref = refs[:n], refs[n], *refs[n + 1 :]
        states = x_refs[0][...].astype(F32)
        if n > 1:
            rest = x_refs[1][...]
            for ref in x_refs[2:]:
                rest = rest + ref[...]
            states = states + rest
        scale = lax.rsqrt(jnp.mean(states * states, axis=0, keepdims=True) + EPS)
        sum_ref[...] = states
        scale_ref[...] = scale
        norm_ref[...] = (states * scale * g_ref[...]).astype(BF)

    spec = pl.BlockSpec((d, tile), lambda i: (0, i))
    return pl.pallas_call(
        body,
        grid=(tokens // tile,),
        in_specs=[spec] * n + [whole((d, 1))],
        out_specs=(spec, spec, pl.BlockSpec((1, tile), lambda i: (0, i))),
        out_shape=(
            jax.ShapeDtypeStruct((d, tokens), F32),
            jax.ShapeDtypeStruct((d, tokens), BF),
            jax.ShapeDtypeStruct((1, tokens), F32),
        ),
        compiler_params=params(40),
    )(*parts, gain)


def norm_out(scalars, states, gain, scale, incoming, before, place=False, tile=256):
    d, tokens = states.shape
    n = len(incoming)
    has = before is not None
    own_tiles = before.shape[1] // tile if has else 1

    def body(*refs):
        s_ref, x_ref, g_ref, r_ref = refs[:4]
        y_refs = refs[4 : 4 + n]
        b_ref = refs[4 + n] if has else None
        outs = refs[4 + n + has :]
        i = pl.program_id(0)
        states_now = x_ref[...].astype(F32)
        dy = y_refs[0][...].astype(F32)
        for ref in y_refs[1:]:
            dy = dy + ref[...].astype(F32)
        scale_now = r_ref[...]
        weighted = dy * g_ref[...]
        inner = jnp.mean(weighted * states_now, axis=0, keepdims=True)
        total = scale_now * weighted - states_now * (scale_now * scale_now * scale_now * inner)
        if has and place:
            here = (i // own_tiles == s_ref[0]) & (s_ref[2] == 0)
            total = total + b_ref[...] * jnp.where(here, 1.0, 0.0)
        elif has:
            total = total + b_ref[...]
        gain_grad = jnp.sum(dy * states_now * scale_now, axis=1, keepdims=True)
        low_ref, gain_ref = outs[-2:]
        if not place:
            outs[0][...] = total
        low_ref[...] = total.astype(BF)

        @pl.when(i == 0)
        def _():
            gain_ref[...] = gain_grad

        @pl.when(i > 0)
        def _():
            gain_ref[...] += gain_grad

    spec = pl.BlockSpec((d, tile), lambda i, s: (0, i))
    out_shape = [] if place else [jax.ShapeDtypeStruct((d, tokens), F32)]
    out_shape += [jax.ShapeDtypeStruct((d, tokens), BF), jax.ShapeDtypeStruct((d, 1), F32)]
    return pl.pallas_call(
        body,
        out_shape=out_shape,
        grid_spec=pltpu.PrefetchScalarGridSpec(
            num_scalar_prefetch=1,
            grid=(tokens // tile,),
            in_specs=[spec, whole((d, 1)), pl.BlockSpec((1, tile), lambda i, s: (0, i))]
            + [spec] * n
            + ([pl.BlockSpec((d, tile), lambda i, s: (0, i % own_tiles))] if has else []),
            out_specs=[spec] * (len(out_shape) - 1) + [whole((d, 1))],
        ),
        compiler_params=params(40),
    )(scalars, states, gain, scale, *incoming, *([before] if has else []))


def lane_block(lanes, low, high):
    if low // 256 == (high - 1) // 256 and lanes % 256 == 0:
        return 256, low // 256, low % 256
    return lanes, 0, low


def project(pack, normed, low, high):
    blocks, d, lanes = pack.shape
    tokens = normed.shape[1]
    size, index, at = lane_block(lanes, low, high)

    def body(w_ref, x_ref, o_ref):
        o_ref[0] = tn(w_ref[0, :, at : at + high - low], x_ref[...]).astype(BF)

    return pl.pallas_call(
        body,
        grid=(blocks,),
        in_specs=[pl.BlockSpec((1, d, size), lambda b: (b, 0, index)), whole((d, tokens))],
        out_specs=pl.BlockSpec((1, high - low, tokens), lambda b: (b, 0, 0)),
        out_shape=jax.ShapeDtypeStruct((blocks, high - low, tokens), BF),
        compiler_params=params(40),
    )(pack, normed)


def combine(pack, rows, low, high):
    blocks, d, lanes = pack.shape
    tokens = rows.shape[2]
    size, index, at = lane_block(lanes, low, high)

    def body(w_ref, x_ref, o_ref):
        part = nn(w_ref[0, :, at : at + high - low], x_ref[0])
        for b in range(1, blocks):
            part += nn(w_ref[b, :, at : at + high - low], x_ref[b])
        o_ref[...] = part

    return pl.pallas_call(
        body,
        grid=(1,),
        in_specs=[
            pl.BlockSpec((blocks, d, size), lambda b: (0, 0, index)),
            whole((blocks, high - low, tokens)),
        ],
        out_specs=whole((d, tokens)),
        out_shape=jax.ShapeDtypeStruct((d, tokens), F32),
        compiler_params=params(40),
    )(pack, rows)


def weight_grads(scalars, pairs, lanes):
    d = pairs[0][0].shape[0]
    n = len(pairs)
    lefts = [left for left, _ in pairs]
    rights = [right for _, right in pairs]

    def body(*refs):
        outs = refs[2 * n + 1 :]
        at = 0
        for left_ref, right_ref in zip(refs[1 : n + 1], refs[n + 1 : 2 * n + 1]):
            width = right_ref.shape[1]
            for b, out_ref in enumerate(outs):
                out_ref[:, at : at + width] = nt(left_ref[...], right_ref[b]).astype(BF)
            at += width

    def left_spec(left, right):
        tokens = right.shape[2]
        if left.shape[1] == tokens:
            return pl.BlockSpec((d, tokens), lambda b, s: (0, 0))
        return pl.BlockSpec((d, tokens), lambda b, s: (0, s[0]))

    return pl.pallas_call(
        body,
        out_shape=[jax.ShapeDtypeStruct((d, lanes), BF)] * 2,
        grid_spec=pltpu.PrefetchScalarGridSpec(
            num_scalar_prefetch=1,
            grid=(1,),
            in_specs=[left_spec(left, right) for left, right in pairs]
            + [whole(right.shape) for right in rights],
            out_specs=[whole((d, lanes))] * 2,
        ),
        compiler_params=params(48),
    )(scalars, *lefts, *rights)


def split_sum(parts):
    d, lanes = parts[0].shape
    size = d // 4
    n = len(parts)

    def body(*refs):
        for f, out_ref in enumerate(refs[n:]):
            rows = slice(f * size, (f + 1) * size)
            acc = refs[0][rows].astype(F32)
            for ref in refs[1:n]:
                acc += ref[rows].astype(F32)
            out_ref[...] = acc.astype(BF)

    return pl.pallas_call(
        body,
        out_shape=[jax.ShapeDtypeStruct((size, lanes), BF)] * 4,
        compiler_params=params(40, 0),
    )(*parts)


def source_grads(pack, own, own_low, wide, wide_low, place, width, kind):
    blocks, d, lanes = pack.shape
    tq = own.shape[2] if own is not None else 0
    n = len(wide)
    tokens = wide[0].shape[2]
    step = min(1024, tokens)

    def body(*refs):
        s_ref, w_ref = refs[0], refs[1]
        wide_refs = refs[2 : 2 + n]
        o_ref = refs[-1]
        acc = jnp.zeros((d, step), F32)
        for b in range(blocks):
            for at, ref in zip(wide_low, wide_refs):
                acc += nn(w_ref[b, :, at : at + width], ref[b])
        o_ref[...] = acc.astype(kind)
        if own is not None:
            own_ref = refs[2 + n]
            part = jnp.zeros((d, tq), F32)
            for b in range(blocks):
                part += nn(w_ref[b, :, own_low : own_low + width], own_ref[b])
            where = pl.ds(pl.multiple_of(s_ref[0] * tq, tq), tq)
            o_ref[:, where] += part.astype(kind)

    return pl.pallas_call(
        body,
        out_shape=jax.ShapeDtypeStruct((d, tokens), kind),
        grid_spec=pltpu.PrefetchScalarGridSpec(
            num_scalar_prefetch=1,
            grid=(tokens // step,),
            in_specs=[pl.BlockSpec((blocks, d, lanes), lambda i, s: (0, 0, 0))]
            + [pl.BlockSpec((blocks, width, step), lambda i, s: (0, 0, i))] * n
            + (
                [pl.BlockSpec((blocks, width, tq), lambda i, s: (0, 0, 0))]
                if own is not None
                else []
            ),
            out_specs=pl.BlockSpec((d, step), lambda i, s: (0, i)),
        ),
        compiler_params=params(40),
    )(place, pack, *wide, *([own] if own is not None else []))


VB = 512


def assemble(s_ref, own_ref, one_ref, two_ref, three_ref, out_ref):
    size = own_ref.shape[0]
    out_ref[:size] = own_ref[...]
    out_ref[pl.ds(pl.multiple_of((1 + s_ref[1]) * size, size), size), :] = one_ref[...]
    out_ref[pl.ds(pl.multiple_of((2 - s_ref[1]) * size, size), size), :] = two_ref[...]
    out_ref[3 * size :] = three_ref[...]


def table_specs(size):
    return [pl.BlockSpec((size, VB), lambda v, s: (0, v))] * 4


def vocab_forward(scalars, hidden, table, wanted):
    half_chunks, d, step = hidden[0].shape
    chunks = 2 * half_chunks
    own = table[0]
    size, width = own.shape
    parts = width // VB

    def body(s_ref, h0_ref, h1_ref, own_ref, one_ref, two_ref, three_ref, t_ref, e_ref, m_ref, st_ref, blk, flip):
        vb = pl.program_id(0)

        @pl.when(vb == 0)
        def _():
            st_ref[0] = jnp.full((chunks, step), NEGATIVE, F32)
            st_ref[1:] = jnp.zeros((2, chunks, step), F32)

        assemble(s_ref, own_ref, one_ref, two_ref, three_ref, blk)
        flip[...] = blk[...].T
        ids = lax.broadcasted_iota(jnp.int32, (VB, step), 0)

        def one_chunk(n, states, masked):
            logits = nn(flip[...], states)
            row = slice(n, n + 1)
            st_ref[2, row] += jnp.sum(
                jnp.where(ids == t_ref[row] - vb * VB, logits, 0.0), axis=0, keepdims=True
            )
            if masked:
                logits = jnp.where(ids < s_ref[0] - vb * VB, logits, NEGATIVE)
            before = st_ref[0, row]
            top = jnp.maximum(before, jnp.max(logits, axis=0, keepdims=True))
            exps = jnp.exp(logits - top)
            st_ref[1, row] = st_ref[1, row] * jnp.exp(before - top) + jnp.sum(
                exps, axis=0, keepdims=True
            )
            st_ref[0, row] = top
            m_ref[0, row] = top
            e_ref[n] = exps.astype(BF)

        def some(masked):
            for n in range(chunks):
                one_chunk(n, (h0_ref, h1_ref)[n // half_chunks][n % half_chunks], masked)

        inside = (vb + 1) * VB <= s_ref[0]
        pl.when(inside)(partial(some, False))
        pl.when(jnp.logical_not(inside))(partial(some, True))

    return pl.pallas_call(
        body,
        out_shape=(
            jax.ShapeDtypeStruct((chunks, width, step), BF),
            jax.ShapeDtypeStruct((parts, chunks, step), F32),
            jax.ShapeDtypeStruct((3, chunks, step), F32),
        ),
        grid_spec=pltpu.PrefetchScalarGridSpec(
            num_scalar_prefetch=1,
            grid=(parts,),
            in_specs=[whole((half_chunks, d, step))] * 2
            + table_specs(size)
            + [whole((chunks, step))],
            out_specs=(
                pl.BlockSpec((chunks, VB, step), lambda v, s: (0, v, 0)),
                pl.BlockSpec((1, chunks, step), lambda v, s: (v, 0, 0)),
                whole((3, chunks, step)),
            ),
            scratch_shapes=[pltpu.VMEM((d, VB), BF), pltpu.VMEM((VB, d), BF)],
        ),
        compiler_params=params(48),
    )(scalars, *hidden, *table, wanted)


def vocab_hidden_grad(scalars, exps, tops, logsum, first_row, table, wanted):
    chunks, width, step = exps.shape
    own = table[0]
    size = own.shape[0]
    d = 4 * size
    parts = width // VB

    def body(s_ref, e_ref, m_ref, l_ref, own_ref, one_ref, two_ref, three_ref, t_ref, g_ref, o_ref, p_ref, blk, acc):
        vb = pl.program_id(0)

        @pl.when(vb == 0)
        def _():
            acc[...] = jnp.zeros_like(acc)

        assemble(s_ref, own_ref, one_ref, two_ref, three_ref, blk)
        ids = lax.broadcasted_iota(jnp.int32, (VB, step), 0)

        for n in range(chunks):
            row, at = slice(n, n + 1), slice(first_row + n, first_row + n + 1)
            scale = jnp.exp(m_ref[0, row] - l_ref[at])
            probs = e_ref[n].astype(F32) * scale
            grads = jnp.where(ids == t_ref[row] - vb * VB, probs - 1.0, probs).astype(BF)
            g_ref[n] = grads
            acc[n] += nn(blk[...], grads)

        @pl.when(vb == parts - 1)
        def _():
            o_ref[...] = acc[: chunks // 2].astype(BF)
            p_ref[...] = acc[chunks // 2 :].astype(BF)

    return pl.pallas_call(
        body,
        out_shape=(
            jax.ShapeDtypeStruct((chunks, width, step), BF),
            jax.ShapeDtypeStruct((chunks // 2, d, step), BF),
            jax.ShapeDtypeStruct((chunks // 2, d, step), BF),
        ),
        grid_spec=pltpu.PrefetchScalarGridSpec(
            num_scalar_prefetch=1,
            grid=(parts,),
            in_specs=[
                pl.BlockSpec((chunks, VB, step), lambda v, s: (0, v, 0)),
                pl.BlockSpec((1, chunks, step), lambda v, s: (v, 0, 0)),
                whole(logsum.shape),
            ]
            + table_specs(size)
            + [whole((chunks, step))],
            out_specs=(
                pl.BlockSpec((chunks, VB, step), lambda v, s: (0, v, 0)),
                whole((chunks // 2, d, step)),
                whole((chunks // 2, d, step)),
            ),
            scratch_shapes=[pltpu.VMEM((d, VB), BF), pltpu.VMEM((chunks, d, step), F32)],
        ),
        input_output_aliases={1: 0},
        compiler_params=params(56),
    )(scalars, exps, tops, logsum, *table, wanted)


def vocab_table_grad(places, hidden, grads):
    per, d, step = hidden[0].shape
    chunks, width, _ = grads[0].shape
    unit = d // 8
    parts = width // VB
    nh, ng = len(hidden), len(grads)

    def body(*refs):
        s_ref, h_refs, g_refs, o_ref = refs[0], refs[1 : 1 + nh], refs[1 + nh : -1], refs[-1]
        acc = None
        for n in range(nh * per):
            part = nt(h_refs[n // per][n % per], g_refs[n // chunks][n % chunks])
            acc = part if acc is None else acc + part
        for u in range(8):
            spot = pl.ds(pl.multiple_of(s_ref[u] * unit, unit), unit)
            o_ref[spot, :] = acc[u * unit : (u + 1) * unit].astype(BF)

    return pl.pallas_call(
        body,
        out_shape=jax.ShapeDtypeStruct((d, width), BF),
        grid_spec=pltpu.PrefetchScalarGridSpec(
            num_scalar_prefetch=1,
            grid=(parts,),
            in_specs=[whole((per, d, step))] * nh
            + [pl.BlockSpec((chunks, VB, step), lambda v, s: (0, v, 0))] * ng,
            out_specs=pl.BlockSpec((d, VB), lambda v, s: (0, v)),
        ),
        compiler_params=params(48),
    )(places, *hidden, *grads)


def merge_core(mine, other):
    def body(a_ref, b_ref, o_ref):
        for i in range(8):
            row, far = slice(i, i + 1), slice(i ^ 2, (i ^ 2) + 1)
            top = jnp.maximum(a_ref[0, row], b_ref[0, far])
            o_ref[0, row] = top
            o_ref[1, row] = a_ref[1, row] * jnp.exp(a_ref[0, row] - top) + b_ref[
                1, far
            ] * jnp.exp(b_ref[0, far] - top)
            o_ref[2, row] = a_ref[2, row] + b_ref[2, far]

    return pl.pallas_call(
        body,
        out_shape=jax.ShapeDtypeStruct(mine.shape, F32),
        compiler_params=params(16, 0),
    )(mine, other)


def merge_chips(spots, items):
    step = items[0].shape[2]
    flips = (0, 4, 1, 5)

    def body(s_ref, *refs):
        log_ref, loss_ref, rows = refs[-3:]
        for i in range(8):
            at = [slice(i ^ f, (i ^ f) + 1) for f in flips]
            top = refs[0][0, at[0]]
            for ref, row in zip(refs[1:4], at[1:]):
                top = jnp.maximum(top, ref[0, row])
            total = jnp.zeros((1, step), F32)
            picked = jnp.zeros((1, step), F32)
            for ref, row in zip(refs[:4], at):
                total += ref[1, row] * jnp.exp(ref[0, row] - top)
                picked += ref[2, row]
            logsum = top + jnp.log(total)
            log_ref[at[0]] = logsum
            rows[i] = logsum - picked
        for n in range(4):
            loss_ref[n] = rows[s_ref[n]]

    return pl.pallas_call(
        body,
        out_shape=(
            jax.ShapeDtypeStruct((8, step), F32),
            jax.ShapeDtypeStruct((4, 1, step), F32),
        ),
        grid_spec=pltpu.PrefetchScalarGridSpec(
            num_scalar_prefetch=1,
            grid=(1,),
            in_specs=[whole(items[0].shape)] * 4,
            out_specs=(whole((8, step)), whole((4, 1, step))),
            scratch_shapes=[pltpu.VMEM((8, 1, step), F32)],
        ),
        compiler_params=params(16),
    )(spots, *items)


class Moves:
    def __init__(self, dp):
        self.dp = dp

    def core(self, x):
        return lax.ppermute(x, "dp", [(i, i ^ 1) for i in range(self.dp)])

    def col(self, x, bit):
        return lax.ppermute(x, "col", [(i, i ^ bit) for i in range(4)])

    def cols(self, x, bit, core):
        perm = []
        for i in range(core, self.dp, 2):
            for c in range(4):
                perm.append((i * 4 + c, i * 4 + (c ^ bit)))
        return lax.ppermute(x, ("dp", "col"), perm)

    def row(self, x, bit):
        return lax.ppermute(x, "row", [(i, i ^ bit) for i in range(4)])

    def rows(self, x, pairs):
        perm = []
        for i in range(self.dp):
            for r in range(4):
                if i % 2 in pairs:
                    flip, bit = pairs[i % 2]
                    perm.append((i * 4 + r, (i ^ flip) * 4 + (r ^ bit)))
        return lax.ppermute(x, ("dp", "row"), perm)

    def spread(self, x, turn, back=False):
        perm = []
        for i in range(self.dp):
            for c in range(4):
                dest = (i - i % 2 + c // 2) * 4 + 2 * (i % 2) + (c % 2 ^ turn)
                perm.append((dest, i * 4 + c) if back else (i * 4 + c, dest))
        return lax.ppermute(x, ("dp", "col"), perm)


STEP_ONE = {0: (0, 1), 1: (0, 2)}
STEP_TWO = {0: (1, 2), 1: (1, 1)}
STEP_TWO_BACK = {0: (1, 1), 1: (1, 2)}
SAME_TWO = {0: (0, 2), 1: (0, 1)}


def same(bit):
    return {0: (0, bit), 1: (0, bit)}


def tie(*xs):
    return lax.optimization_barrier(xs)


def plus(a, b, kind=BF):
    return (a.astype(F32) + b.astype(F32)).astype(kind)


def local(
    inputs,
    encoder,
    prefix,
    targets,
    gain_self,
    w_query,
    w_key,
    w_value,
    w_attn_out,
    gain_cross,
    w_cross_query,
    w_cross_key,
    w_cross_value,
    w_cross_out,
    gain_ff,
    w_gate,
    w_up,
    w_ff_out,
    gain_final,
    embed_table,
    *,
    dp,
):
    move = Moves(dp)
    core = lax.axis_index("dp") % 2
    row = lax.axis_index("row")
    col = lax.axis_index("col")
    first_core = core == 0
    side = col // 2
    half = col % 2
    block = inputs.shape[0]
    d = 4 * block
    seq = inputs.shape[1]
    tq = seq // 2
    tc = tq // 2
    heads = w_query.shape[1] // HEAD
    hw = heads * HEAD
    ff_half = w_gate.shape[1] // 2
    vocab = embed_table.shape[1]
    width = -(-vocab // (2 * VB)) * VB
    mine = side == core
    pick = jnp.where

    def settle(got):
        other = move.core(got)
        near, far = pick(mine, got, other), pick(mine, other, got)
        return jnp.concatenate([near[0], far[0], near[1], far[1]], axis=0)

    def hand_back(parts):
        hi = [pick(mine, parts[0], parts[1]), pick(mine, parts[2], parts[3])]
        return [move.spread(hi[0], 0, True), move.spread(hi[1], 1, True)]

    def in_order(got):
        return pick(
            half == 0,
            jnp.concatenate([got[0], got[1]], axis=1),
            jnp.concatenate([got[1], got[0]], axis=1),
        )

    def fold_core(partial_sum):
        blocks4 = partial_sum.reshape(4, block, -1)
        near = jnp.stack([blocks4[0], blocks4[2]])
        far = jnp.stack([blocks4[1], blocks4[3]])
        return pick(mine, near, far), move.core(pick(mine, far, near))

    def fold_out(keep, got):
        return [move.spread(plus(keep[n], got[n]), n, True) for n in range(2)]

    def z_sum(parts, cores):
        own, two, one, three = split_sum(parts)
        send = [(two, 2), (one, 1), (three, 3)]
        if cores is None:
            return [own] + [move.col(x, bit) for x, bit in send]
        return [own] + [move.cols(x, bit, cores) for x, bit in send]

    def total(parts):
        return sum(x.astype(F32) for x in parts)

    def swap_bits(n):
        return n // 2 + 2 * (n % 2)

    valid = jnp.where(first_core, width, vocab - width)
    vocab_scalars = jnp.stack([valid, core]).astype(jnp.int32)
    chip = jnp.where(mine, 0, 1)
    spots = []
    for lo in range(2):
        for h in range(2):
            spots.append((half ^ lo) * 4 + (core ^ h) * 2 + chip)
    spots = jnp.stack(spots).astype(jnp.int32)
    own_places = [row, row ^ (1 + core), row ^ (2 - core), row ^ 3]
    own_places += [col ^ swap_bits(p) for p in range(4)]
    own_places = jnp.stack(own_places).astype(jnp.int32)
    places = []
    for unit in range(8):
        e = 2 * (row ^ (unit // 2)) + unit % 2
        places.append(e % 4 * 2 + e // 4)
    places = jnp.stack(places).astype(jnp.int32)

    pack_self = jnp.concatenate([w_query, w_key, w_value, w_attn_out.T], axis=1)
    pack_cross = jnp.concatenate([w_cross_query, w_cross_key, w_cross_value, w_cross_out.T], axis=1)
    sc_own = pick(first_core, pack_self, pack_cross)
    sc_own, embed_table = tie(sc_own, embed_table)
    padded = jnp.pad(embed_table, ((0, 0), (0, 2 * width - vocab)))
    table_own = pick(first_core, padded[:, :width], padded[:, width:])
    pack_ff = [
        jnp.concatenate([w[:, s : s + ff_half] for w in (w_gate, w_up, w_ff_out)], axis=1)
        for s in (0, ff_half)
    ]
    ff_own = pick(first_core, *pack_ff)

    columns = [gain_self, gain_cross, gain_ff, gain_final]
    tops = [lax.reduce_precision(g, 8, 7) for g in columns]
    columns = tops + [g - t for g, t in zip(columns, tops)]
    high = (prefix // 256).astype(F32)
    columns += [jnp.broadcast_to(high, (block,)), jnp.broadcast_to(prefix - high * 256, (block,))]
    extras = jnp.pad(jnp.stack(columns, axis=1).astype(BF), ((0, 0), (0, 128 - len(columns))))
    x_in = jnp.concatenate([inputs, extras], axis=1)

    sc_got = [move.col(sc_own, bit) for bit in (2, 1, 3)]
    table_one = move.rows(table_own, STEP_ONE)
    table_two = move.rows(table_own, SAME_TWO)
    sc, x_in, ff_own, targets, spots, places, own_places = tie(
        jnp.concatenate([sc_own, *sc_got]), x_in, ff_own, targets, spots, places, own_places
    )
    other_targets = move.core(targets)
    near, far = pick(mine, targets, other_targets), pick(mine, other_targets, targets)

    def target_chunks(lo):
        out = []
        for which in (core, 1 - core):
            for seq_targets in (near, far):
                out.append(lax.dynamic_slice_in_dim(seq_targets, lo * tq + which * tc, tc, 0))
        wanted = jnp.stack(out) - col * vocab
        return jnp.where((wanted >= 0) & (wanted < vocab), wanted - core * width, -1)

    want_near, want_far = target_chunks(half), target_chunks(1 - half)
    sc_row = move.rows(sc, STEP_ONE)
    x_got = [move.spread(x_in, 0), move.spread(x_in, 1)]
    x_near, x_far, sc_row, sc, ff_own, table_one, table_two, enc_in = tie(
        *x_got, sc_row, sc, ff_own, table_one, table_two, encoder
    )
    sc_one = move.rows(sc, STEP_TWO)
    sc_two = move.rows(sc_row, STEP_TWO)
    ff_far = move.col(ff_own, 2)
    enc_zero = move.spread(enc_in, 0)
    states_low = settle(jnp.stack([x_near, x_far]))
    small = states_low[:, seq : seq + 16].astype(F32)
    g_self, g_cross, g_ff, g_final = (small[:, n : n + 1] + small[:, n + 4 : n + 5] for n in range(4))
    length = lax.dynamic_slice(small, (swap_bits(col ^ row) * block, 8), (1, 2))
    length = (length[0, :1] * 256 + length[0, 1:]).astype(jnp.int32)
    scalars = jnp.concatenate([half[None], length, core[None]]).astype(jnp.int32)
    info = {"tq": tq, "heads": heads, "scalars": scalars}
    states_all, normed_all, scale_all = norm_in([states_low], g_self, seq)
    states_own = lax.dynamic_slice_in_dim(states_low, half * tq, tq, 1)
    own_blocks = jnp.stack([sc, sc_row])
    normed_all, states_own, own_blocks, scalars, ff_own, want_near, want_far, ff_far, enc_zero, enc_in = tie(
        normed_all, states_own, own_blocks, scalars, ff_own, want_near, want_far, ff_far, enc_zero, enc_in
    )
    ff = jnp.concatenate([ff_own, ff_far])
    ff_got = move.col(ff, 1)
    enc_one = move.spread(enc_in, 1)
    other_blocks = jnp.stack([sc_one, sc_two])
    ws = pick(first_core, own_blocks, other_blocks)
    wc = pick(first_core, other_blocks, own_blocks)

    qkv = project(ws, normed_all, 0, 3 * hw)
    self_args = ((qkv, 0, True), (qkv, heads), (qkv, 2 * heads))
    self_args = ((qkv, 0, True), (qkv, heads), (qkv, 2 * heads))
    attended, totals_self = attend_forward(info, *self_args, True)
    attended, enc_one, ff, ff_got = tie(attended, enc_one, ff, ff_got)
    ff = jnp.concatenate([ff, ff_got])
    ff_row = move.rows(ff, STEP_ONE)
    ff_one = move.rows(ff, SAME_TWO)
    enc_all = settle(jnp.stack([enc_zero, enc_one]))
    branch = combine(ws, attended, 3 * hw, 4 * hw)
    first, normed_cross, scale_cross = norm_in([states_own, branch, move.core(branch)], g_cross, tq)


    cq = project(wc, normed_cross, 0, hw)
    ckv = project(wc, enc_all, hw, 3 * hw)
    cq, ckv, ff_row, ff_one = tie(cq, ckv, ff_row, ff_one)
    ff_two = move.rows(ff_row, SAME_TWO)
    cross_args = ((cq, 0, False), (ckv, 0), (ckv, heads))
    crossed, totals_cross = attend_forward(info, *cross_args, False)
    crossed, ff_two, table_one = tie(crossed, ff_two, table_one)
    table_three = move.rows(table_one, SAME_TWO)
    branch = combine(wc, crossed, 3 * hw, 4 * hw)
    second, normed_ff, scale_ff = norm_in([first, branch, move.core(branch)], g_ff, tq)

    wf = (ff, ff_row, ff_one, ff_two)
    *saved, branch = ff_forward(wf, normed_ff)
    third, normed_final, scale_final = norm_in([second, branch, move.core(branch)], g_final, tq)

    def reorder(x, index):
        parts = x.reshape(4, block, x.shape[-1])
        return jnp.concatenate(
            [lax.dynamic_index_in_dim(parts, i, 0, keepdims=False) for i in index], axis=0
        )

    piece = lax.dynamic_slice_in_dim(normed_final, core * tc, tc, 1)
    piece = reorder(piece, [swap_bits(col ^ row ^ s) for s in range(4)])
    near_pieces, table_three = tie(jnp.stack([piece, move.col(piece, 2)]), table_three)
    table = (table_own, table_one, table_two, table_three)
    far_pieces = move.col(near_pieces, 1)
    hidden_near = (near_pieces, move.core(near_pieces))
    exps_near, tops_near, stats_near = vocab_forward(
        vocab_scalars, hidden_near, table, want_near
    )
    far_pieces, stats_near, out_low = tie(far_pieces, stats_near, third.astype(BF))
    hidden_far = (far_pieces, move.core(far_pieces))
    out_got = hand_back(out_low.reshape(4, block, tq))
    exps_far, tops_far, stats_far = vocab_forward(vocab_scalars, hidden_far, table, want_far)
    stats_far, *out_got = tie(stats_far, *out_got)

    stats = jnp.concatenate([stats_near, stats_far], axis=1)
    stats = merge_core(stats, move.core(stats))
    items = [stats] + [move.col(stats, bit) for bit in (1, 2, 3)]
    logsum, loss = merge_chips(spots, items)
    loss = loss.reshape(seq)

    grads_far, own_far, oth_far = vocab_hidden_grad(
        vocab_scalars, exps_far, tops_far, logsum, 4, table, want_far
    )
    part_far, exps_near = tie(plus(own_far, move.core(oth_far)), exps_near)
    come_far = move.col(part_far, 1)
    grads_near, own_near, oth_near = vocab_hidden_grad(
        vocab_scalars, exps_near, tops_near, logsum, 0, table, want_near
    )
    part = plus(own_near, move.core(oth_near), F32) + come_far.astype(F32)
    part_last, grads_near = tie(part[1].astype(BF), grads_near)
    come_last = move.col(part_last, 2)
    grad_table = vocab_table_grad(
        places, (*hidden_near, *hidden_far), (grads_near, grads_far)
    )
    come_last, grad_table = tie(come_last, grad_table)
    if dp == 2:
        table_sum = lax.psum_scatter(grad_table, "row", scatter_dimension=0, tiled=True)
    part = plus(part[0], come_last)
    part = reorder(part, [col ^ row ^ swap_bits(n) for n in range(4)])
    other = move.core(part)
    grad_normed = jnp.concatenate(
        [pick(first_core, part, other), pick(first_core, other, part)], axis=1
    )

    grad_third, low, gg_final = norm_out(
        scalars, third, g_final, scale_final, [grad_normed], None
    )
    ff_grads, partial_normed = ff_backward(own_places, wf, saved, normed_ff, low)
    ff_sum = lax.psum_scatter(ff_grads.reshape(4 * d, -1), "row", scatter_dimension=0, tiled=True)
    grad_second, low, gg_ff = norm_out(
        scalars, second, g_ff, scale_ff, [partial_normed, move.core(partial_normed)], grad_third
    )
    grad_crossed = project(wc, low, 3 * hw, 4 * hw)
    dcq, dck, dcv = attend_backward(info, *cross_args, grad_crossed, totals_cross, False)
    partial_normed = combine(wc, dcq, 0, hw)
    partial_other = move.core(partial_normed)
    dck, partial_normed = tie(dck, partial_normed)
    grad_enc = source_grads(wc, None, 0, (dck, dcv), (hw, 2 * hw), scalars, hw, BF)
    partial_other, grad_enc = tie(partial_other, grad_enc)
    grad_first, low_self, gg_cross = norm_out(
        scalars, first, g_cross, scale_cross, [partial_normed, partial_other], grad_second
    )
    enc_keep, enc_come = fold_core(grad_enc)
    enc_keep, enc_come, low_self, normed_cross = tie(enc_keep, enc_come, low_self, normed_cross)
    enc_come = fold_out(enc_keep, enc_come)
    cross_zero, cross_one = weight_grads(
        scalars, [(normed_cross, dcq), (enc_all, dck), (enc_all, dcv), (low, crossed)], 4 * hw
    )
    cross_zero, cross_one, low_self = tie(cross_zero, cross_one, low_self)
    cross_come = [
        move.rows(cross_zero, {0: (1, 1)}),
        move.rows(cross_one, {0: (1, 3)}),
        move.rows(cross_one, {1: (0, 2)}),
    ]

    grad_attended = project(ws, low_self, 3 * hw, 4 * hw)
    dq, dk, dv = attend_backward(info, *self_args, grad_attended, totals_self, True)
    if dp == 2:
        dq, table_sum = tie(dq, table_sum)
    dq, dk, cross_come = tie(dq, dk, cross_come)
    self_zero, self_one = weight_grads(
        scalars, [(normed_all, dq), (normed_all, dk), (normed_all, dv), (low_self, attended)], 4 * hw
    )
    self_come = [
        move.rows(self_one, {0: (0, 1)}),
        move.rows(self_zero, {1: (1, 2)}),
        move.rows(self_one, {1: (1, 3)}),
    ]
    dk, self_zero, ff_sum = tie(dk, self_zero, ff_sum)
    sum_ff = lax.psum_scatter(ff_sum, "col", scatter_dimension=0, tiled=True)
    cross_sum = [cross_zero, *cross_come]
    cut = d // 2
    cross_send = total([x[cut:] for x in cross_sum]).astype(BF)
    cross_keep = total([x[:cut] for x in cross_sum]).astype(BF)
    cross_got = move.cols(cross_send, 1, 1)
    dk, cross_keep = tie(dk, cross_keep)
    partial_normed = source_grads(ws, dq, 0, (dk, dv), (hw, 2 * hw), scalars, hw, F32)
    grad_states, gg_self = norm_out(
        scalars, states_all, g_self, scale_all, [partial_normed], grad_first, True
    )
    once = jnp.where(first_core, 1.0, 0.0)
    gain_columns = jnp.concatenate([gg_self, gg_cross * once, gg_ff * once, gg_final * once], axis=1)
    gain_columns = jnp.pad(gain_columns.astype(BF), ((0, 0), (0, 124)))
    grad_states = jnp.concatenate([grad_states, gain_columns], axis=1)
    grad_states, enc_come, self_come, cross_got = tie(grad_states, enc_come, self_come, cross_got)
    in_keep, in_come = fold_core(grad_states)
    in_come = fold_out(in_keep, in_come)
    self_parts = z_sum([self_zero, *self_come], 0)
    cross_sum = plus(cross_keep, cross_got)
    cross_got = move.cols(cross_sum[block:], 2, 1)
    in_come = in_come[0].astype(F32) + in_come[1].astype(F32)
    in_come, self_own = tie(in_come, self_parts[0])
    packed = in_come[:, seq : seq + 4].T
    if dp == 2:
        come = [move.row(packed, bit) for bit in (1, 2, 3)]
        packed, come, self_parts[1:], sum_ff = tie(packed, come, self_parts[1:], sum_ff)
        packed = packed + come[0] + come[1] + come[2]
        packed = packed + move.core(packed)
    else:
        packed = lax.psum(packed, ("dp", "row"))

    grad_encoder = enc_come[0].astype(F32) + enc_come[1].astype(F32)
    grad_inputs = in_come[:, :seq]
    sum_self = total([self_own, *self_parts[1:]])
    sum_cross = cross_sum[:block].astype(F32) + cross_got.astype(F32)
    sum_ff = sum_ff.astype(F32)

    if dp == 2:
        cut = table_sum.reshape(2, d // 8, width)
        keep, got = pick(first_core, cut[0], cut[1]), move.core(pick(first_core, cut[1], cut[0]))
        table_sum = jnp.concatenate(
            [pick(first_core, keep, got), pick(first_core, got, keep)[:, : vocab - width]], axis=1
        ).astype(F32)
    else:
        full = grad_table.reshape(4, 2, d // 8, width).transpose(1, 0, 2, 3).reshape(d, width)
        blank = jnp.zeros_like(full)
        full = pick(
            first_core,
            jnp.concatenate([full, blank], axis=1),
            jnp.concatenate([blank, full], axis=1),
        )[:, :vocab]
        table_sum = lax.psum_scatter(
            full, ("dp", "row"), scatter_dimension=0, tiled=True
        ).astype(F32)

    def flip_last(x):
        return jnp.concatenate([x[:, :-hw], x[:, -hw:].T], axis=1)

    both = jnp.concatenate(
        [flip_last(pick(first_core, sum_self, sum_cross)), sum_ff], axis=1
    )
    if dp == 2:
        rows_half = block // 2
        keep = pick(first_core, both[:rows_half], both[rows_half:])
        got = move.core(pick(first_core, both[rows_half:], both[:rows_half]))
        lower, upper = pick(first_core, keep, got), pick(first_core, got, keep)
    else:
        both = jnp.concatenate([pick(first_core, both, 0.0), pick(first_core, 0.0, both)], axis=1)
        both = lax.psum_scatter(both, "dp", scatter_dimension=0, tiled=True)
        lower, upper = jnp.split(both, 2, axis=1)
    out_ff0, out_ff1 = lower[:, 4 * hw :], upper[:, 4 * hw :]

    def ff_part(n):
        sl = slice(n * ff_half, (n + 1) * ff_half)
        return jnp.concatenate([out_ff0[:, sl], out_ff1[:, sl]], axis=1)

    return (
        in_order(out_got),
        loss,
        grad_inputs,
        grad_encoder,
        packed[0],
        *(lower[:, n * hw : (n + 1) * hw] for n in range(4)),
        packed[1],
        *(upper[:, n * hw : (n + 1) * hw] for n in range(4)),
        packed[2],
        ff_part(0),
        ff_part(1),
        ff_part(2),
        packed[3],
        table_sum,
    )


def solution(mesh):
    return jax.shard_map(
        partial(local, dp=mesh.shape["dp"]),
        mesh=mesh,
        in_specs=(
            P("col", ("dp", "row")),
            P("col", ("dp", "row")),
            P(("dp", "col")),
            P(("dp", "row")),
            P("col"),
            P("col", "row"),
            P("col", "row"),
            P("col", "row"),
            P("row", "col"),
            P("col"),
            P("col", "row"),
            P("col", "row"),
            P("col", "row"),
            P("row", "col"),
            P("col"),
            P("col", "row"),
            P("col", "row"),
            P("col", "row"),
            P("col"),
            P("row", "col"),
        ),
        out_specs=(
            P("col", ("dp", "row")),
            P(("dp", "row")),
            P("col", ("dp", "row")),
            P("col", ("dp", "row")),
            P("col"),
            P(("col", "dp"), "row"),
            P(("col", "dp"), "row"),
            P(("col", "dp"), "row"),
            P(("row", "dp"), "col"),
            P("col"),
            P(("col", "dp"), "row"),
            P(("col", "dp"), "row"),
            P(("col", "dp"), "row"),
            P(("row", "dp"), "col"),
            P("col"),
            P(("col", "dp"), "row"),
            P(("col", "dp"), "row"),
            P(("col", "dp"), "row"),
            P("col"),
            P(("dp", "row"), "col"),
        ),
        check_vma=False,
    )
```

```python
from functools import partial

import jax
import jax.numpy as jnp
from jax import lax
from jax.experimental import pallas as pl
from jax.experimental.pallas import tpu as pltpu
from jax.sharding import PartitionSpec as P

HEAD = 64
EPS = 1e-06
NEGATIVE = -1e30
BF = jnp.bfloat16
F32 = jnp.float32
MIB = 1 << 20


def mm(left, right, dims):
    return lax.dot_general(left, right, (dims, ((), ())), preferred_element_type=F32)


def nn(left, right):
    return mm(left, right, ((1,), (0,)))


def tn(left, right):
    return mm(left, right, ((0,), (0,)))


def nt(left, right):
    return mm(left, right, ((1,), (1,)))


def params(mib, axes=1):
    return pltpu.CompilerParams(
        dimension_semantics=("arbitrary",) * axes, vmem_limit_bytes=mib * MIB
    )


def whole(shape):
    return pl.BlockSpec(shape, lambda *_: (0,) * len(shape))


def scores_of(key, query, start, prefix, causal):
    scores = tn(key, query * jnp.asarray(HEAD**-0.5, BF))
    if causal:
        keys = lax.broadcasted_iota(jnp.int32, scores.shape, 0)
        rows = lax.broadcasted_iota(jnp.int32, scores.shape, 1) + start
        scores = jnp.where((keys <= rows) | (keys < prefix), scores, NEGATIVE)
    return scores


def attend_forward(info, query, key, value, causal):
    (q_arr, q_row, q_moves), (k_arr, k_row), (v_arr, v_row) = query, key, value
    tq = info["tq"]
    blocks = q_arr.shape[0]
    heads = info["heads"]
    tk = k_arr.shape[2]

    def body(s_ref, q_ref, k_ref, v_ref, o_ref, l_ref):
        scores = scores_of(k_ref[0], q_ref[0], s_ref[0] * tq, s_ref[1], causal)
        top = jnp.max(scores, axis=0, keepdims=True)
        weights = jnp.exp(scores - top)
        total = jnp.sum(weights, axis=0, keepdims=True)
        mixed = nn(v_ref[0], weights.astype(BF))
        o_ref[0] = (mixed / total).astype(BF)
        l_ref[0] = top + jnp.log(total)

    return pl.pallas_call(
        body,
        out_shape=(
            jax.ShapeDtypeStruct((blocks, heads * HEAD, tq), BF),
            jax.ShapeDtypeStruct((blocks * heads, 1, tq), F32),
        ),
        grid_spec=pltpu.PrefetchScalarGridSpec(
            num_scalar_prefetch=1,
            grid=(blocks, heads),
            in_specs=[
                pl.BlockSpec(
                    (1, HEAD, tq), lambda b, h, s: (b, q_row + h, s[0] if q_moves else 0)
                ),
                pl.BlockSpec((1, HEAD, tk), lambda b, h, s: (b, k_row + h, 0)),
                pl.BlockSpec((1, HEAD, tk), lambda b, h, s: (b, v_row + h, 0)),
            ],
            out_specs=(
                pl.BlockSpec((1, HEAD, tq), lambda b, h, s: (b, h, 0)),
                pl.BlockSpec((1, 1, tq), lambda b, h, s: (b * heads + h, 0, 0)),
            ),
        ),
        compiler_params=params(48, 2),
    )(info["scalars"], q_arr, k_arr, v_arr)


def attend_backward(info, query, key, value, incoming, totals, causal):
    (q_arr, q_row, q_moves), (k_arr, k_row), (v_arr, v_row) = query, key, value
    tq = info["tq"]
    blocks = q_arr.shape[0]
    heads = info["heads"]
    tk = k_arr.shape[2]

    def body(s_ref, q_ref, k_ref, v_ref, g_ref, l_ref, dq_ref, dk_ref, dv_ref):
        q = q_ref[0]
        scores = scores_of(k_ref[0], q, s_ref[0] * tq, s_ref[1], causal)
        weights = jnp.exp(scores - l_ref[0])
        dp = tn(v_ref[0], g_ref[0])
        inner = weights * dp
        centre = jnp.sum(inner, axis=0, keepdims=True)
        ds = (inner - weights * centre).astype(BF)
        dv_ref[0] = nt(g_ref[0], weights.astype(BF)).astype(BF)
        dq_ref[0] = (nn(k_ref[0], ds) * HEAD**-0.5).astype(BF)
        dk_ref[0] = (nt(q, ds) * HEAD**-0.5).astype(BF)

    return pl.pallas_call(
        body,
        out_shape=(
            jax.ShapeDtypeStruct((blocks, heads * HEAD, tq), BF),
            jax.ShapeDtypeStruct((blocks, heads * HEAD, tk), BF),
            jax.ShapeDtypeStruct((blocks, heads * HEAD, tk), BF),
        ),
        grid_spec=pltpu.PrefetchScalarGridSpec(
            num_scalar_prefetch=1,
            grid=(blocks, heads),
            in_specs=[
                pl.BlockSpec(
                    (1, HEAD, tq), lambda b, h, s: (b, q_row + h, s[0] if q_moves else 0)
                ),
                pl.BlockSpec((1, HEAD, tk), lambda b, h, s: (b, k_row + h, 0)),
                pl.BlockSpec((1, HEAD, tk), lambda b, h, s: (b, v_row + h, 0)),
                pl.BlockSpec((1, HEAD, tq), lambda b, h, s: (b, h, 0)),
                pl.BlockSpec((1, 1, tq), lambda b, h, s: (b * heads + h, 0, 0)),
            ],
            out_specs=(
                pl.BlockSpec((1, HEAD, tq), lambda b, h, s: (b, h, 0)),
                pl.BlockSpec((1, HEAD, tk), lambda b, h, s: (b, h, 0)),
                pl.BlockSpec((1, HEAD, tk), lambda b, h, s: (b, h, 0)),
            ),
        ),
        compiler_params=params(48, 2),
    )(info["scalars"], q_arr, k_arr, v_arr, incoming, totals)


GELU_A = 0.7978845608028654
GELU_B = 0.044715


def gelu_parts(gate):
    inner = jnp.tanh(GELU_A * (gate + GELU_B * gate * gate * gate))
    value = 0.5 * gate * (1.0 + inner)
    slope = 0.5 * (1.0 + inner) + 0.5 * gate * (1.0 - inner * inner) * (
        GELU_A * (1.0 + 3.0 * GELU_B * gate * gate)
    )
    return value, slope


def ff_forward(packs, normed):
    d, lanes = packs[0].shape
    wide = lanes // 3
    tokens = normed.shape[1]
    n = len(packs)

    def body(*refs):
        w_refs, x_ref, save_refs, out_ref = refs[:n], refs[n], refs[n + 1 : 2 * n + 1], refs[-1]
        for b, (w_ref, save_ref) in enumerate(zip(w_refs, save_refs)):
            both = tn(w_ref[:, : 2 * wide], x_ref[...])
            save_ref[...] = both.astype(BF)
            value, _ = gelu_parts(both[:wide])
            hidden = (value * both[wide:]).astype(BF)
            part = nn(w_ref[:, 2 * wide :], hidden)
            out_ref[...] = part if b == 0 else out_ref[...] + part

    return pl.pallas_call(
        body,
        out_shape=[jax.ShapeDtypeStruct((2 * wide, tokens), BF)] * n
        + [jax.ShapeDtypeStruct((d, tokens), F32)],
        compiler_params=params(48, 0),
    )(*packs, normed)


def ff_backward(order, packs, saved, normed, grad):
    d, lanes = packs[0].shape
    wide = lanes // 3
    tokens = normed.shape[1]
    n = len(packs)
    size = d // 4

    def body(s_ref, *refs):
        w_refs, save_refs = refs[:n], refs[n : 2 * n]
        x_ref, g_ref, dw_ref, out_ref = refs[2 * n :]
        for b, (w_ref, save_ref) in enumerate(zip(w_refs, save_refs)):
            dh = tn(w_ref[:, 2 * wide :], g_ref[...])
            gate, up = save_ref[:wide].astype(F32), save_ref[wide:].astype(F32)
            value, slope = gelu_parts(gate)
            hidden = (value * up).astype(BF)
            grads = jnp.concatenate(
                [(dh * up * slope).astype(BF), (dh * value).astype(BF)], axis=0
            )
            first = nt(x_ref[...], grads).astype(BF)
            second = nt(g_ref[...], hidden).astype(BF)
            for p in range(4):
                at = pl.ds(pl.multiple_of(s_ref[4 + p] * size, size), size)
                dw_ref[s_ref[b], at, : 2 * wide] = first[p * size : (p + 1) * size]
                dw_ref[s_ref[b], at, 2 * wide :] = second[p * size : (p + 1) * size]
            part = nn(w_ref[:, : 2 * wide], grads)
            out_ref[...] = part if b == 0 else out_ref[...] + part

    return pl.pallas_call(
        body,
        out_shape=(
            jax.ShapeDtypeStruct((n, d, lanes), BF),
            jax.ShapeDtypeStruct((d, tokens), F32),
        ),
        grid_spec=pltpu.PrefetchScalarGridSpec(
            num_scalar_prefetch=1,
            grid=(1,),
            in_specs=[whole((d, lanes))] * n
            + [whole((2 * wide, tokens))] * n
            + [whole((d, tokens))] * 2,
            out_specs=(whole((n, d, lanes)), whole((d, tokens))),
        ),
        compiler_params=params(60),
    )(order, *packs, *saved, normed, grad)


def norm_in(parts, gain, tokens, tile=256):
    d = parts[0].shape[0]
    n = len(parts)

    def body(*refs):
        x_refs, g_ref, sum_ref, norm_ref, scale_ref = refs[:n], refs[n], *refs[n + 1 :]
        states = x_refs[0][...].astype(F32)
        if n > 1:
            rest = x_refs[1][...]
            for ref in x_refs[2:]:
                rest = rest + ref[...]
            states = states + rest
        scale = lax.rsqrt(jnp.mean(states * states, axis=0, keepdims=True) + EPS)
        sum_ref[...] = states
        scale_ref[...] = scale
        norm_ref[...] = (states * scale * g_ref[...]).astype(BF)

    spec = pl.BlockSpec((d, tile), lambda i: (0, i))
    return pl.pallas_call(
        body,
        grid=(tokens // tile,),
        in_specs=[spec] * n + [whole((d, 1))],
        out_specs=(spec, spec, pl.BlockSpec((1, tile), lambda i: (0, i))),
        out_shape=(
            jax.ShapeDtypeStruct((d, tokens), F32),
            jax.ShapeDtypeStruct((d, tokens), BF),
            jax.ShapeDtypeStruct((1, tokens), F32),
        ),
        compiler_params=params(40),
    )(*parts, gain)


def norm_out(scalars, states, gain, scale, incoming, before, place=False, tile=256):
    d, tokens = states.shape
    n = len(incoming)
    has = before is not None
    own_tiles = before.shape[1] // tile if has else 1

    def body(*refs):
        s_ref, x_ref, g_ref, r_ref = refs[:4]
        y_refs = refs[4 : 4 + n]
        b_ref = refs[4 + n] if has else None
        outs = refs[4 + n + has :]
        i = pl.program_id(0)
        states_now = x_ref[...].astype(F32)
        dy = y_refs[0][...].astype(F32)
        for ref in y_refs[1:]:
            dy = dy + ref[...].astype(F32)
        scale_now = r_ref[...]
        weighted = dy * g_ref[...]
        inner = jnp.mean(weighted * states_now, axis=0, keepdims=True)
        total = scale_now * weighted - states_now * (scale_now * scale_now * scale_now * inner)
        if has and place:
            here = (i // own_tiles == s_ref[0]) & (s_ref[2] == 0)
            total = total + b_ref[...] * jnp.where(here, 1.0, 0.0)
        elif has:
            total = total + b_ref[...]
        gain_grad = jnp.sum(dy * states_now * scale_now, axis=1, keepdims=True)
        low_ref, gain_ref = outs[-2:]
        if not place:
            outs[0][...] = total
        low_ref[...] = total.astype(BF)

        @pl.when(i == 0)
        def _():
            gain_ref[...] = gain_grad

        @pl.when(i > 0)
        def _():
            gain_ref[...] += gain_grad

    spec = pl.BlockSpec((d, tile), lambda i, s: (0, i))
    out_shape = [] if place else [jax.ShapeDtypeStruct((d, tokens), F32)]
    out_shape += [jax.ShapeDtypeStruct((d, tokens), BF), jax.ShapeDtypeStruct((d, 1), F32)]
    return pl.pallas_call(
        body,
        out_shape=out_shape,
        grid_spec=pltpu.PrefetchScalarGridSpec(
            num_scalar_prefetch=1,
            grid=(tokens // tile,),
            in_specs=[spec, whole((d, 1)), pl.BlockSpec((1, tile), lambda i, s: (0, i))]
            + [spec] * n
            + ([pl.BlockSpec((d, tile), lambda i, s: (0, i % own_tiles))] if has else []),
            out_specs=[spec] * (len(out_shape) - 1) + [whole((d, 1))],
        ),
        compiler_params=params(40),
    )(scalars, states, gain, scale, *incoming, *([before] if has else []))


def lane_block(lanes, low, high):
    if low // 256 == (high - 1) // 256 and lanes % 256 == 0:
        return 256, low // 256, low % 256
    return lanes, 0, low


def project(pack, normed, low, high):
    blocks, d, lanes = pack.shape
    tokens = normed.shape[1]
    size, index, at = lane_block(lanes, low, high)

    def body(w_ref, x_ref, o_ref):
        o_ref[0] = tn(w_ref[0, :, at : at + high - low], x_ref[...]).astype(BF)

    return pl.pallas_call(
        body,
        grid=(blocks,),
        in_specs=[pl.BlockSpec((1, d, size), lambda b: (b, 0, index)), whole((d, tokens))],
        out_specs=pl.BlockSpec((1, high - low, tokens), lambda b: (b, 0, 0)),
        out_shape=jax.ShapeDtypeStruct((blocks, high - low, tokens), BF),
        compiler_params=params(40),
    )(pack, normed)


def combine(pack, rows, low, high):
    blocks, d, lanes = pack.shape
    tokens = rows.shape[2]
    size, index, at = lane_block(lanes, low, high)

    def body(w_ref, x_ref, o_ref):
        part = nn(w_ref[0, :, at : at + high - low], x_ref[0])
        for b in range(1, blocks):
            part += nn(w_ref[b, :, at : at + high - low], x_ref[b])
        o_ref[...] = part

    return pl.pallas_call(
        body,
        grid=(1,),
        in_specs=[
            pl.BlockSpec((blocks, d, size), lambda b: (0, 0, index)),
            whole((blocks, high - low, tokens)),
        ],
        out_specs=whole((d, tokens)),
        out_shape=jax.ShapeDtypeStruct((d, tokens), F32),
        compiler_params=params(40),
    )(pack, rows)


def weight_grads(scalars, pairs, lanes):
    d = pairs[0][0].shape[0]
    n = len(pairs)
    lefts = [left for left, _ in pairs]
    rights = [right for _, right in pairs]

    def body(*refs):
        outs = refs[2 * n + 1 :]
        at = 0
        for left_ref, right_ref in zip(refs[1 : n + 1], refs[n + 1 : 2 * n + 1]):
            width = right_ref.shape[1]
            for b, out_ref in enumerate(outs):
                out_ref[:, at : at + width] = nt(left_ref[...], right_ref[b]).astype(BF)
            at += width

    def left_spec(left, right):
        tokens = right.shape[2]
        if left.shape[1] == tokens:
            return pl.BlockSpec((d, tokens), lambda b, s: (0, 0))
        return pl.BlockSpec((d, tokens), lambda b, s: (0, s[0]))

    return pl.pallas_call(
        body,
        out_shape=[jax.ShapeDtypeStruct((d, lanes), BF)] * 2,
        grid_spec=pltpu.PrefetchScalarGridSpec(
            num_scalar_prefetch=1,
            grid=(1,),
            in_specs=[left_spec(left, right) for left, right in pairs]
            + [whole(right.shape) for right in rights],
            out_specs=[whole((d, lanes))] * 2,
        ),
        compiler_params=params(48),
    )(scalars, *lefts, *rights)


def split_sum(parts):
    d, lanes = parts[0].shape
    size = d // 4
    n = len(parts)

    def body(*refs):
        for f, out_ref in enumerate(refs[n:]):
            rows = slice(f * size, (f + 1) * size)
            acc = refs[0][rows].astype(F32)
            for ref in refs[1:n]:
                acc += ref[rows].astype(F32)
            out_ref[...] = acc.astype(BF)

    return pl.pallas_call(
        body,
        out_shape=[jax.ShapeDtypeStruct((size, lanes), BF)] * 4,
        compiler_params=params(40, 0),
    )(*parts)


def source_grads(pack, own, own_low, wide, wide_low, place, width, kind):
    blocks, d, lanes = pack.shape
    tq = own.shape[2] if own is not None else 0
    n = len(wide)
    tokens = wide[0].shape[2]
    step = min(1024, tokens)

    def body(*refs):
        s_ref, w_ref = refs[0], refs[1]
        wide_refs = refs[2 : 2 + n]
        o_ref = refs[-1]
        acc = jnp.zeros((d, step), F32)
        for b in range(blocks):
            for at, ref in zip(wide_low, wide_refs):
                acc += nn(w_ref[b, :, at : at + width], ref[b])
        o_ref[...] = acc.astype(kind)
        if own is not None:
            own_ref = refs[2 + n]
            part = jnp.zeros((d, tq), F32)
            for b in range(blocks):
                part += nn(w_ref[b, :, own_low : own_low + width], own_ref[b])
            where = pl.ds(pl.multiple_of(s_ref[0] * tq, tq), tq)
            o_ref[:, where] += part.astype(kind)

    return pl.pallas_call(
        body,
        out_shape=jax.ShapeDtypeStruct((d, tokens), kind),
        grid_spec=pltpu.PrefetchScalarGridSpec(
            num_scalar_prefetch=1,
            grid=(tokens // step,),
            in_specs=[pl.BlockSpec((blocks, d, lanes), lambda i, s: (0, 0, 0))]
            + [pl.BlockSpec((blocks, width, step), lambda i, s: (0, 0, i))] * n
            + (
                [pl.BlockSpec((blocks, width, tq), lambda i, s: (0, 0, 0))]
                if own is not None
                else []
            ),
            out_specs=pl.BlockSpec((d, step), lambda i, s: (0, i)),
        ),
        compiler_params=params(40),
    )(place, pack, *wide, *([own] if own is not None else []))


VB = 512


def assemble(s_ref, own_ref, one_ref, two_ref, three_ref, out_ref):
    size = own_ref.shape[0]
    out_ref[:size] = own_ref[...]
    out_ref[pl.ds(pl.multiple_of((1 + s_ref[1]) * size, size), size), :] = one_ref[...]
    out_ref[pl.ds(pl.multiple_of((2 - s_ref[1]) * size, size), size), :] = two_ref[...]
    out_ref[3 * size :] = three_ref[...]


def table_specs(size):
    return [pl.BlockSpec((size, VB), lambda v, s: (0, v))] * 4


def vocab_forward(scalars, hidden, table, wanted):
    half_chunks, d, step = hidden[0].shape
    chunks = 2 * half_chunks
    own = table[0]
    size, width = own.shape
    parts = width // VB

    def body(s_ref, h0_ref, h1_ref, own_ref, one_ref, two_ref, three_ref, t_ref, e_ref, m_ref, st_ref, blk, flip):
        vb = pl.program_id(0)

        @pl.when(vb == 0)
        def _():
            st_ref[0] = jnp.full((chunks, step), NEGATIVE, F32)
            st_ref[1:] = jnp.zeros((2, chunks, step), F32)

        assemble(s_ref, own_ref, one_ref, two_ref, three_ref, blk)
        flip[...] = blk[...].T
        ids = lax.broadcasted_iota(jnp.int32, (VB, step), 0)

        def one_chunk(n, states, masked):
            logits = nn(flip[...], states)
            row = slice(n, n + 1)
            st_ref[2, row] += jnp.sum(
                jnp.where(ids == t_ref[row] - vb * VB, logits, 0.0), axis=0, keepdims=True
            )
            if masked:
                logits = jnp.where(ids < s_ref[0] - vb * VB, logits, NEGATIVE)
            before = st_ref[0, row]
            top = jnp.maximum(before, jnp.max(logits, axis=0, keepdims=True))
            exps = jnp.exp(logits - top)
            st_ref[1, row] = st_ref[1, row] * jnp.exp(before - top) + jnp.sum(
                exps, axis=0, keepdims=True
            )
            st_ref[0, row] = top
            m_ref[0, row] = top
            e_ref[n] = exps.astype(BF)

        def some(masked):
            for n in range(chunks):
                one_chunk(n, (h0_ref, h1_ref)[n // half_chunks][n % half_chunks], masked)

        inside = (vb + 1) * VB <= s_ref[0]
        pl.when(inside)(partial(some, False))
        pl.when(jnp.logical_not(inside))(partial(some, True))

    return pl.pallas_call(
        body,
        out_shape=(
            jax.ShapeDtypeStruct((chunks, width, step), BF),
            jax.ShapeDtypeStruct((parts, chunks, step), F32),
            jax.ShapeDtypeStruct((3, chunks, step), F32),
        ),
        grid_spec=pltpu.PrefetchScalarGridSpec(
            num_scalar_prefetch=1,
            grid=(parts,),
            in_specs=[whole((half_chunks, d, step))] * 2
            + table_specs(size)
            + [whole((chunks, step))],
            out_specs=(
                pl.BlockSpec((chunks, VB, step), lambda v, s: (0, v, 0)),
                pl.BlockSpec((1, chunks, step), lambda v, s: (v, 0, 0)),
                whole((3, chunks, step)),
            ),
            scratch_shapes=[pltpu.VMEM((d, VB), BF), pltpu.VMEM((VB, d), BF)],
        ),
        compiler_params=params(48),
    )(scalars, *hidden, *table, wanted)


def vocab_hidden_grad(scalars, exps, tops, logsum, first_row, table, wanted):
    chunks, width, step = exps.shape
    own = table[0]
    size = own.shape[0]
    d = 4 * size
    parts = width // VB

    def body(s_ref, e_ref, m_ref, l_ref, own_ref, one_ref, two_ref, three_ref, t_ref, g_ref, o_ref, p_ref, blk, acc):
        vb = pl.program_id(0)

        @pl.when(vb == 0)
        def _():
            acc[...] = jnp.zeros_like(acc)

        assemble(s_ref, own_ref, one_ref, two_ref, three_ref, blk)
        ids = lax.broadcasted_iota(jnp.int32, (VB, step), 0)

        for n in range(chunks):
            row, at = slice(n, n + 1), slice(first_row + n, first_row + n + 1)
            scale = jnp.exp(m_ref[0, row] - l_ref[at])
            probs = e_ref[n].astype(F32) * scale
            grads = jnp.where(ids == t_ref[row] - vb * VB, probs - 1.0, probs).astype(BF)
            g_ref[n] = grads
            acc[n] += nn(blk[...], grads)

        @pl.when(vb == parts - 1)
        def _():
            o_ref[...] = acc[: chunks // 2].astype(BF)
            p_ref[...] = acc[chunks // 2 :].astype(BF)

    return pl.pallas_call(
        body,
        out_shape=(
            jax.ShapeDtypeStruct((chunks, width, step), BF),
            jax.ShapeDtypeStruct((chunks // 2, d, step), BF),
            jax.ShapeDtypeStruct((chunks // 2, d, step), BF),
        ),
        grid_spec=pltpu.PrefetchScalarGridSpec(
            num_scalar_prefetch=1,
            grid=(parts,),
            in_specs=[
                pl.BlockSpec((chunks, VB, step), lambda v, s: (0, v, 0)),
                pl.BlockSpec((1, chunks, step), lambda v, s: (v, 0, 0)),
                whole(logsum.shape),
            ]
            + table_specs(size)
            + [whole((chunks, step))],
            out_specs=(
                pl.BlockSpec((chunks, VB, step), lambda v, s: (0, v, 0)),
                whole((chunks // 2, d, step)),
                whole((chunks // 2, d, step)),
            ),
            scratch_shapes=[pltpu.VMEM((d, VB), BF), pltpu.VMEM((chunks, d, step), F32)],
        ),
        input_output_aliases={1: 0},
        compiler_params=params(56),
    )(scalars, exps, tops, logsum, *table, wanted)


def vocab_table_grad(places, hidden, grads):
    per, d, step = hidden[0].shape
    chunks, width, _ = grads[0].shape
    unit = d // 8
    parts = width // VB
    nh, ng = len(hidden), len(grads)

    def body(*refs):
        s_ref, h_refs, g_refs, o_ref = refs[0], refs[1 : 1 + nh], refs[1 + nh : -1], refs[-1]
        acc = None
        for n in range(nh * per):
            part = nt(h_refs[n // per][n % per], g_refs[n // chunks][n % chunks])
            acc = part if acc is None else acc + part
        for u in range(8):
            spot = pl.ds(pl.multiple_of(s_ref[u] * unit, unit), unit)
            o_ref[spot, :] = acc[u * unit : (u + 1) * unit].astype(BF)

    return pl.pallas_call(
        body,
        out_shape=jax.ShapeDtypeStruct((d, width), BF),
        grid_spec=pltpu.PrefetchScalarGridSpec(
            num_scalar_prefetch=1,
            grid=(parts,),
            in_specs=[whole((per, d, step))] * nh
            + [pl.BlockSpec((chunks, VB, step), lambda v, s: (0, v, 0))] * ng,
            out_specs=pl.BlockSpec((d, VB), lambda v, s: (0, v)),
        ),
        compiler_params=params(48),
    )(places, *hidden, *grads)


def merge_core(mine, other):
    def body(a_ref, b_ref, o_ref):
        for i in range(8):
            row, far = slice(i, i + 1), slice(i ^ 2, (i ^ 2) + 1)
            top = jnp.maximum(a_ref[0, row], b_ref[0, far])
            o_ref[0, row] = top
            o_ref[1, row] = a_ref[1, row] * jnp.exp(a_ref[0, row] - top) + b_ref[
                1, far
            ] * jnp.exp(b_ref[0, far] - top)
            o_ref[2, row] = a_ref[2, row] + b_ref[2, far]

    return pl.pallas_call(
        body,
        out_shape=jax.ShapeDtypeStruct(mine.shape, F32),
        compiler_params=params(16, 0),
    )(mine, other)


def merge_chips(spots, items):
    step = items[0].shape[2]
    flips = (0, 4, 1, 5)

    def body(s_ref, *refs):
        log_ref, loss_ref, rows = refs[-3:]
        for i in range(8):
            at = [slice(i ^ f, (i ^ f) + 1) for f in flips]
            top = refs[0][0, at[0]]
            for ref, row in zip(refs[1:4], at[1:]):
                top = jnp.maximum(top, ref[0, row])
            total = jnp.zeros((1, step), F32)
            picked = jnp.zeros((1, step), F32)
            for ref, row in zip(refs[:4], at):
                total += ref[1, row] * jnp.exp(ref[0, row] - top)
                picked += ref[2, row]
            logsum = top + jnp.log(total)
            log_ref[at[0]] = logsum
            rows[i] = logsum - picked
        for n in range(4):
            loss_ref[n] = rows[s_ref[n]]

    return pl.pallas_call(
        body,
        out_shape=(
            jax.ShapeDtypeStruct((8, step), F32),
            jax.ShapeDtypeStruct((4, 1, step), F32),
        ),
        grid_spec=pltpu.PrefetchScalarGridSpec(
            num_scalar_prefetch=1,
            grid=(1,),
            in_specs=[whole(items[0].shape)] * 4,
            out_specs=(whole((8, step)), whole((4, 1, step))),
            scratch_shapes=[pltpu.VMEM((8, 1, step), F32)],
        ),
        compiler_params=params(16),
    )(spots, *items)


class Moves:
    def __init__(self, dp):
        self.dp = dp

    def core(self, x):
        return lax.ppermute(x, "dp", [(i, i ^ 1) for i in range(self.dp)])

    def col(self, x, bit):
        return lax.ppermute(x, "col", [(i, i ^ bit) for i in range(4)])

    def cols(self, x, bit, core):
        perm = []
        for i in range(core, self.dp, 2):
            for c in range(4):
                perm.append((i * 4 + c, i * 4 + (c ^ bit)))
        return lax.ppermute(x, ("dp", "col"), perm)

    def row(self, x, bit):
        return lax.ppermute(x, "row", [(i, i ^ bit) for i in range(4)])

    def rows(self, x, pairs):
        perm = []
        for i in range(self.dp):
            for r in range(4):
                if i % 2 in pairs:
                    flip, bit = pairs[i % 2]
                    perm.append((i * 4 + r, (i ^ flip) * 4 + (r ^ bit)))
        return lax.ppermute(x, ("dp", "row"), perm)

    def spread(self, x, turn, back=False):
        perm = []
        for i in range(self.dp):
            for c in range(4):
                dest = (i - i % 2 + c // 2) * 4 + 2 * (i % 2) + (c % 2 ^ turn)
                perm.append((dest, i * 4 + c) if back else (i * 4 + c, dest))
        return lax.ppermute(x, ("dp", "col"), perm)


STEP_ONE = {0: (0, 1), 1: (0, 2)}
STEP_TWO = {0: (1, 2), 1: (1, 1)}
STEP_TWO_BACK = {0: (1, 1), 1: (1, 2)}
SAME_TWO = {0: (0, 2), 1: (0, 1)}


def same(bit):
    return {0: (0, bit), 1: (0, bit)}


def tie(*xs):
    return lax.optimization_barrier(xs)


def plus(a, b, kind=BF):
    return (a.astype(F32) + b.astype(F32)).astype(kind)


def local(
    inputs,
    encoder,
    prefix,
    targets,
    gain_self,
    w_query,
    w_key,
    w_value,
    w_attn_out,
    gain_cross,
    w_cross_query,
    w_cross_key,
    w_cross_value,
    w_cross_out,
    gain_ff,
    w_gate,
    w_up,
    w_ff_out,
    gain_final,
    embed_table,
    *,
    dp,
):
    move = Moves(dp)
    core = lax.axis_index("dp") % 2
    row = lax.axis_index("row")
    col = lax.axis_index("col")
    first_core = core == 0
    side = col // 2
    half = col % 2
    block = inputs.shape[0]
    d = 4 * block
    seq = inputs.shape[1]
    tq = seq // 2
    tc = tq // 2
    heads = w_query.shape[1] // HEAD
    hw = heads * HEAD
    ff_half = w_gate.shape[1] // 2
    vocab = embed_table.shape[1]
    width = -(-vocab // (2 * VB)) * VB
    mine = side == core
    pick = jnp.where

    def settle(got):
        other = move.core(got)
        near, far = pick(mine, got, other), pick(mine, other, got)
        return jnp.concatenate([near[0], far[0], near[1], far[1]], axis=0)

    def hand_back(parts):
        hi = [pick(mine, parts[0], parts[1]), pick(mine, parts[2], parts[3])]
        return [move.spread(hi[0], 0, True), move.spread(hi[1], 1, True)]

    def in_order(got):
        return pick(
            half == 0,
            jnp.concatenate([got[0], got[1]], axis=1),
            jnp.concatenate([got[1], got[0]], axis=1),
        )

    def fold_core(partial_sum):
        blocks4 = partial_sum.reshape(4, block, -1)
        near = jnp.stack([blocks4[0], blocks4[2]])
        far = jnp.stack([blocks4[1], blocks4[3]])
        return pick(mine, near, far), move.core(pick(mine, far, near))

    def fold_out(keep, got):
        return [move.spread(plus(keep[n], got[n]), n, True) for n in range(2)]

    def z_sum(parts, cores):
        own, two, one, three = split_sum(parts)
        send = [(two, 2), (one, 1), (three, 3)]
        if cores is None:
            return [own] + [move.col(x, bit) for x, bit in send]
        return [own] + [move.cols(x, bit, cores) for x, bit in send]

    def total(parts):
        return sum(x.astype(F32) for x in parts)

    def swap_bits(n):
        return n // 2 + 2 * (n % 2)

    valid = jnp.where(first_core, width, vocab - width)
    vocab_scalars = jnp.stack([valid, core]).astype(jnp.int32)
    chip = jnp.where(mine, 0, 1)
    spots = []
    for lo in range(2):
        for h in range(2):
            spots.append((half ^ lo) * 4 + (core ^ h) * 2 + chip)
    spots = jnp.stack(spots).astype(jnp.int32)
    own_places = [row, row ^ (1 + core), row ^ (2 - core), row ^ 3]
    own_places += [col ^ swap_bits(p) for p in range(4)]
    own_places = jnp.stack(own_places).astype(jnp.int32)
    places = []
    for unit in range(8):
        e = 2 * (row ^ (unit // 2)) + unit % 2
        places.append(e % 4 * 2 + e // 4)
    places = jnp.stack(places).astype(jnp.int32)

    pack_self = jnp.concatenate([w_query, w_key, w_value, w_attn_out.T], axis=1)
    pack_cross = jnp.concatenate([w_cross_query, w_cross_key, w_cross_value, w_cross_out.T], axis=1)
    sc_own = pick(first_core, pack_self, pack_cross)
    sc_own, embed_table = tie(sc_own, embed_table)
    padded = jnp.pad(embed_table, ((0, 0), (0, 2 * width - vocab)))
    table_own = pick(first_core, padded[:, :width], padded[:, width:])
    pack_ff = [
        jnp.concatenate([w[:, s : s + ff_half] for w in (w_gate, w_up, w_ff_out)], axis=1)
        for s in (0, ff_half)
    ]
    ff_own = pick(first_core, *pack_ff)

    columns = [gain_self, gain_cross, gain_ff, gain_final]
    tops = [lax.reduce_precision(g, 8, 7) for g in columns]
    columns = tops + [g - t for g, t in zip(columns, tops)]
    high = (prefix // 256).astype(F32)
    columns += [jnp.broadcast_to(high, (block,)), jnp.broadcast_to(prefix - high * 256, (block,))]
    extras = jnp.pad(jnp.stack(columns, axis=1).astype(BF), ((0, 0), (0, 128 - len(columns))))
    x_in = jnp.concatenate([inputs, extras], axis=1)

    sc_got = [move.col(sc_own, bit) for bit in (2, 1, 3)]
    table_one = move.rows(table_own, STEP_ONE)
    table_two = move.rows(table_own, SAME_TWO)
    sc, x_in, ff_own, targets, spots, places, own_places = tie(
        jnp.concatenate([sc_own, *sc_got]), x_in, ff_own, targets, spots, places, own_places
    )
    other_targets = move.core(targets)
    near, far = pick(mine, targets, other_targets), pick(mine, other_targets, targets)

    def target_chunks(lo):
        out = []
        for which in (core, 1 - core):
            for seq_targets in (near, far):
                out.append(lax.dynamic_slice_in_dim(seq_targets, lo * tq + which * tc, tc, 0))
        wanted = jnp.stack(out) - col * vocab
        return jnp.where((wanted >= 0) & (wanted < vocab), wanted - core * width, -1)

    want_near, want_far = target_chunks(half), target_chunks(1 - half)
    sc_row = move.rows(sc, STEP_ONE)
    x_got = [move.spread(x_in, 0), move.spread(x_in, 1)]
    x_near, x_far, ff_own = tie(*x_got, ff_own)
    ff_far = move.col(ff_own, 2)
    x_near, x_far, sc_row, sc, ff_own, ff_far, table_one, table_two, enc_in = tie(
        x_near, x_far, sc_row, sc, ff_own, ff_far, table_one, table_two, encoder
    )
    sc_one = move.rows(sc, STEP_TWO)
    sc_two = move.rows(sc_row, STEP_TWO)
    ff = jnp.concatenate([ff_own, ff_far])
    ff_got = move.col(ff, 1)
    enc_zero = move.spread(enc_in, 0)
    states_low = settle(jnp.stack([x_near, x_far]))
    small = states_low[:, seq : seq + 16].astype(F32)
    g_self, g_cross, g_ff, g_final = (small[:, n : n + 1] + small[:, n + 4 : n + 5] for n in range(4))
    length = lax.dynamic_slice(small, (swap_bits(col ^ row) * block, 8), (1, 2))
    length = (length[0, :1] * 256 + length[0, 1:]).astype(jnp.int32)
    scalars = jnp.concatenate([half[None], length, core[None]]).astype(jnp.int32)
    info = {"tq": tq, "heads": heads, "scalars": scalars}
    states_all, normed_all, scale_all = norm_in([states_low], g_self, seq)
    states_own = lax.dynamic_slice_in_dim(states_low, half * tq, tq, 1)
    own_blocks = jnp.stack([sc, sc_row])
    normed_all, states_own, own_blocks, scalars, want_near, want_far, ff, ff_got, enc_zero, enc_in = tie(
        normed_all, states_own, own_blocks, scalars, want_near, want_far, ff, ff_got, enc_zero, enc_in
    )
    ff = jnp.concatenate([ff, ff_got])
    ff_row = move.rows(ff, STEP_ONE)
    enc_one = move.spread(enc_in, 1)
    other_blocks = jnp.stack([sc_one, sc_two])
    ws = pick(first_core, own_blocks, other_blocks)
    wc = pick(first_core, other_blocks, own_blocks)

    qkv = project(ws, normed_all, 0, 3 * hw)
    self_args = ((qkv, 0, True), (qkv, heads), (qkv, 2 * heads))
    self_args = ((qkv, 0, True), (qkv, heads), (qkv, 2 * heads))
    attended, totals_self = attend_forward(info, *self_args, True)
    attended, enc_one, ff, ff_row = tie(attended, enc_one, ff, ff_row)
    ff_one = move.rows(ff, SAME_TWO)
    enc_all = settle(jnp.stack([enc_zero, enc_one]))
    branch = combine(ws, attended, 3 * hw, 4 * hw)
    first, normed_cross, scale_cross = norm_in([states_own, branch, move.core(branch)], g_cross, tq)


    cq = project(wc, normed_cross, 0, hw)
    ckv = project(wc, enc_all, hw, 3 * hw)
    cq, ckv, ff_row, ff_one = tie(cq, ckv, ff_row, ff_one)
    ff_two = move.rows(ff_row, SAME_TWO)
    cross_args = ((cq, 0, False), (ckv, 0), (ckv, heads))
    crossed, totals_cross = attend_forward(info, *cross_args, False)
    crossed, ff_two, table_one = tie(crossed, ff_two, table_one)
    table_three = move.rows(table_one, SAME_TWO)
    branch = combine(wc, crossed, 3 * hw, 4 * hw)
    second, normed_ff, scale_ff = norm_in([first, branch, move.core(branch)], g_ff, tq)

    wf = (ff, ff_row, ff_one, ff_two)
    *saved, branch = ff_forward(wf, normed_ff)
    third, normed_final, scale_final = norm_in([second, branch, move.core(branch)], g_final, tq)

    def reorder(x, index):
        parts = x.reshape(4, block, x.shape[-1])
        return jnp.concatenate(
            [lax.dynamic_index_in_dim(parts, i, 0, keepdims=False) for i in index], axis=0
        )

    piece = lax.dynamic_slice_in_dim(normed_final, core * tc, tc, 1)
    piece = reorder(piece, [swap_bits(col ^ row ^ s) for s in range(4)])
    near_pieces, table_three = tie(jnp.stack([piece, move.col(piece, 2)]), table_three)
    table = (table_own, table_one, table_two, table_three)
    far_pieces = move.col(near_pieces, 1)
    hidden_near = (near_pieces, move.core(near_pieces))
    exps_near, tops_near, stats_near = vocab_forward(
        vocab_scalars, hidden_near, table, want_near
    )
    far_pieces, stats_near, out_low = tie(far_pieces, stats_near, third.astype(BF))
    hidden_far = (far_pieces, move.core(far_pieces))
    out_got = hand_back(out_low.reshape(4, block, tq))
    exps_far, tops_far, stats_far = vocab_forward(vocab_scalars, hidden_far, table, want_far)
    stats_far, *out_got = tie(stats_far, *out_got)

    stats = jnp.concatenate([stats_near, stats_far], axis=1)
    stats = merge_core(stats, move.core(stats))
    items = [stats] + [move.col(stats, bit) for bit in (1, 2, 3)]
    logsum, loss = merge_chips(spots, items)
    loss = loss.reshape(seq)

    grads_far, own_far, oth_far = vocab_hidden_grad(
        vocab_scalars, exps_far, tops_far, logsum, 4, table, want_far
    )
    part_far, exps_near = tie(plus(own_far, move.core(oth_far)), exps_near)
    come_far = move.col(part_far, 1)
    grads_near, own_near, oth_near = vocab_hidden_grad(
        vocab_scalars, exps_near, tops_near, logsum, 0, table, want_near
    )
    part = plus(own_near, move.core(oth_near), F32) + come_far.astype(F32)
    part_last, grads_near = tie(part[1].astype(BF), grads_near)
    come_last = move.col(part_last, 2)
    grad_table = vocab_table_grad(
        places, (*hidden_near, *hidden_far), (grads_near, grads_far)
    )
    come_last, grad_table = tie(come_last, grad_table)
    if dp == 2:
        table_sum = lax.psum_scatter(grad_table, "row", scatter_dimension=0, tiled=True)
    part = plus(part[0], come_last)
    part = reorder(part, [col ^ row ^ swap_bits(n) for n in range(4)])
    other = move.core(part)
    grad_normed = jnp.concatenate(
        [pick(first_core, part, other), pick(first_core, other, part)], axis=1
    )

    grad_third, low, gg_final = norm_out(
        scalars, third, g_final, scale_final, [grad_normed], None
    )
    ff_grads, partial_normed = ff_backward(own_places, wf, saved, normed_ff, low)
    ff_sum = lax.psum_scatter(ff_grads.reshape(4 * d, -1), "row", scatter_dimension=0, tiled=True)
    grad_second, low, gg_ff = norm_out(
        scalars, second, g_ff, scale_ff, [partial_normed, move.core(partial_normed)], grad_third
    )
    grad_crossed = project(wc, low, 3 * hw, 4 * hw)
    dcq, dck, dcv = attend_backward(info, *cross_args, grad_crossed, totals_cross, False)
    partial_normed = combine(wc, dcq, 0, hw)
    partial_other = move.core(partial_normed)
    dck, partial_normed = tie(dck, partial_normed)
    grad_enc = source_grads(wc, None, 0, (dck, dcv), (hw, 2 * hw), scalars, hw, BF)
    partial_other, grad_enc = tie(partial_other, grad_enc)
    grad_first, low_self, gg_cross = norm_out(
        scalars, first, g_cross, scale_cross, [partial_normed, partial_other], grad_second
    )
    enc_keep, enc_come = fold_core(grad_enc)
    enc_keep, enc_come, low_self, normed_cross = tie(enc_keep, enc_come, low_self, normed_cross)
    enc_come = fold_out(enc_keep, enc_come)
    cross_zero, cross_one = weight_grads(
        scalars, [(normed_cross, dcq), (enc_all, dck), (enc_all, dcv), (low, crossed)], 4 * hw
    )
    cross_zero, cross_one, low_self = tie(cross_zero, cross_one, low_self)
    cross_come = [
        move.rows(cross_zero, {0: (1, 1)}),
        move.rows(cross_one, {0: (1, 3)}),
        move.rows(cross_one, {1: (0, 2)}),
    ]

    grad_attended = project(ws, low_self, 3 * hw, 4 * hw)
    dq, dk, dv = attend_backward(info, *self_args, grad_attended, totals_self, True)
    if dp == 2:
        dq, table_sum = tie(dq, table_sum)
    dq, dk, cross_come = tie(dq, dk, cross_come)
    self_zero, self_one = weight_grads(
        scalars, [(normed_all, dq), (normed_all, dk), (normed_all, dv), (low_self, attended)], 4 * hw
    )
    self_come = [
        move.rows(self_one, {0: (0, 1)}),
        move.rows(self_zero, {1: (1, 2)}),
        move.rows(self_one, {1: (1, 3)}),
    ]
    dk, self_zero, ff_sum = tie(dk, self_zero, ff_sum)
    sum_ff = lax.psum_scatter(ff_sum, "col", scatter_dimension=0, tiled=True)
    cross_sum = [cross_zero, *cross_come]
    cut = d // 2
    cross_send = total([x[cut:] for x in cross_sum]).astype(BF)
    cross_keep = total([x[:cut] for x in cross_sum]).astype(BF)
    cross_got = move.cols(cross_send, 1, 1)
    dk, cross_keep = tie(dk, cross_keep)
    partial_normed = source_grads(ws, dq, 0, (dk, dv), (hw, 2 * hw), scalars, hw, F32)
    grad_states, gg_self = norm_out(
        scalars, states_all, g_self, scale_all, [partial_normed], grad_first, True
    )
    once = jnp.where(first_core, 1.0, 0.0)
    gain_columns = jnp.concatenate([gg_self, gg_cross * once, gg_ff * once, gg_final * once], axis=1)
    gain_columns = jnp.pad(gain_columns.astype(BF), ((0, 0), (0, 124)))
    grad_states = jnp.concatenate([grad_states, gain_columns], axis=1)
    grad_states, enc_come, self_come, cross_got = tie(grad_states, enc_come, self_come, cross_got)
    in_keep, in_come = fold_core(grad_states)
    in_come = fold_out(in_keep, in_come)
    self_parts = z_sum([self_zero, *self_come], 0)
    cross_sum = plus(cross_keep, cross_got)
    cross_got = move.cols(cross_sum[block:], 2, 1)
    in_come = in_come[0].astype(F32) + in_come[1].astype(F32)
    in_come, self_own = tie(in_come, self_parts[0])
    packed = in_come[:, seq : seq + 4].T
    if dp == 2:
        come = [move.row(packed, bit) for bit in (1, 2, 3)]
        packed, come, self_parts[1:], sum_ff = tie(packed, come, self_parts[1:], sum_ff)
        packed = packed + come[0] + come[1] + come[2]
        packed = packed + move.core(packed)
    else:
        packed = lax.psum(packed, ("dp", "row"))

    grad_encoder = enc_come[0].astype(F32) + enc_come[1].astype(F32)
    grad_inputs = in_come[:, :seq]
    sum_self = total([self_own, *self_parts[1:]])
    sum_cross = cross_sum[:block].astype(F32) + cross_got.astype(F32)
    sum_ff = sum_ff.astype(F32)

    if dp == 2:
        cut = table_sum.reshape(2, d // 8, width)
        keep, got = pick(first_core, cut[0], cut[1]), move.core(pick(first_core, cut[1], cut[0]))
        table_sum = jnp.concatenate(
            [pick(first_core, keep, got), pick(first_core, got, keep)[:, : vocab - width]], axis=1
        ).astype(F32)
    else:
        full = grad_table.reshape(4, 2, d // 8, width).transpose(1, 0, 2, 3).reshape(d, width)
        blank = jnp.zeros_like(full)
        full = pick(
            first_core,
            jnp.concatenate([full, blank], axis=1),
            jnp.concatenate([blank, full], axis=1),
        )[:, :vocab]
        table_sum = lax.psum_scatter(
            full, ("dp", "row"), scatter_dimension=0, tiled=True
        ).astype(F32)

    def flip_last(x):
        return jnp.concatenate([x[:, :-hw], x[:, -hw:].T], axis=1)

    both = jnp.concatenate(
        [flip_last(pick(first_core, sum_self, sum_cross)), sum_ff], axis=1
    )
    if dp == 2:
        rows_half = block // 2
        keep = pick(first_core, both[:rows_half], both[rows_half:])
        got = move.core(pick(first_core, both[rows_half:], both[:rows_half]))
        lower, upper = pick(first_core, keep, got), pick(first_core, got, keep)
    else:
        both = jnp.concatenate([pick(first_core, both, 0.0), pick(first_core, 0.0, both)], axis=1)
        both = lax.psum_scatter(both, "dp", scatter_dimension=0, tiled=True)
        lower, upper = jnp.split(both, 2, axis=1)
    out_ff0, out_ff1 = lower[:, 4 * hw :], upper[:, 4 * hw :]

    def ff_part(n):
        sl = slice(n * ff_half, (n + 1) * ff_half)
        return jnp.concatenate([out_ff0[:, sl], out_ff1[:, sl]], axis=1)

    return (
        in_order(out_got),
        loss,
        grad_inputs,
        grad_encoder,
        packed[0],
        *(lower[:, n * hw : (n + 1) * hw] for n in range(4)),
        packed[1],
        *(upper[:, n * hw : (n + 1) * hw] for n in range(4)),
        packed[2],
        ff_part(0),
        ff_part(1),
        ff_part(2),
        packed[3],
        table_sum,
    )


def solution(mesh):
    return jax.shard_map(
        partial(local, dp=mesh.shape["dp"]),
        mesh=mesh,
        in_specs=(
            P("col", ("dp", "row")),
            P("col", ("dp", "row")),
            P(("dp", "col")),
            P(("dp", "row")),
            P("col"),
            P("col", "row"),
            P("col", "row"),
            P("col", "row"),
            P("row", "col"),
            P("col"),
            P("col", "row"),
            P("col", "row"),
            P("col", "row"),
            P("row", "col"),
            P("col"),
            P("col", "row"),
            P("col", "row"),
            P("col", "row"),
            P("col"),
            P("row", "col"),
        ),
        out_specs=(
            P("col", ("dp", "row")),
            P(("dp", "row")),
            P("col", ("dp", "row")),
            P("col", ("dp", "row")),
            P("col"),
            P(("col", "dp"), "row"),
            P(("col", "dp"), "row"),
            P(("col", "dp"), "row"),
            P(("row", "dp"), "col"),
            P("col"),
            P(("col", "dp"), "row"),
            P(("col", "dp"), "row"),
            P(("col", "dp"), "row"),
            P(("row", "dp"), "col"),
            P("col"),
            P(("col", "dp"), "row"),
            P(("col", "dp"), "row"),
            P(("col", "dp"), "row"),
            P("col"),
            P(("dp", "row"), "col"),
        ),
        check_vma=False,
    )
```

```python
from functools import partial

import jax
import jax.numpy as jnp
from jax import lax
from jax.experimental import pallas as pl
from jax.experimental.pallas import tpu as pltpu
from jax.sharding import PartitionSpec as P

HEAD = 64
EPS = 1e-06
NEGATIVE = -1e30
BF = jnp.bfloat16
F32 = jnp.float32
MIB = 1 << 20


def mm(left, right, dims):
    return lax.dot_general(left, right, (dims, ((), ())), preferred_element_type=F32)


def nn(left, right):
    return mm(left, right, ((1,), (0,)))


def tn(left, right):
    return mm(left, right, ((0,), (0,)))


def nt(left, right):
    return mm(left, right, ((1,), (1,)))


def params(mib, axes=1):
    return pltpu.CompilerParams(
        dimension_semantics=("arbitrary",) * axes, vmem_limit_bytes=mib * MIB
    )


def whole(shape):
    return pl.BlockSpec(shape, lambda *_: (0,) * len(shape))


def scores_of(key, query, start, prefix, causal):
    scores = tn(key, query * jnp.asarray(HEAD**-0.5, BF))
    if causal:
        keys = lax.broadcasted_iota(jnp.int32, scores.shape, 0)
        rows = lax.broadcasted_iota(jnp.int32, scores.shape, 1) + start
        scores = jnp.where((keys <= rows) | (keys < prefix), scores, NEGATIVE)
    return scores


def attend_forward(info, query, key, value, causal):
    (q_arr, q_row, q_moves), (k_arr, k_row), (v_arr, v_row) = query, key, value
    tq = info["tq"]
    blocks = q_arr.shape[0]
    heads = info["heads"]
    tk = k_arr.shape[2]

    def body(s_ref, q_ref, k_ref, v_ref, o_ref, l_ref):
        scores = scores_of(k_ref[0], q_ref[0], s_ref[0] * tq, s_ref[1], causal)
        top = jnp.max(scores, axis=0, keepdims=True)
        weights = jnp.exp(scores - top)
        total = jnp.sum(weights, axis=0, keepdims=True)
        mixed = nn(v_ref[0], weights.astype(BF))
        o_ref[0] = (mixed / total).astype(BF)
        l_ref[0] = top + jnp.log(total)

    return pl.pallas_call(
        body,
        out_shape=(
            jax.ShapeDtypeStruct((blocks, heads * HEAD, tq), BF),
            jax.ShapeDtypeStruct((blocks * heads, 1, tq), F32),
        ),
        grid_spec=pltpu.PrefetchScalarGridSpec(
            num_scalar_prefetch=1,
            grid=(blocks, heads),
            in_specs=[
                pl.BlockSpec(
                    (1, HEAD, tq), lambda b, h, s: (b, q_row + h, s[0] if q_moves else 0)
                ),
                pl.BlockSpec((1, HEAD, tk), lambda b, h, s: (b, k_row + h, 0)),
                pl.BlockSpec((1, HEAD, tk), lambda b, h, s: (b, v_row + h, 0)),
            ],
            out_specs=(
                pl.BlockSpec((1, HEAD, tq), lambda b, h, s: (b, h, 0)),
                pl.BlockSpec((1, 1, tq), lambda b, h, s: (b * heads + h, 0, 0)),
            ),
        ),
        compiler_params=params(48, 2),
    )(info["scalars"], q_arr, k_arr, v_arr)


def attend_backward(info, query, key, value, incoming, totals, causal):
    (q_arr, q_row, q_moves), (k_arr, k_row), (v_arr, v_row) = query, key, value
    tq = info["tq"]
    blocks = q_arr.shape[0]
    heads = info["heads"]
    tk = k_arr.shape[2]

    def body(s_ref, q_ref, k_ref, v_ref, g_ref, l_ref, dq_ref, dk_ref, dv_ref):
        q = q_ref[0]
        scores = scores_of(k_ref[0], q, s_ref[0] * tq, s_ref[1], causal)
        weights = jnp.exp(scores - l_ref[0])
        dp = tn(v_ref[0], g_ref[0])
        inner = weights * dp
        centre = jnp.sum(inner, axis=0, keepdims=True)
        ds = (inner - weights * centre).astype(BF)
        dv_ref[0] = nt(g_ref[0], weights.astype(BF)).astype(BF)
        dq_ref[0] = (nn(k_ref[0], ds) * HEAD**-0.5).astype(BF)
        dk_ref[0] = (nt(q, ds) * HEAD**-0.5).astype(BF)

    return pl.pallas_call(
        body,
        out_shape=(
            jax.ShapeDtypeStruct((blocks, heads * HEAD, tq), BF),
            jax.ShapeDtypeStruct((blocks, heads * HEAD, tk), BF),
            jax.ShapeDtypeStruct((blocks, heads * HEAD, tk), BF),
        ),
        grid_spec=pltpu.PrefetchScalarGridSpec(
            num_scalar_prefetch=1,
            grid=(blocks, heads),
            in_specs=[
                pl.BlockSpec(
                    (1, HEAD, tq), lambda b, h, s: (b, q_row + h, s[0] if q_moves else 0)
                ),
                pl.BlockSpec((1, HEAD, tk), lambda b, h, s: (b, k_row + h, 0)),
                pl.BlockSpec((1, HEAD, tk), lambda b, h, s: (b, v_row + h, 0)),
                pl.BlockSpec((1, HEAD, tq), lambda b, h, s: (b, h, 0)),
                pl.BlockSpec((1, 1, tq), lambda b, h, s: (b * heads + h, 0, 0)),
            ],
            out_specs=(
                pl.BlockSpec((1, HEAD, tq), lambda b, h, s: (b, h, 0)),
                pl.BlockSpec((1, HEAD, tk), lambda b, h, s: (b, h, 0)),
                pl.BlockSpec((1, HEAD, tk), lambda b, h, s: (b, h, 0)),
            ),
        ),
        compiler_params=params(48, 2),
    )(info["scalars"], q_arr, k_arr, v_arr, incoming, totals)


GELU_A = 0.7978845608028654
GELU_B = 0.044715


def gelu_parts(gate):
    inner = jnp.tanh(GELU_A * (gate + GELU_B * gate * gate * gate))
    value = 0.5 * gate * (1.0 + inner)
    slope = 0.5 * (1.0 + inner) + 0.5 * gate * (1.0 - inner * inner) * (
        GELU_A * (1.0 + 3.0 * GELU_B * gate * gate)
    )
    return value, slope


def ff_forward(packs, normed):
    d, lanes = packs[0].shape
    wide = lanes // 3
    tokens = normed.shape[1]
    n = len(packs)

    def body(*refs):
        w_refs, x_ref, save_refs, out_ref = refs[:n], refs[n], refs[n + 1 : 2 * n + 1], refs[-1]
        for b, (w_ref, save_ref) in enumerate(zip(w_refs, save_refs)):
            both = tn(w_ref[:, : 2 * wide], x_ref[...])
            save_ref[...] = both.astype(BF)
            value, _ = gelu_parts(both[:wide])
            hidden = (value * both[wide:]).astype(BF)
            part = nn(w_ref[:, 2 * wide :], hidden)
            acc = part if b == 0 else acc + part
        out_ref[...] = acc.astype(BF)

    return pl.pallas_call(
        body,
        out_shape=[jax.ShapeDtypeStruct((2 * wide, tokens), BF)] * n
        + [jax.ShapeDtypeStruct((d, tokens), BF)],
        compiler_params=params(48, 0),
    )(*packs, normed)


def ff_backward(order, packs, saved, normed, grad):
    d, lanes = packs[0].shape
    wide = lanes // 3
    tokens = normed.shape[1]
    n = len(packs)
    size = d // 4

    def body(s_ref, *refs):
        w_refs, save_refs = refs[:n], refs[n : 2 * n]
        x_ref, g_ref, dw_ref, out_ref = refs[2 * n :]
        for b, (w_ref, save_ref) in enumerate(zip(w_refs, save_refs)):
            dh = tn(w_ref[:, 2 * wide :], g_ref[...])
            gate, up = save_ref[:wide].astype(F32), save_ref[wide:].astype(F32)
            value, slope = gelu_parts(gate)
            hidden = (value * up).astype(BF)
            grads = jnp.concatenate(
                [(dh * up * slope).astype(BF), (dh * value).astype(BF)], axis=0
            )
            first = nt(x_ref[...], grads).astype(BF)
            second = nt(g_ref[...], hidden).astype(BF)
            for p in range(4):
                at = pl.ds(pl.multiple_of(s_ref[4 + p] * size, size), size)
                dw_ref[s_ref[b], at, : 2 * wide] = first[p * size : (p + 1) * size]
                dw_ref[s_ref[b], at, 2 * wide :] = second[p * size : (p + 1) * size]
            part = nn(w_ref[:, : 2 * wide], grads)
            acc = part if b == 0 else acc + part
        out_ref[...] = acc.astype(BF)

    return pl.pallas_call(
        body,
        out_shape=(
            jax.ShapeDtypeStruct((n, d, lanes), BF),
            jax.ShapeDtypeStruct((d, tokens), BF),
        ),
        grid_spec=pltpu.PrefetchScalarGridSpec(
            num_scalar_prefetch=1,
            grid=(1,),
            in_specs=[whole((d, lanes))] * n
            + [whole((2 * wide, tokens))] * n
            + [whole((d, tokens))] * 2,
            out_specs=(whole((n, d, lanes)), whole((d, tokens))),
        ),
        compiler_params=params(60),
    )(order, *packs, *saved, normed, grad)


def norm_in(parts, gain, tokens, tile=256):
    d = parts[0].shape[0]
    n = len(parts)

    def body(*refs):
        x_refs, g_ref, sum_ref, norm_ref, scale_ref = refs[:n], refs[n], *refs[n + 1 :]
        states = x_refs[0][...].astype(F32)
        if n > 1:
            rest = x_refs[1][...].astype(F32)
            for ref in x_refs[2:]:
                rest = rest + ref[...].astype(F32)
            states = states + rest
        scale = lax.rsqrt(jnp.mean(states * states, axis=0, keepdims=True) + EPS)
        sum_ref[...] = states
        scale_ref[...] = scale
        norm_ref[...] = (states * scale * g_ref[...]).astype(BF)

    spec = pl.BlockSpec((d, tile), lambda i: (0, i))
    return pl.pallas_call(
        body,
        grid=(tokens // tile,),
        in_specs=[spec] * n + [whole((d, 1))],
        out_specs=(spec, spec, pl.BlockSpec((1, tile), lambda i: (0, i))),
        out_shape=(
            jax.ShapeDtypeStruct((d, tokens), F32),
            jax.ShapeDtypeStruct((d, tokens), BF),
            jax.ShapeDtypeStruct((1, tokens), F32),
        ),
        compiler_params=params(40),
    )(*parts, gain)


def norm_out(scalars, states, gain, scale, incoming, before, place=False, tile=256):
    d, tokens = states.shape
    n = len(incoming)
    has = before is not None
    own_tiles = before.shape[1] // tile if has else 1

    def body(*refs):
        s_ref, x_ref, g_ref, r_ref = refs[:4]
        y_refs = refs[4 : 4 + n]
        b_ref = refs[4 + n] if has else None
        outs = refs[4 + n + has :]
        i = pl.program_id(0)
        states_now = x_ref[...].astype(F32)
        dy = y_refs[0][...].astype(F32)
        for ref in y_refs[1:]:
            dy = dy + ref[...].astype(F32)
        scale_now = r_ref[...]
        weighted = dy * g_ref[...]
        inner = jnp.mean(weighted * states_now, axis=0, keepdims=True)
        total = scale_now * weighted - states_now * (scale_now * scale_now * scale_now * inner)
        if has and place:
            here = (i // own_tiles == s_ref[0]) & (s_ref[2] == 0)
            total = total + b_ref[...] * jnp.where(here, 1.0, 0.0)
        elif has:
            total = total + b_ref[...]
        gain_grad = jnp.sum(dy * states_now * scale_now, axis=1, keepdims=True)
        low_ref, gain_ref = outs[-2:]
        if not place:
            outs[0][...] = total
        low_ref[...] = total.astype(BF)

        @pl.when(i == 0)
        def _():
            gain_ref[...] = gain_grad

        @pl.when(i > 0)
        def _():
            gain_ref[...] += gain_grad

    spec = pl.BlockSpec((d, tile), lambda i, s: (0, i))
    out_shape = [] if place else [jax.ShapeDtypeStruct((d, tokens), F32)]
    out_shape += [jax.ShapeDtypeStruct((d, tokens), BF), jax.ShapeDtypeStruct((d, 1), F32)]
    return pl.pallas_call(
        body,
        out_shape=out_shape,
        grid_spec=pltpu.PrefetchScalarGridSpec(
            num_scalar_prefetch=1,
            grid=(tokens // tile,),
            in_specs=[spec, whole((d, 1)), pl.BlockSpec((1, tile), lambda i, s: (0, i))]
            + [spec] * n
            + ([pl.BlockSpec((d, tile), lambda i, s: (0, i % own_tiles))] if has else []),
            out_specs=[spec] * (len(out_shape) - 1) + [whole((d, 1))],
        ),
        compiler_params=params(40),
    )(scalars, states, gain, scale, *incoming, *([before] if has else []))


def lane_block(lanes, low, high):
    if low // 256 == (high - 1) // 256 and lanes % 256 == 0:
        return 256, low // 256, low % 256
    return lanes, 0, low


def project(pack, normed, low, high):
    blocks, d, lanes = pack.shape
    tokens = normed.shape[1]
    size, index, at = lane_block(lanes, low, high)

    def body(w_ref, x_ref, o_ref):
        o_ref[0] = tn(w_ref[0, :, at : at + high - low], x_ref[...]).astype(BF)

    return pl.pallas_call(
        body,
        grid=(blocks,),
        in_specs=[pl.BlockSpec((1, d, size), lambda b: (b, 0, index)), whole((d, tokens))],
        out_specs=pl.BlockSpec((1, high - low, tokens), lambda b: (b, 0, 0)),
        out_shape=jax.ShapeDtypeStruct((blocks, high - low, tokens), BF),
        compiler_params=params(40),
    )(pack, normed)


def combine(pack, rows, low, high):
    blocks, d, lanes = pack.shape
    tokens = rows.shape[2]
    size, index, at = lane_block(lanes, low, high)

    def body(w_ref, x_ref, o_ref):
        part = nn(w_ref[0, :, at : at + high - low], x_ref[0])
        for b in range(1, blocks):
            part += nn(w_ref[b, :, at : at + high - low], x_ref[b])
        o_ref[...] = part.astype(BF)

    return pl.pallas_call(
        body,
        grid=(1,),
        in_specs=[
            pl.BlockSpec((blocks, d, size), lambda b: (0, 0, index)),
            whole((blocks, high - low, tokens)),
        ],
        out_specs=whole((d, tokens)),
        out_shape=jax.ShapeDtypeStruct((d, tokens), BF),
        compiler_params=params(40),
    )(pack, rows)


def weight_grads(scalars, pairs, lanes):
    d = pairs[0][0].shape[0]
    n = len(pairs)
    lefts = [left for left, _ in pairs]
    rights = [right for _, right in pairs]

    def body(*refs):
        outs = refs[2 * n + 1 :]
        at = 0
        for left_ref, right_ref in zip(refs[1 : n + 1], refs[n + 1 : 2 * n + 1]):
            width = right_ref.shape[1]
            for b, out_ref in enumerate(outs):
                out_ref[:, at : at + width] = nt(left_ref[...], right_ref[b]).astype(BF)
            at += width

    def left_spec(left, right):
        tokens = right.shape[2]
        if left.shape[1] == tokens:
            return pl.BlockSpec((d, tokens), lambda b, s: (0, 0))
        return pl.BlockSpec((d, tokens), lambda b, s: (0, s[0]))

    return pl.pallas_call(
        body,
        out_shape=[jax.ShapeDtypeStruct((d, lanes), BF)] * 2,
        grid_spec=pltpu.PrefetchScalarGridSpec(
            num_scalar_prefetch=1,
            grid=(1,),
            in_specs=[left_spec(left, right) for left, right in pairs]
            + [whole(right.shape) for right in rights],
            out_specs=[whole((d, lanes))] * 2,
        ),
        compiler_params=params(48),
    )(scalars, *lefts, *rights)


def split_sum(parts):
    d, lanes = parts[0].shape
    size = d // 4
    n = len(parts)

    def body(*refs):
        for f, out_ref in enumerate(refs[n:]):
            rows = slice(f * size, (f + 1) * size)
            acc = refs[0][rows].astype(F32)
            for ref in refs[1:n]:
                acc += ref[rows].astype(F32)
            out_ref[...] = acc.astype(BF)

    return pl.pallas_call(
        body,
        out_shape=[jax.ShapeDtypeStruct((size, lanes), BF)] * 4,
        compiler_params=params(40, 0),
    )(*parts)


def source_grads(pack, own, own_low, wide, wide_low, place, width, kind):
    blocks, d, lanes = pack.shape
    tq = own.shape[2] if own is not None else 0
    n = len(wide)
    tokens = wide[0].shape[2]
    step = min(1024, tokens)

    def body(*refs):
        s_ref, w_ref = refs[0], refs[1]
        wide_refs = refs[2 : 2 + n]
        o_ref = refs[-1]
        acc = jnp.zeros((d, step), F32)
        for b in range(blocks):
            for at, ref in zip(wide_low, wide_refs):
                acc += nn(w_ref[b, :, at : at + width], ref[b])
        o_ref[...] = acc.astype(kind)
        if own is not None:
            own_ref = refs[2 + n]
            part = jnp.zeros((d, tq), F32)
            for b in range(blocks):
                part += nn(w_ref[b, :, own_low : own_low + width], own_ref[b])
            where = pl.ds(pl.multiple_of(s_ref[0] * tq, tq), tq)
            o_ref[:, where] += part.astype(kind)

    return pl.pallas_call(
        body,
        out_shape=jax.ShapeDtypeStruct((d, tokens), kind),
        grid_spec=pltpu.PrefetchScalarGridSpec(
            num_scalar_prefetch=1,
            grid=(tokens // step,),
            in_specs=[pl.BlockSpec((blocks, d, lanes), lambda i, s: (0, 0, 0))]
            + [pl.BlockSpec((blocks, width, step), lambda i, s: (0, 0, i))] * n
            + (
                [pl.BlockSpec((blocks, width, tq), lambda i, s: (0, 0, 0))]
                if own is not None
                else []
            ),
            out_specs=pl.BlockSpec((d, step), lambda i, s: (0, i)),
        ),
        compiler_params=params(40),
    )(place, pack, *wide, *([own] if own is not None else []))


VB = 512


def assemble(s_ref, own_ref, one_ref, two_ref, three_ref, out_ref):
    size = own_ref.shape[0]
    out_ref[:size] = own_ref[...]
    out_ref[pl.ds(pl.multiple_of((1 + s_ref[1]) * size, size), size), :] = one_ref[...]
    out_ref[pl.ds(pl.multiple_of((2 - s_ref[1]) * size, size), size), :] = two_ref[...]
    out_ref[3 * size :] = three_ref[...]


def table_specs(size):
    return [pl.BlockSpec((size, VB), lambda v, s: (0, v))] * 4


def vocab_forward(scalars, hidden, table, wanted):
    half_chunks, d, step = hidden[0].shape
    chunks = 2 * half_chunks
    own = table[0]
    size, width = own.shape
    parts = width // VB

    def body(s_ref, h0_ref, h1_ref, own_ref, one_ref, two_ref, three_ref, t_ref, e_ref, m_ref, st_ref, blk, flip):
        vb = pl.program_id(0)

        @pl.when(vb == 0)
        def _():
            st_ref[0] = jnp.full((chunks, step), NEGATIVE, F32)
            st_ref[1:] = jnp.zeros((2, chunks, step), F32)

        assemble(s_ref, own_ref, one_ref, two_ref, three_ref, blk)
        flip[...] = blk[...].T
        ids = lax.broadcasted_iota(jnp.int32, (VB, step), 0)

        def one_chunk(n, states, masked):
            logits = nn(flip[...], states)
            row = slice(n, n + 1)
            st_ref[2, row] += jnp.sum(
                jnp.where(ids == t_ref[row] - vb * VB, logits, 0.0), axis=0, keepdims=True
            )
            if masked:
                logits = jnp.where(ids < s_ref[0] - vb * VB, logits, NEGATIVE)
            before = st_ref[0, row]
            top = jnp.maximum(before, jnp.max(logits, axis=0, keepdims=True))
            exps = jnp.exp(logits - top)
            st_ref[1, row] = st_ref[1, row] * jnp.exp(before - top) + jnp.sum(
                exps, axis=0, keepdims=True
            )
            st_ref[0, row] = top
            m_ref[0, row] = top
            e_ref[n] = exps.astype(BF)

        def some(masked):
            for n in range(chunks):
                one_chunk(n, (h0_ref, h1_ref)[n // half_chunks][n % half_chunks], masked)

        inside = (vb + 1) * VB <= s_ref[0]
        pl.when(inside)(partial(some, False))
        pl.when(jnp.logical_not(inside))(partial(some, True))

    return pl.pallas_call(
        body,
        out_shape=(
            jax.ShapeDtypeStruct((chunks, width, step), BF),
            jax.ShapeDtypeStruct((parts, chunks, step), F32),
            jax.ShapeDtypeStruct((3, chunks, step), F32),
        ),
        grid_spec=pltpu.PrefetchScalarGridSpec(
            num_scalar_prefetch=1,
            grid=(parts,),
            in_specs=[whole((half_chunks, d, step))] * 2
            + table_specs(size)
            + [whole((chunks, step))],
            out_specs=(
                pl.BlockSpec((chunks, VB, step), lambda v, s: (0, v, 0)),
                pl.BlockSpec((1, chunks, step), lambda v, s: (v, 0, 0)),
                whole((3, chunks, step)),
            ),
            scratch_shapes=[pltpu.VMEM((d, VB), BF), pltpu.VMEM((VB, d), BF)],
        ),
        compiler_params=params(48),
    )(scalars, *hidden, *table, wanted)


def vocab_hidden_grad(scalars, exps, tops, logsum, first_row, table, wanted):
    chunks, width, step = exps.shape
    own = table[0]
    size = own.shape[0]
    d = 4 * size
    parts = width // VB

    def body(s_ref, e_ref, m_ref, l_ref, own_ref, one_ref, two_ref, three_ref, t_ref, g_ref, o_ref, p_ref, blk, acc):
        vb = pl.program_id(0)

        @pl.when(vb == 0)
        def _():
            acc[...] = jnp.zeros_like(acc)

        assemble(s_ref, own_ref, one_ref, two_ref, three_ref, blk)
        ids = lax.broadcasted_iota(jnp.int32, (VB, step), 0)

        for n in range(chunks):
            row, at = slice(n, n + 1), slice(first_row + n, first_row + n + 1)
            scale = jnp.exp(m_ref[0, row] - l_ref[at])
            probs = e_ref[n].astype(F32) * scale
            grads = jnp.where(ids == t_ref[row] - vb * VB, probs - 1.0, probs).astype(BF)
            g_ref[n] = grads
            acc[n] += nn(blk[...], grads)

        @pl.when(vb == parts - 1)
        def _():
            o_ref[...] = acc[: chunks // 2].astype(BF)
            p_ref[...] = acc[chunks // 2 :].astype(BF)

    return pl.pallas_call(
        body,
        out_shape=(
            jax.ShapeDtypeStruct((chunks, width, step), BF),
            jax.ShapeDtypeStruct((chunks // 2, d, step), BF),
            jax.ShapeDtypeStruct((chunks // 2, d, step), BF),
        ),
        grid_spec=pltpu.PrefetchScalarGridSpec(
            num_scalar_prefetch=1,
            grid=(parts,),
            in_specs=[
                pl.BlockSpec((chunks, VB, step), lambda v, s: (0, v, 0)),
                pl.BlockSpec((1, chunks, step), lambda v, s: (v, 0, 0)),
                whole(logsum.shape),
            ]
            + table_specs(size)
            + [whole((chunks, step))],
            out_specs=(
                pl.BlockSpec((chunks, VB, step), lambda v, s: (0, v, 0)),
                whole((chunks // 2, d, step)),
                whole((chunks // 2, d, step)),
            ),
            scratch_shapes=[pltpu.VMEM((d, VB), BF), pltpu.VMEM((chunks, d, step), F32)],
        ),
        input_output_aliases={1: 0},
        compiler_params=params(56),
    )(scalars, exps, tops, logsum, *table, wanted)


def vocab_table_grad(places, hidden, grads):
    per, d, step = hidden[0].shape
    chunks, width, _ = grads[0].shape
    unit = d // 8
    parts = width // VB
    nh, ng = len(hidden), len(grads)

    def body(*refs):
        s_ref, h_refs, g_refs, o_ref = refs[0], refs[1 : 1 + nh], refs[1 + nh : -1], refs[-1]
        acc = None
        for n in range(nh * per):
            part = nt(h_refs[n // per][n % per], g_refs[n // chunks][n % chunks])
            acc = part if acc is None else acc + part
        for u in range(8):
            spot = pl.ds(pl.multiple_of(s_ref[u] * unit, unit), unit)
            o_ref[spot, :] = acc[u * unit : (u + 1) * unit].astype(BF)

    return pl.pallas_call(
        body,
        out_shape=jax.ShapeDtypeStruct((d, width), BF),
        grid_spec=pltpu.PrefetchScalarGridSpec(
            num_scalar_prefetch=1,
            grid=(parts,),
            in_specs=[whole((per, d, step))] * nh
            + [pl.BlockSpec((chunks, VB, step), lambda v, s: (0, v, 0))] * ng,
            out_specs=pl.BlockSpec((d, VB), lambda v, s: (0, v)),
        ),
        compiler_params=params(48),
    )(places, *hidden, *grads)


def merge_core(mine, other):
    def body(a_ref, b_ref, o_ref):
        for i in range(8):
            row, far = slice(i, i + 1), slice(i ^ 2, (i ^ 2) + 1)
            top = jnp.maximum(a_ref[0, row], b_ref[0, far])
            o_ref[0, row] = top
            o_ref[1, row] = a_ref[1, row] * jnp.exp(a_ref[0, row] - top) + b_ref[
                1, far
            ] * jnp.exp(b_ref[0, far] - top)
            o_ref[2, row] = a_ref[2, row] + b_ref[2, far]

    return pl.pallas_call(
        body,
        out_shape=jax.ShapeDtypeStruct(mine.shape, F32),
        compiler_params=params(16, 0),
    )(mine, other)


def merge_chips(spots, items):
    step = items[0].shape[2]
    flips = (0, 4, 1, 5)

    def body(s_ref, *refs):
        log_ref, loss_ref, rows = refs[-3:]
        for i in range(8):
            at = [slice(i ^ f, (i ^ f) + 1) for f in flips]
            top = refs[0][0, at[0]]
            for ref, row in zip(refs[1:4], at[1:]):
                top = jnp.maximum(top, ref[0, row])
            total = jnp.zeros((1, step), F32)
            picked = jnp.zeros((1, step), F32)
            for ref, row in zip(refs[:4], at):
                total += ref[1, row] * jnp.exp(ref[0, row] - top)
                picked += ref[2, row]
            logsum = top + jnp.log(total)
            log_ref[at[0]] = logsum
            rows[i] = logsum - picked
        for n in range(4):
            loss_ref[n] = rows[s_ref[n]]

    return pl.pallas_call(
        body,
        out_shape=(
            jax.ShapeDtypeStruct((8, step), F32),
            jax.ShapeDtypeStruct((4, 1, step), F32),
        ),
        grid_spec=pltpu.PrefetchScalarGridSpec(
            num_scalar_prefetch=1,
            grid=(1,),
            in_specs=[whole(items[0].shape)] * 4,
            out_specs=(whole((8, step)), whole((4, 1, step))),
            scratch_shapes=[pltpu.VMEM((8, 1, step), F32)],
        ),
        compiler_params=params(16),
    )(spots, *items)


class Moves:
    def __init__(self, dp):
        self.dp = dp

    def core(self, x):
        return lax.ppermute(x, "dp", [(i, i ^ 1) for i in range(self.dp)])

    def col(self, x, bit):
        return lax.ppermute(x, "col", [(i, i ^ bit) for i in range(4)])

    def cols(self, x, bit, core):
        perm = []
        for i in range(core, self.dp, 2):
            for c in range(4):
                perm.append((i * 4 + c, i * 4 + (c ^ bit)))
        return lax.ppermute(x, ("dp", "col"), perm)

    def row(self, x, bit):
        return lax.ppermute(x, "row", [(i, i ^ bit) for i in range(4)])

    def rows(self, x, pairs):
        perm = []
        for i in range(self.dp):
            for r in range(4):
                if i % 2 in pairs:
                    flip, bit = pairs[i % 2]
                    perm.append((i * 4 + r, (i ^ flip) * 4 + (r ^ bit)))
        return lax.ppermute(x, ("dp", "row"), perm)

    def spread(self, x, turn, back=False):
        perm = []
        for i in range(self.dp):
            for c in range(4):
                dest = (i - i % 2 + c // 2) * 4 + 2 * (i % 2) + (c % 2 ^ turn)
                perm.append((dest, i * 4 + c) if back else (i * 4 + c, dest))
        return lax.ppermute(x, ("dp", "col"), perm)


STEP_ONE = {0: (0, 1), 1: (0, 2)}
STEP_TWO = {0: (1, 2), 1: (1, 1)}
STEP_TWO_BACK = {0: (1, 1), 1: (1, 2)}
SAME_TWO = {0: (0, 2), 1: (0, 1)}


def same(bit):
    return {0: (0, bit), 1: (0, bit)}


def tie(*xs):
    return lax.optimization_barrier(xs)


def plus(a, b, kind=BF):
    return (a.astype(F32) + b.astype(F32)).astype(kind)


def local(
    inputs,
    encoder,
    prefix,
    targets,
    gain_self,
    w_query,
    w_key,
    w_value,
    w_attn_out,
    gain_cross,
    w_cross_query,
    w_cross_key,
    w_cross_value,
    w_cross_out,
    gain_ff,
    w_gate,
    w_up,
    w_ff_out,
    gain_final,
    embed_table,
    *,
    dp,
):
    move = Moves(dp)
    core = lax.axis_index("dp") % 2
    row = lax.axis_index("row")
    col = lax.axis_index("col")
    first_core = core == 0
    side = col // 2
    half = col % 2
    block = inputs.shape[0]
    d = 4 * block
    seq = inputs.shape[1]
    tq = seq // 2
    tc = tq // 2
    heads = w_query.shape[1] // HEAD
    hw = heads * HEAD
    ff_half = w_gate.shape[1] // 2
    vocab = embed_table.shape[1]
    width = -(-vocab // (2 * VB)) * VB
    mine = side == core
    pick = jnp.where

    def settle(got):
        other = move.core(got)
        near, far = pick(mine, got, other), pick(mine, other, got)
        return jnp.concatenate([near[0], far[0], near[1], far[1]], axis=0)

    def hand_back(parts):
        hi = [pick(mine, parts[0], parts[1]), pick(mine, parts[2], parts[3])]
        return [move.spread(hi[0], 0, True), move.spread(hi[1], 1, True)]

    def in_order(got):
        return pick(
            half == 0,
            jnp.concatenate([got[0], got[1]], axis=1),
            jnp.concatenate([got[1], got[0]], axis=1),
        )

    def fold_core(partial_sum):
        blocks4 = partial_sum.reshape(4, block, -1)
        near = jnp.stack([blocks4[0], blocks4[2]])
        far = jnp.stack([blocks4[1], blocks4[3]])
        return pick(mine, near, far), move.core(pick(mine, far, near))

    def fold_out(keep, got):
        return [move.spread(plus(keep[n], got[n]), n, True) for n in range(2)]

    def z_sum(parts, cores):
        own, two, one, three = split_sum(parts)
        send = [(two, 2), (one, 1), (three, 3)]
        if cores is None:
            return [own] + [move.col(x, bit) for x, bit in send]
        return [own] + [move.cols(x, bit, cores) for x, bit in send]

    def total(parts):
        return sum(x.astype(F32) for x in parts)

    def swap_bits(n):
        return n // 2 + 2 * (n % 2)

    valid = jnp.where(first_core, width, vocab - width)
    vocab_scalars = jnp.stack([valid, core]).astype(jnp.int32)
    chip = jnp.where(mine, 0, 1)
    spots = []
    for lo in range(2):
        for h in range(2):
            spots.append((half ^ lo) * 4 + (core ^ h) * 2 + chip)
    spots = jnp.stack(spots).astype(jnp.int32)
    own_places = [row, row ^ (1 + core), row ^ (2 - core), row ^ 3]
    own_places += [col ^ swap_bits(p) for p in range(4)]
    own_places = jnp.stack(own_places).astype(jnp.int32)
    places = []
    for unit in range(8):
        e = 2 * (row ^ (unit // 2)) + unit % 2
        places.append(e % 4 * 2 + e // 4)
    places = jnp.stack(places).astype(jnp.int32)

    pack_self = jnp.concatenate([w_query, w_key, w_value, w_attn_out.T], axis=1)
    pack_cross = jnp.concatenate([w_cross_query, w_cross_key, w_cross_value, w_cross_out.T], axis=1)
    sc_own = pick(first_core, pack_self, pack_cross)
    sc_own, embed_table = tie(sc_own, embed_table)
    padded = jnp.pad(embed_table, ((0, 0), (0, 2 * width - vocab)))
    table_own = pick(first_core, padded[:, :width], padded[:, width:])
    pack_ff = [
        jnp.concatenate([w[:, s : s + ff_half] for w in (w_gate, w_up, w_ff_out)], axis=1)
        for s in (0, ff_half)
    ]
    ff_own = pick(first_core, *pack_ff)

    columns = [gain_self, gain_cross, gain_ff, gain_final]
    tops = [lax.reduce_precision(g, 8, 7) for g in columns]
    columns = tops + [g - t for g, t in zip(columns, tops)]
    high = (prefix // 256).astype(F32)
    columns += [jnp.broadcast_to(high, (block,)), jnp.broadcast_to(prefix - high * 256, (block,))]
    extras = jnp.pad(jnp.stack(columns, axis=1).astype(BF), ((0, 0), (0, 128 - len(columns))))
    x_in = jnp.concatenate([inputs, extras], axis=1)

    sc_got = [move.col(sc_own, bit) for bit in (2, 1, 3)]
    table_one = move.rows(table_own, STEP_ONE)
    table_two = move.rows(table_own, SAME_TWO)
    sc, x_in, ff_own, targets, spots, places, own_places = tie(
        jnp.concatenate([sc_own, *sc_got]), x_in, ff_own, targets, spots, places, own_places
    )
    other_targets = move.core(targets)
    near, far = pick(mine, targets, other_targets), pick(mine, other_targets, targets)

    def target_chunks(lo):
        out = []
        for which in (core, 1 - core):
            for seq_targets in (near, far):
                out.append(lax.dynamic_slice_in_dim(seq_targets, lo * tq + which * tc, tc, 0))
        wanted = jnp.stack(out) - col * vocab
        return jnp.where((wanted >= 0) & (wanted < vocab), wanted - core * width, -1)

    want_near, want_far = target_chunks(half), target_chunks(1 - half)
    sc_row = move.rows(sc, STEP_ONE)
    x_got = [move.spread(x_in, 0), move.spread(x_in, 1)]
    x_near, x_far, ff_own = tie(*x_got, ff_own)
    ff_far = move.col(ff_own, 2)
    x_near, x_far, sc_row, sc, ff_own, ff_far, table_one, table_two, enc_in = tie(
        x_near, x_far, sc_row, sc, ff_own, ff_far, table_one, table_two, encoder
    )
    sc_one = move.rows(sc, STEP_TWO)
    sc_two = move.rows(sc_row, STEP_TWO)
    ff = jnp.concatenate([ff_own, ff_far])
    ff_got = move.col(ff, 1)
    enc_zero = move.spread(enc_in, 0)
    states_low = settle(jnp.stack([x_near, x_far]))
    small = states_low[:, seq : seq + 16].astype(F32)
    g_self, g_cross, g_ff, g_final = (small[:, n : n + 1] + small[:, n + 4 : n + 5] for n in range(4))
    length = lax.dynamic_slice(small, (swap_bits(col ^ row) * block, 8), (1, 2))
    length = (length[0, :1] * 256 + length[0, 1:]).astype(jnp.int32)
    scalars = jnp.concatenate([half[None], length, core[None]]).astype(jnp.int32)
    info = {"tq": tq, "heads": heads, "scalars": scalars}
    states_all, normed_all, scale_all = norm_in([states_low], g_self, seq)
    states_own = lax.dynamic_slice_in_dim(states_low, half * tq, tq, 1)
    own_blocks = jnp.stack([sc, sc_row])
    normed_all, states_own, own_blocks, scalars, want_near, want_far, ff, ff_got, enc_zero, enc_in = tie(
        normed_all, states_own, own_blocks, scalars, want_near, want_far, ff, ff_got, enc_zero, enc_in
    )
    ff = jnp.concatenate([ff, ff_got])
    ff_row = move.rows(ff, STEP_ONE)
    enc_one = move.spread(enc_in, 1)
    other_blocks = jnp.stack([sc_one, sc_two])
    ws = pick(first_core, own_blocks, other_blocks)
    wc = pick(first_core, other_blocks, own_blocks)

    qkv = project(ws, normed_all, 0, 3 * hw)
    self_args = ((qkv, 0, True), (qkv, heads), (qkv, 2 * heads))
    self_args = ((qkv, 0, True), (qkv, heads), (qkv, 2 * heads))
    attended, totals_self = attend_forward(info, *self_args, True)
    attended, enc_one, ff, ff_row = tie(attended, enc_one, ff, ff_row)
    ff_one = move.rows(ff, SAME_TWO)
    enc_all = settle(jnp.stack([enc_zero, enc_one]))
    branch = combine(ws, attended, 3 * hw, 4 * hw)
    first, normed_cross, scale_cross = norm_in([states_own, branch, move.core(branch)], g_cross, tq)


    cq = project(wc, normed_cross, 0, hw)
    ckv = project(wc, enc_all, hw, 3 * hw)
    cq, ckv, ff_row, ff_one = tie(cq, ckv, ff_row, ff_one)
    ff_two = move.rows(ff_row, SAME_TWO)
    cross_args = ((cq, 0, False), (ckv, 0), (ckv, heads))
    crossed, totals_cross = attend_forward(info, *cross_args, False)
    crossed, ff_two, table_one = tie(crossed, ff_two, table_one)
    table_three = move.rows(table_one, SAME_TWO)
    branch = combine(wc, crossed, 3 * hw, 4 * hw)
    second, normed_ff, scale_ff = norm_in([first, branch, move.core(branch)], g_ff, tq)

    wf = (ff, ff_row, ff_one, ff_two)
    *saved, branch = ff_forward(wf, normed_ff)
    third, normed_final, scale_final = norm_in([second, branch, move.core(branch)], g_final, tq)

    def reorder(x, index):
        parts = x.reshape(4, block, x.shape[-1])
        return jnp.concatenate(
            [lax.dynamic_index_in_dim(parts, i, 0, keepdims=False) for i in index], axis=0
        )

    piece = lax.dynamic_slice_in_dim(normed_final, core * tc, tc, 1)
    piece = reorder(piece, [swap_bits(col ^ row ^ s) for s in range(4)])
    near_pieces, table_three = tie(jnp.stack([piece, move.col(piece, 2)]), table_three)
    table = (table_own, table_one, table_two, table_three)
    far_pieces = move.col(near_pieces, 1)
    hidden_near = (near_pieces, move.core(near_pieces))
    exps_near, tops_near, stats_near = vocab_forward(
        vocab_scalars, hidden_near, table, want_near
    )
    far_pieces, stats_near, out_low = tie(far_pieces, stats_near, third.astype(BF))
    hidden_far = (far_pieces, move.core(far_pieces))
    out_got = hand_back(out_low.reshape(4, block, tq))
    exps_far, tops_far, stats_far = vocab_forward(vocab_scalars, hidden_far, table, want_far)
    stats_far, *out_got = tie(stats_far, *out_got)

    stats = jnp.concatenate([stats_near, stats_far], axis=1)
    stats = merge_core(stats, move.core(stats))
    items = [stats] + [move.col(stats, bit) for bit in (1, 2, 3)]
    logsum, loss = merge_chips(spots, items)
    loss = loss.reshape(seq)

    grads_far, own_far, oth_far = vocab_hidden_grad(
        vocab_scalars, exps_far, tops_far, logsum, 4, table, want_far
    )
    part_far, exps_near = tie(plus(own_far, move.core(oth_far)), exps_near)
    come_far = move.col(part_far, 1)
    grads_near, own_near, oth_near = vocab_hidden_grad(
        vocab_scalars, exps_near, tops_near, logsum, 0, table, want_near
    )
    part = plus(own_near, move.core(oth_near), F32) + come_far.astype(F32)
    part_last, grads_near = tie(part[1].astype(BF), grads_near)
    come_last = move.col(part_last, 2)
    grad_table = vocab_table_grad(
        places, (*hidden_near, *hidden_far), (grads_near, grads_far)
    )
    come_last, grad_table = tie(come_last, grad_table)
    if dp == 2:
        table_sum = lax.psum_scatter(grad_table, "row", scatter_dimension=0, tiled=True)
    part = plus(part[0], come_last)
    part = reorder(part, [col ^ row ^ swap_bits(n) for n in range(4)])
    other = move.core(part)
    grad_normed = jnp.concatenate(
        [pick(first_core, part, other), pick(first_core, other, part)], axis=1
    )

    grad_third, low, gg_final = norm_out(
        scalars, third, g_final, scale_final, [grad_normed], None
    )
    ff_grads, partial_normed = ff_backward(own_places, wf, saved, normed_ff, low)
    ff_sum = lax.psum_scatter(ff_grads.reshape(4 * d, -1), "row", scatter_dimension=0, tiled=True)
    grad_second, low, gg_ff = norm_out(
        scalars, second, g_ff, scale_ff, [partial_normed, move.core(partial_normed)], grad_third
    )
    grad_crossed = project(wc, low, 3 * hw, 4 * hw)
    dcq, dck, dcv = attend_backward(info, *cross_args, grad_crossed, totals_cross, False)
    partial_normed = combine(wc, dcq, 0, hw)
    partial_other = move.core(partial_normed)
    dck, partial_normed = tie(dck, partial_normed)
    grad_enc = source_grads(wc, None, 0, (dck, dcv), (hw, 2 * hw), scalars, hw, BF)
    partial_other, grad_enc = tie(partial_other, grad_enc)
    grad_first, low_self, gg_cross = norm_out(
        scalars, first, g_cross, scale_cross, [partial_normed, partial_other], grad_second
    )
    enc_keep, enc_come = fold_core(grad_enc)
    enc_keep, enc_come, low_self, normed_cross = tie(enc_keep, enc_come, low_self, normed_cross)
    enc_come = fold_out(enc_keep, enc_come)
    cross_zero, cross_one = weight_grads(
        scalars, [(normed_cross, dcq), (enc_all, dck), (enc_all, dcv), (low, crossed)], 4 * hw
    )
    cross_zero, cross_one, low_self = tie(cross_zero, cross_one, low_self)
    cross_come = [
        move.rows(cross_zero, {0: (1, 1)}),
        move.rows(cross_one, {0: (1, 3)}),
        move.rows(cross_one, {1: (0, 2)}),
    ]

    grad_attended = project(ws, low_self, 3 * hw, 4 * hw)
    dq, dk, dv = attend_backward(info, *self_args, grad_attended, totals_self, True)
    if dp == 2:
        dq, table_sum = tie(dq, table_sum)
    dq, dk, cross_come = tie(dq, dk, cross_come)
    self_zero, self_one = weight_grads(
        scalars, [(normed_all, dq), (normed_all, dk), (normed_all, dv), (low_self, attended)], 4 * hw
    )
    self_come = [
        move.rows(self_one, {0: (0, 1)}),
        move.rows(self_zero, {1: (1, 2)}),
        move.rows(self_one, {1: (1, 3)}),
    ]
    dk, self_zero, ff_sum = tie(dk, self_zero, ff_sum)
    sum_ff = lax.psum_scatter(ff_sum, "col", scatter_dimension=0, tiled=True)
    cross_sum = [cross_zero, *cross_come]
    cut = d // 2
    cross_send = total([x[cut:] for x in cross_sum]).astype(BF)
    cross_keep = total([x[:cut] for x in cross_sum]).astype(BF)
    cross_got = move.cols(cross_send, 1, 1)
    dk, cross_keep = tie(dk, cross_keep)
    partial_normed = source_grads(ws, dq, 0, (dk, dv), (hw, 2 * hw), scalars, hw, F32)
    grad_states, gg_self = norm_out(
        scalars, states_all, g_self, scale_all, [partial_normed], grad_first, True
    )
    once = jnp.where(first_core, 1.0, 0.0)
    gain_columns = jnp.concatenate([gg_self, gg_cross * once, gg_ff * once, gg_final * once], axis=1)
    gain_columns = jnp.pad(gain_columns.astype(BF), ((0, 0), (0, 124)))
    grad_states = jnp.concatenate([grad_states, gain_columns], axis=1)
    grad_states, enc_come, self_come, cross_got = tie(grad_states, enc_come, self_come, cross_got)
    in_keep, in_come = fold_core(grad_states)
    in_come = fold_out(in_keep, in_come)
    self_parts = z_sum([self_zero, *self_come], 0)
    cross_sum = plus(cross_keep, cross_got)
    cross_got = move.cols(cross_sum[block:], 2, 1)
    in_come = in_come[0].astype(F32) + in_come[1].astype(F32)
    in_come, self_own = tie(in_come, self_parts[0])
    packed = in_come[:, seq : seq + 4].T
    if dp == 2:
        come = [move.row(packed, bit) for bit in (1, 2, 3)]
        packed, come, self_parts[1:], sum_ff = tie(packed, come, self_parts[1:], sum_ff)
        packed = packed + come[0] + come[1] + come[2]
        packed = packed + move.core(packed)
    else:
        packed = lax.psum(packed, ("dp", "row"))

    grad_encoder = enc_come[0].astype(F32) + enc_come[1].astype(F32)
    grad_inputs = in_come[:, :seq]
    sum_self = total([self_own, *self_parts[1:]])
    sum_cross = cross_sum[:block].astype(F32) + cross_got.astype(F32)
    sum_ff = sum_ff.astype(F32)

    if dp == 2:
        cut = table_sum.reshape(2, d // 8, width)
        keep, got = pick(first_core, cut[0], cut[1]), move.core(pick(first_core, cut[1], cut[0]))
        table_sum = jnp.concatenate(
            [pick(first_core, keep, got), pick(first_core, got, keep)[:, : vocab - width]], axis=1
        ).astype(F32)
    else:
        full = grad_table.reshape(4, 2, d // 8, width).transpose(1, 0, 2, 3).reshape(d, width)
        blank = jnp.zeros_like(full)
        full = pick(
            first_core,
            jnp.concatenate([full, blank], axis=1),
            jnp.concatenate([blank, full], axis=1),
        )[:, :vocab]
        table_sum = lax.psum_scatter(
            full, ("dp", "row"), scatter_dimension=0, tiled=True
        ).astype(F32)

    def flip_last(x):
        return jnp.concatenate([x[:, :-hw], x[:, -hw:].T], axis=1)

    both = jnp.concatenate(
        [flip_last(pick(first_core, sum_self, sum_cross)), sum_ff], axis=1
    )
    if dp == 2:
        rows_half = block // 2
        keep = pick(first_core, both[:rows_half], both[rows_half:])
        got = move.core(pick(first_core, both[rows_half:], both[:rows_half]))
        lower, upper = pick(first_core, keep, got), pick(first_core, got, keep)
    else:
        both = jnp.concatenate([pick(first_core, both, 0.0), pick(first_core, 0.0, both)], axis=1)
        both = lax.psum_scatter(both, "dp", scatter_dimension=0, tiled=True)
        lower, upper = jnp.split(both, 2, axis=1)
    out_ff0, out_ff1 = lower[:, 4 * hw :], upper[:, 4 * hw :]

    def ff_part(n):
        sl = slice(n * ff_half, (n + 1) * ff_half)
        return jnp.concatenate([out_ff0[:, sl], out_ff1[:, sl]], axis=1)

    return (
        in_order(out_got),
        loss,
        grad_inputs,
        grad_encoder,
        packed[0],
        *(lower[:, n * hw : (n + 1) * hw] for n in range(4)),
        packed[1],
        *(upper[:, n * hw : (n + 1) * hw] for n in range(4)),
        packed[2],
        ff_part(0),
        ff_part(1),
        ff_part(2),
        packed[3],
        table_sum,
    )


def solution(mesh):
    return jax.shard_map(
        partial(local, dp=mesh.shape["dp"]),
        mesh=mesh,
        in_specs=(
            P("col", ("dp", "row")),
            P("col", ("dp", "row")),
            P(("dp", "col")),
            P(("dp", "row")),
            P("col"),
            P("col", "row"),
            P("col", "row"),
            P("col", "row"),
            P("row", "col"),
            P("col"),
            P("col", "row"),
            P("col", "row"),
            P("col", "row"),
            P("row", "col"),
            P("col"),
            P("col", "row"),
            P("col", "row"),
            P("col", "row"),
            P("col"),
            P("row", "col"),
        ),
        out_specs=(
            P("col", ("dp", "row")),
            P(("dp", "row")),
            P("col", ("dp", "row")),
            P("col", ("dp", "row")),
            P("col"),
            P(("col", "dp"), "row"),
            P(("col", "dp"), "row"),
            P(("col", "dp"), "row"),
            P(("row", "dp"), "col"),
            P("col"),
            P(("col", "dp"), "row"),
            P(("col", "dp"), "row"),
            P(("col", "dp"), "row"),
            P(("row", "dp"), "col"),
            P("col"),
            P(("col", "dp"), "row"),
            P(("col", "dp"), "row"),
            P(("col", "dp"), "row"),
            P("col"),
            P(("dp", "row"), "col"),
        ),
        check_vma=False,
    )
```
